32 devices in a mesh: dp: 8 (over z, y), tensor: 4 (over x, core).
Axes of the slice: x: 2, y: 2, z: 4, core: 2. Of those that a mesh axis runs over, the one named last changes fastest.
Arguments:
- inputs: bfloat16 [16, 1024, 512], P('dp', 'tensor'), may hold values from -6 to 6
- memory: bfloat16 [16, 1024, 512], P('dp', 'tensor'), may hold values from -6 to 6
- tgt_len: int32 [16], P('dp'), may hold values from 512 to 1024, as said below
- src_len: int32 [16], P('dp'), may hold values from 512 to 1024, as said below
- cotangent: bfloat16 [16, 1024, 512], P('dp', 'tensor'), may hold values from -6 to 6
- w_qkv: bfloat16 [3, 512, 512], P(None, 'dp', 'tensor'), may hold values from -0.25 to 0.25
- w_out: bfloat16 [512, 512], P('tensor', 'dp'), may hold values from -6 to 6
- cross_query: bfloat16 [512, 512], P('dp', 'tensor'), may hold values from -0.25 to 0.25
- cross_kv: bfloat16 [2, 512, 512], P(None, 'dp', 'tensor'), may hold values from -0.25 to 0.25
- cross_out: bfloat16 [512, 512], P('tensor', 'dp'), may hold values from -6 to 6
- ffn_up: bfloat16 [512, 2048], P('dp', 'tensor'), may hold values from -0.25 to 0.25
- ffn_down: bfloat16 [2048, 512], P('tensor', 'dp'), may hold values from -0.1875 to 0.1875
- gain_one: bfloat16 [512], P('dp'), may hold values from 0.099609375 to 1.8984375
- bias_one: bfloat16 [512], P('dp'), may hold values from -3 to 3
- gain_two: bfloat16 [512], P('dp'), may hold values from 0.099609375 to 1.8984375
- bias_two: bfloat16 [512], P('dp'), may hold values from -3 to 3
- gain_three: bfloat16 [512], P('dp'), may hold values from 0.099609375 to 1.8984375
- bias_three: bfloat16 [512], P('dp'), may hold values from -3 to 3
Outputs:
- output: bfloat16 [16, 1024, 512], P('dp', 'tensor')
- grad_inputs: float32 [16, 1024, 512], P('dp', 'tensor')
- grad_memory: float32 [16, 1024, 512], P('dp', 'tensor')
- grad_w_qkv: float32 [3, 512, 512], P(None, 'dp', 'tensor')
- grad_w_out: float32 [512, 512], P('tensor', 'dp')
- grad_cross_query: float32 [512, 512], P('dp', 'tensor')
- grad_cross_kv: float32 [2, 512, 512], P(None, 'dp', 'tensor')
- grad_cross_out: float32 [512, 512], P('tensor', 'dp')
- grad_ffn_up: float32 [512, 2048], P('dp', 'tensor')
- grad_ffn_down: float32 [2048, 512], P('tensor', 'dp')
- grad_gain_one: float32 [512], P('dp')
- grad_bias_one: float32 [512], P('dp')
- grad_gain_two: float32 [512], P('dp')
- grad_bias_two: float32 [512], P('dp')
- grad_gain_three: float32 [512], P('dp')
- grad_bias_three: float32 [512], P('dp')
The draws below stay inside these ranges and needn't reach their ends.
Inputs may be any that keep to these rules, and one draw needn't show every extreme that they name: `tgt_len`: one sequence has a target length of 1024 and another of 512. `src_len`: one sequence has a source length of 1024 and another of 512.
All inputs are finite; a program needn't handle non-finite values.
Results may differ from the reference program's by a relative error of at most 0.015.
Values may be sent and summed in bfloat16 or wider, within the bound.
A program may use at most 128 MiB of HBM per device.

```python
import jax
import jax.numpy as jnp
from jax import lax

D = 512
HEADS = 8
DH = 64
FF = 2048
SLOT = 1024
SRC = 1024
HD = 512
SEQS = 16


def length_draw(key, longest):
    first_key = jax.random.fold_in(key, 1)
    second_key = jax.random.fold_in(key, 2)
    third_key = jax.random.fold_in(key, 3)
    lengths = jax.random.randint(first_key, (SEQS,), longest // 2, longest + 1)
    full_index = jax.random.randint(second_key, (), 0, SEQS)
    offset = jax.random.randint(third_key, (), 1, SEQS)
    half_index = (full_index + offset) % SEQS
    positions = jnp.arange(SEQS, dtype=jnp.int32)
    lengths = jnp.where(positions == full_index, longest, lengths)
    lengths = jnp.where(positions == half_index, longest // 2, lengths)
    return lengths.astype(jnp.int32)


def draw_tgt_len(key, part):
    return length_draw(jax.random.fold_in(key, 17), SLOT)


def draw_src_len(key, part):
    return length_draw(jax.random.fold_in(key, 29), SRC)


def levels(rng, extent, cuts, least, high):
    gain = 1.0
    for axis_at, blocks in cuts:
        heights = jax.random.uniform(jax.random.fold_in(jax.random.fold_in(rng, 6), axis_at), (blocks,), jnp.float32, least / len(cuts), high / len(cuts))
        gain = gain * jnp.repeat(jnp.exp(heights), extent[axis_at] // blocks).reshape((-1,) + (1,) * (len(extent) - 1 - axis_at))
    return gain


def bell_draw(stream_key, shape, scale, reach, split=(), kind=jnp.bfloat16):
    loudness = levels(stream_key, shape, split, -0.22, 0.18) if split else 1.0
    drawn = jax.random.normal(stream_key, shape, jnp.float32) * scale * loudness
    return jnp.minimum(jnp.maximum(drawn, -reach), reach).astype(kind)


def setup_inputs(seed: int = 0) -> dict:
    arg_keys = jax.random.split(jax.random.key(seed), 19)
    inputs = bell_draw(arg_keys[0], (SEQS, SLOT, D), 1.0, 6.0, ((0, 8), (1, 4)))
    memory = bell_draw(arg_keys[1], (SEQS, SRC, D), 1.0, 6.0, ((0, 8), (1, 4)))
    tgt_len = draw_tgt_len(jax.random.fold_in(arg_keys[18], 71), 0)
    src_len = draw_src_len(jax.random.fold_in(arg_keys[18], 71), 0)
    cotangent = bell_draw(arg_keys[4], (SEQS, SLOT, D), 1.0, 6.0, ((0, 8), (1, 4)))
    w_qkv = bell_draw(arg_keys[5], (3, D, HD), D ** -0.5, 0.25, ((1, 8), (2, 4)))
    w_out = bell_draw(arg_keys[6], (HD, D), (max(1, 2 * HD // SLOT)) ** -0.5, 6.0, ((0, 4), (1, 8)))
    cross_query = bell_draw(arg_keys[7], (D, HD), D ** -0.5, 0.25, ((0, 8), (1, 4)))
    cross_kv = bell_draw(arg_keys[8], (2, D, HD), D ** -0.5, 0.25, ((1, 8), (2, 4)))
    cross_out = bell_draw(arg_keys[9], (HD, D), (max(1, 2 * HD // SRC)) ** -0.5, 6.0, ((0, 4), (1, 8)))
    ffn_up = bell_draw(arg_keys[10], (D, FF), D ** -0.5, 0.25, ((0, 8), (1, 4)))
    ffn_down = bell_draw(arg_keys[11], (FF, D), (FF // 2) ** -0.5, 0.1875, ((0, 4), (1, 8)))
    gain_one = jnp.clip(1.0 + 0.18 * jax.random.normal(arg_keys[12], (D,), jnp.float32), 0.099609375, 1.8984375).astype(jnp.bfloat16)
    bias_one = bell_draw(arg_keys[13], (D,), 0.5, 3.0, ((0, 8),))
    gain_two = jnp.clip(1.0 + 0.18 * jax.random.normal(arg_keys[14], (D,), jnp.float32), 0.099609375, 1.8984375).astype(jnp.bfloat16)
    bias_two = bell_draw(arg_keys[15], (D,), 0.5, 3.0, ((0, 8),))
    gain_three = jnp.clip(1.0 + 0.18 * jax.random.normal(arg_keys[16], (D,), jnp.float32), 0.099609375, 1.8984375).astype(jnp.bfloat16)
    bias_three = bell_draw(arg_keys[17], (D,), 0.5, 3.0, ((0, 8),))
    return dict(inputs=inputs, memory=memory, tgt_len=tgt_len, src_len=src_len, cotangent=cotangent, w_qkv=w_qkv, w_out=w_out, cross_query=cross_query, cross_kv=cross_kv, cross_out=cross_out, ffn_up=ffn_up, ffn_down=ffn_down, gain_one=gain_one, bias_one=bias_one, gain_two=gain_two, bias_two=bias_two, gain_three=gain_three, bias_three=bias_three)


@jax.custom_vjp
def low(v):
    return lax.optimization_barrier(v.astype(jnp.bfloat16)).astype(jnp.float32)

@jax.custom_vjp
def low_back(v):
    return v

def low_keep(v):
    return (low(v), None)

def low_pass(kept, grad):
    return (grad,)

def back_keep(v):
    return (v, None)

def back_low(kept, grad):
    return (low(grad),)
low.defvjp(low_keep, low_pass)
low_back.defvjp(back_keep, back_low)
EPSILON = 1e-05
HIGHEST = lax.Precision.HIGHEST

def matmul(left_side, right_side):
    return jnp.dot(left_side, right_side, precision=HIGHEST)

def layer_norm(values, gain_vec, bias_vec):
    center = values - lax.optimization_barrier(jnp.mean(values, axis=-1, keepdims=True))
    spread = lax.optimization_barrier(jnp.mean(center * center, axis=-1, keepdims=True))
    return center * lax.rsqrt(spread + EPSILON) * gain_vec + bias_vec

def attention(queries, key_rows, value_rows, live_mask):
    query_heads = queries.reshape(queries.shape[0], HEADS, DH)
    key_heads = key_rows.reshape(key_rows.shape[0], HEADS, DH)
    value_heads = value_rows.reshape(value_rows.shape[0], HEADS, DH)
    scores = jnp.einsum('qhd,khd->hqk', query_heads, key_heads, precision=HIGHEST)
    scores = low_back(scores * DH ** (-0.5))
    allowed = jnp.broadcast_to(live_mask[None], scores.shape)
    safe = jnp.where(allowed, scores, jnp.zeros_like(scores))
    row_max = lax.optimization_barrier(jnp.max(jnp.where(allowed, scores, jnp.full_like(scores, -1e+30)), axis=-1, keepdims=True))
    shifted = jnp.where(allowed, jnp.exp(safe - row_max), jnp.zeros_like(scores))
    weights = shifted / lax.optimization_barrier(jnp.sum(shifted, axis=-1, keepdims=True))
    mixture = jnp.einsum('hqk,khd->qhd', low(weights), value_heads, precision=HIGHEST)
    return mixture.reshape(queries.shape[0], HEADS * DH)

def one_sequence(params, values, memory, tgt_count, src_count):
    w_qkv, w_out, cross_query, cross_kv, cross_out, ffn_up, ffn_down, gain_one, bias_one, gain_two, bias_two, gain_three, bias_three = params
    tgt_count = tgt_count.astype(jnp.int32)
    src_count = src_count.astype(jnp.int32)
    row_ids = jnp.arange(SLOT, dtype=jnp.int32)
    src_ids = jnp.arange(SRC, dtype=jnp.int32)
    self_live = (row_ids[None, :] <= row_ids[:, None]) & (row_ids[None, :] < tgt_count)
    cross_live = jnp.broadcast_to(src_ids[None, :] < src_count, (SLOT, SRC))
    live_rows = jnp.where(row_ids < tgt_count, 1.0, 0.0).astype(values.dtype)[:, None]
    normed = low(layer_norm(values, gain_one, bias_one))
    queries = low_back(low(matmul(normed, w_qkv[0])))
    key_rows = low_back(low(matmul(normed, w_qkv[1])))
    value_rows = low_back(low(matmul(normed, w_qkv[2])))
    mixture = low_back(low(attention(queries, key_rows, value_rows, self_live)))
    hidden_one = values + low_back(matmul(mixture, w_out))
    normed = low(layer_norm(hidden_one, gain_two, bias_two))
    queries = low_back(low(matmul(normed, cross_query)))
    key_rows = low_back(low(matmul(memory, cross_kv[0])))
    value_rows = low_back(low(matmul(memory, cross_kv[1])))
    mixture = low_back(low(attention(queries, key_rows, value_rows, cross_live)))
    hidden_two = hidden_one + low_back(matmul(mixture, cross_out))
    normed = low(layer_norm(hidden_two, gain_three, bias_three))
    before = low_back(matmul(normed, ffn_up))
    active = low(jax.nn.gelu(before, approximate=True))
    return live_rows * (hidden_two + low_back(matmul(active, ffn_down)))

def reference(inputs, memory, tgt_len, src_len, cotangent, w_qkv, w_out, cross_query, cross_kv, cross_out, ffn_up, ffn_down, gain_one, bias_one, gain_two, bias_two, gain_three, bias_three):
    params = tuple((operand.astype(jnp.float32) for operand in (w_qkv, w_out, cross_query, cross_kv, cross_out, ffn_up, ffn_down, gain_one, bias_one, gain_two, bias_two, gain_three, bias_three)))
    tgt_counts = tgt_len.astype(jnp.int32)
    src_counts = src_len.astype(jnp.int32)
    values_in = inputs.astype(jnp.float32)
    encoded_in = memory.astype(jnp.float32)

    def forward(params, values, encoded):

        def advance(carry, members):
            return (carry, jax.checkpoint(one_sequence)(params, members[0], members[1], members[2], members[3]))
        start = jnp.zeros((), jnp.float32)
        _, outputs = lax.scan(advance, start, (values, encoded, tgt_counts, src_counts))
        return outputs
    outputs, pull = jax.vjp(forward, params, values_in, encoded_in)
    grads, grad_values, grad_encoded = pull(cotangent.astype(jnp.float32))
    return (outputs.astype(jnp.bfloat16), grad_values, grad_encoded, grads[0], grads[1], grads[2], grads[3], grads[4], grads[5], grads[6], grads[7], grads[8], grads[9], grads[10], grads[11], grads[12])
```

```python
import functools

import jax
import jax.numpy as jnp
from jax import lax
from jax.experimental import pallas as pl
from jax.experimental.pallas import tpu as pltpu
from jax.sharding import PartitionSpec as P

DH = 64
LANES = 128
EPSILON = 1e-05
MASKED = -1e30
F32 = jnp.float32
BF16 = jnp.bfloat16
MESH = pl.DeviceIdType.MESH
HIGHEST = lax.Precision.HIGHEST


def nn(a, b):
    return lax.dot_general(a, b, (((1,), (0,)), ((), ())), preferred_element_type=F32)


def nt(a, b):
    return lax.dot_general(a, b, (((1,), (1,)), ((), ())), preferred_element_type=F32)


def normalize(values):
    center = values - jnp.mean(values, axis=-1, keepdims=True)
    spread = jnp.mean(center * center, axis=-1, keepdims=True)
    inv = lax.rsqrt(spread + EPSILON)
    return center * inv, inv


def norm_grad(values, grad, gain):
    xhat, inv = normalize(values)
    e = grad * gain
    back = inv * (
        e
        - jnp.mean(e, axis=-1, keepdims=True)
        - xhat * jnp.mean(e * xhat, axis=-1, keepdims=True)
    )
    return (
        back,
        jnp.sum(grad * xhat, axis=0, keepdims=True),
        jnp.sum(grad, axis=0, keepdims=True),
    )


def gelu_both(v):
    c = 0.7978845608028654
    v2 = v * v
    t = jnp.tanh(v * (c + (c * 0.044715) * v2))
    half = 0.5 * (1.0 + t)
    slope = half + (0.5 * v) * (1.0 - t * t) * (c + (3.0 * c * 0.044715) * v2)
    return v * half, slope


def layer_kernel(cfg, *refs):
    fused, nz, ny, rb, own, wide, nf = cfg
    rows_all = 4 * own
    nseg = 8 + 2 * nf
    gseg = nseg
    refs = list(refs)

    def take(count):
        got, refs[:count] = refs[:count], []
        return got

    x_ref, m_ref, c_ref, tl_ref, sl_ref = take(5)
    if fused:
        wqkv_ref, wo_ref, cq_ref, ckv_ref, co_ref, up_ref, dn_ref = take(7)
        gain_refs = take(6)
    else:
        wfull_ref, gfull_ref = take(2)
    out_ref, gi_ref, gm_ref, gw_ref = take(4)
    (xs, ms, cs, wg, gains, n1, n2, n3, h1, h2, gh, gb16, qs, ks, vs, cqs, cks, cvs,
     vt, smix, cmix, slse, clse, act, gbf, dm, dq, dka, dva, dk, dv, ps, pr, ys, yr,
     us, ur, outs, osend, gis, gisend, gms, gmsend, gs, bias, gacc) = take(46)
    if fused:
        pack, gz, gy, rx, hx, ry, hy, rz = take(8)
    ssem, rsem, xss, xrs, lsem = take(5)

    p = lax.axis_index("tensor") // 2
    c = lax.axis_index("tensor") % 2
    t = 2 * p + c
    tx = 2 * (1 - p) + c
    dp_at = lax.axis_index("dp")
    core_peer = {"dp": dp_at, "tensor": 2 * p + 1 - c}
    x_peer = {"dp": dp_at, "tensor": tx}
    z = dp_at // ny
    y = dp_at % ny
    y_peer = {"dp": z * ny + (1 - y), "tensor": t}

    def z_peer(k):
        return {"dp": ((z + k) % nz) * ny + y, "tensor": t}

    counter = [0]
    sent = []

    def push(src, dst, peer):
        i = counter[0]
        counter[0] += 1
        cp = pltpu.make_async_remote_copy(
            src, dst, ssem.at[i], rsem.at[i], device_id=peer, device_id_type=MESH
        )
        cp.start()
        sent.append(cp)
        return cp

    lcount = [0]
    local_open = []

    def local(src, dst):
        cp = pltpu.make_async_copy(src, dst, lsem.at[lcount[0]])
        lcount[0] += 1
        cp.start()
        return cp

    def rows(j, size=own):
        return pl.ds(pl.multiple_of(j * size, size), size)

    peers = [core_peer, x_peer]
    if fused:
        if ny > 1:
            peers.append(y_peer)
        peers += [z_peer(k) for k in range(1, nz)]
    barrier = pltpu.get_barrier_semaphore()
    for peer in peers:
        pl.semaphore_signal(barrier, inc=1, device_id=peer, device_id_type=MESH)
    pl.semaphore_wait(barrier, len(peers))

    def spread(src, buf):
        over = push(src.at[1 - p], buf.at[rows(t)], x_peer)
        keep = local(src.at[p], buf.at[rows(t)])
        near = push(src.at[p], buf.at[rows(t)], core_peer)
        return over, keep, near

    def settle(src_copies, buf):
        over, keep, near = src_copies
        over.wait_recv()
        relay = push(buf.at[rows(tx)], buf.at[rows(tx)], core_peer)
        keep.wait()
        near.wait_recv()
        return relay

    half = pl.ds(pl.multiple_of(p * LANES, LANES), LANES)
    other_half = pl.ds(pl.multiple_of((1 - p) * LANES, LANES), LANES)

    def gather_one(lo, hi):
        return [
            push(pack.at[lo:hi], wg.at[lo:hi, z, y, :, half], z_peer(k)) for k in range(1, nz)
        ]

    def gather_two(lo, hi, prior):
        for cp in prior:
            cp.wait_recv()
        if ny == 1:
            return []
        part = wg.at[lo:hi, :, y, :, half]
        return [push(part, part, y_peer)]

    def gather_three(lo, hi, prior):
        for cp in prior:
            cp.wait_recv()
        part = wg.at[lo:hi, :, :, :, half]
        return [push(part, part, x_peer)]

    def weight(s):
        return wg[s].reshape(nz * ny * rb, 2 * LANES)

    xin = spread(x_ref, xs)
    if fused:
        eye = (
            lax.broadcasted_iota(jnp.int32, (rb, rb), 0)
            == lax.broadcasted_iota(jnp.int32, (rb, rb), 1)
        ).astype(BF16)
        pack[0:3] = wqkv_ref[...]
        pack[3] = nt(eye, wo_ref[...]).astype(BF16)
        pack[4] = cq_ref[...]
        pack[5:7] = ckv_ref[...]
        pack[7] = nt(eye, co_ref[...]).astype(BF16)
        ga = gather_one(0, 3)
        place = (
            lax.broadcasted_iota(jnp.int32, (rb, wide), 0) + dp_at * rb
            == lax.broadcasted_iota(jnp.int32, (rb, wide), 1)
        ).astype(BF16)
        gz[0] = jnp.zeros((16, wide), BF16)
        for i in range(6):
            gz[0, i : i + 1, :] = nn(gain_refs[i][...], place).astype(BF16)
        gcp = [push(gz.at[0], gz.at[k], z_peer(k)) for k in range(1, nz)]
        for i in range(nf):
            pack[8 + i] = up_ref[:, i * LANES : (i + 1) * LANES]
            pack[8 + nf + i] = nt(eye, dn_ref[i * LANES : (i + 1) * LANES, :]).astype(BF16)
        wg[:, z, y, :, half] = pack[...]
        for cp in gcp:
            cp.wait_recv()
        total = gz[0].astype(F32)
        for k in range(1, nz):
            total = total + gz[k].astype(F32)
        if ny > 1:
            gy[0] = total.astype(BF16)
            gcp = push(gy.at[0], gy.at[1], y_peer)
            gcp.wait_recv()
            total = total + gy[1].astype(F32)
        gains[...] = total
        ga = gather_two(0, 3, ga)
        go = gather_one(3, 4)
        gb = gather_one(4, 8)
    else:
        wcp = local(wfull_ref, wg)
        gains[...] = gfull_ref[...]
        wcp.wait()
    min_ = spread(m_ref, ms)
    cin = spread(c_ref, cs)

    relay = settle(xin, xs)
    relay.wait_recv()

    sub = min(64, own)
    per = own // sub
    gacc[...] = jnp.zeros_like(gacc)

    def norm_rows(i, _):
        r = rows(i, sub)
        xhat, _unused = normalize(xs[r, :].astype(F32))
        n1[r, :] = (xhat * gains[0:1, :] + gains[1:2, :]).astype(BF16)
        return 0

    lax.fori_loop(0, 4 * per, norm_rows, 0)

    if fused:
        ga = gather_three(0, 3, ga)
        go = gather_two(3, 4, go)
        gb = gather_two(4, 8, gb)
        gc = gather_one(8, nseg)
        for cp in ga:
            cp.wait_recv()

    def put_pairs(buf, r, value):
        v = value.astype(BF16)
        buf[0, r, :] = v[:, :LANES]
        buf[1, r, :] = v[:, LANES:]

    def pairs(buf, r):
        return jnp.concatenate([buf[0, r, :], buf[1, r, :]], axis=1)

    scale = DH ** (-0.5)

    def put_transposed(buf, r, value):
        vt_ = value.T.astype(BF16)
        buf[0, :, r] = vt_[:LANES]
        buf[1, :, r] = vt_[LANES:]

    def project(j, _):
        r = rows(j)
        rowsv = n1[r, :]
        put_pairs(qs, r, nn(rowsv, weight(0)).astype(BF16) * jnp.asarray(scale, BF16))
        put_pairs(ks, r, nn(rowsv, weight(1)))
        val = nn(rowsv, weight(2))
        put_pairs(vs, r, val)
        put_transposed(vt, r, val.astype(BF16).astype(F32))
        return 0

    lax.fori_loop(0, 4, project, 0)

    if fused:
        go = gather_three(3, 4, go)
        gb = gather_three(4, 8, gb)
        gc = gather_two(8, nseg, gc)

    def only(value, u):
        lane = lax.broadcasted_iota(jnp.int32, value.shape, 1)
        keep = (lane // DH) == u
        return jnp.where(keep, value, jnp.zeros_like(value))

    def causal_mask(scores, keys):
        tail = scores[keys - own :]
        key_at = lax.broadcasted_iota(jnp.int32, tail.shape, 0)
        query_at = lax.broadcasted_iota(jnp.int32, tail.shape, 1)
        tail = jnp.where(key_at <= query_at, tail, MASKED)
        if keys == own:
            return tail
        return jnp.concatenate([scores[: keys - own], tail], axis=0)

    def masked(scores, keys, causal):
        if causal:
            return causal_mask(scores, keys)
        b = bias[...]
        return scores + jnp.concatenate([b] * (own // LANES), axis=1)

    def attend(q_s, k_s, v_t, mix, lse, r, keys, causal):
        def pair(pp, _):
            q = q_s[pp, r, :]
            k = k_s[pp, 0:keys, :]
            parts = []
            for u in range(2):
                s = masked(nt(only(k, u), q), keys, causal)
                top = jnp.max(s, axis=0, keepdims=True)
                e = jnp.exp(s - top)
                total = jnp.sum(e, axis=0, keepdims=True)
                o = nn(v_t[pp, u * DH : (u + 1) * DH, 0:keys], e.astype(BF16))
                parts.append(o * (1.0 / total))
                lse[2 * pp + u, :, r] = top + jnp.log(total)
            mix[pp, r, :] = jnp.concatenate(parts, axis=0).T.astype(BF16)
            return 0

        lax.fori_loop(0, 2, pair, 0)

    def exchange(point, j):
        b = point % 2
        i = point * 4 + j
        return pltpu.make_async_remote_copy(
            ps.at[b, rows(j)], pr.at[b, rows(j)], xss.at[i], xrs.at[i],
            device_id=core_peer, device_id_type=MESH,
        )

    def send_sum(point, j, value):
        ps[point % 2, rows(j), :] = value.astype(BF16)
        exchange(point, j).start()

    def summed(point, r):
        b = point % 2
        return ps[b, r, :].astype(F32) + pr[b, r, :].astype(F32)

    for j in range(4):
        r = rows(j)
        attend(qs, ks, vt, smix, slse, r, own * (j + 1), True)
        if fused and j == 0:
            for cp in go:
                cp.wait_recv()
        send_sum(0, j, nt(pairs(smix, r), weight(3)))
        if j == 1:
            mrelay = settle(min_, ms)

    if fused:
        for cp in gb:
            cp.wait_recv()
        gc = gather_three(8, nseg, gc)
    mrelay.wait_recv()

    key_at = lax.broadcasted_iota(jnp.int32, (rows_all, LANES), 0)
    bias[...] = jnp.where(key_at < sl_ref[p], 0.0, MASKED)

    def project_cross(j, _):
        r = rows(j)
        rowsv = ms[r, :]
        put_pairs(cks, r, nn(rowsv, weight(5)))
        val = nn(rowsv, weight(6))
        put_pairs(cvs, r, val)
        put_transposed(vt, r, val.astype(BF16).astype(F32))
        return 0

    lax.fori_loop(0, 4, project_cross, 0)

    def second(j, _):
        exchange(0, j).wait_recv()
        exchange(0, j).wait_send()

        def part(i, _):
            r = rows(j * per + i, sub)
            h = xs[r, :].astype(F32) + summed(0, r)
            h1[r, :] = h
            xhat, _unused = normalize(h)
            n2[r, :] = (xhat * gains[2:3, :] + gains[3:4, :]).astype(BF16)
            return 0

        lax.fori_loop(0, per, part, 0)
        r = rows(j)
        put_pairs(cqs, r, nn(n2[r, :], weight(4)).astype(BF16) * jnp.asarray(scale, BF16))
        return 0

    lax.fori_loop(0, 4, second, 0)

    def cross_block(j, _):
        r = rows(j)
        attend(cqs, cks, vt, cmix, clse, r, rows_all, False)
        send_sum(1, j, nt(pairs(cmix, r), weight(7)))
        return 0

    lax.fori_loop(0, 4, cross_block, 0)
    crelay = settle(cin, cs)
    crelay.wait_recv()
    if fused:
        for cp in gc:
            cp.wait_recv()

    limit = tl_ref[p]

    def live(r_first, size):
        at = lax.broadcasted_iota(jnp.int32, (size, wide), 0) + r_first
        return at < limit

    def third(j, _):
        exchange(1, j).wait_recv()
        exchange(1, j).wait_send()

        def part(i, _):
            r = rows(j * per + i, sub)
            h = h1[r, :] + summed(1, r)
            h2[r, :] = h
            xhat, _unused = normalize(h)
            n3[r, :] = (xhat * gains[4:5, :] + gains[5:6, :]).astype(BF16)
            first = (j * per + i) * sub
            cot = cs[r, :]
            gb16[r, :] = jnp.where(live(first, sub), cot, jnp.zeros_like(cot))
            return 0

        lax.fori_loop(0, per, part, 0)
        r = rows(j)
        rowsv = n3[r, :]
        cot = gb16[r, :]
        for s in range(nf):
            before = nn(rowsv, weight(8 + s))
            active, slope = gelu_both(before)
            act[s, r, :] = active.astype(BF16)
            gbf[s, r, :] = (nn(cot, weight(8 + nf + s)) * slope).astype(BF16)
        back = nt(gbf[0, r, :], weight(8))
        for s in range(1, nf):
            back = back + nt(gbf[s, r, :], weight(8 + s))
        send_sum(2, j, back)
        val = nt(act[0, r, :], weight(8 + nf))
        for s in range(1, nf):
            val = val + nt(act[s, r, :], weight(8 + nf + s))
        ys[r, :] = val.astype(BF16)
        return 0

    lax.fori_loop(0, 4, third, 0)

    ycp = [
        push(ys.at[rows(2 * k + 1 - c)], yr.at[k], core_peer) for k in range(2)
    ]

    def weight_grads(a_buf, items):
        chunk = ny * rb
        for zi in range(nz):
            at = a_buf[:, zi * chunk : (zi + 1) * chunk].T
            for s, load in items:
                gs[s, zi] = nn(at, load()).astype(BF16).reshape(ny, rb, 2 * LANES)

    every = pl.ds(0, rows_all)

    def whole(buf):
        return lambda: pairs(buf, every)

    def plane(buf, s):
        return lambda: buf[s]

    weight_grads(gb16, [(8 + nf + s, plane(act, s)) for s in range(nf)])
    weight_grads(n3, [(8 + s, plane(gbf, s)) for s in range(nf)])

    def reduce_one(lo, hi):
        return push(gs.at[lo:hi, :, :, :, other_half], rx.at[lo:hi], x_peer)

    def reduce_two(lo, hi, prior):
        prior.wait_recv()
        def one(s, _):
            mine = gs[s, :, :, :, half].astype(F32)
            hx[s] = (mine + rx[s].astype(F32)).astype(BF16)
            return 0
        lax.fori_loop(lo, hi, one, 0)
        if ny == 1:
            return None
        return push(hx.at[lo:hi, :, 1 - y], ry.at[lo:hi], y_peer)

    def reduce_three(lo, hi, prior):
        if prior is not None:
            prior.wait_recv()
        def one(s, _):
            v = hx[s, :, y].astype(F32)
            if ny > 1:
                v = v + ry[s].astype(F32)
            hy[s] = v.astype(BF16)
            return 0
        lax.fori_loop(lo, hi, one, 0)
        return [
            push(hy.at[lo:hi, (z + k) % nz], rz.at[k - 1, lo:hi], z_peer(k))
            for k in range(1, nz)
        ]

    def reduce_done(lo, hi, prior):
        for cp in prior:
            cp.wait_recv()
        def one(s, _):
            v = hy[s, z].astype(F32)
            for k in range(1, nz):
                v = v + rz[k - 1, s].astype(F32)
            gw_ref[s] = v
            return 0
        lax.fori_loop(lo, hi, one, 0)

    if fused:
        rf = reduce_one(8, nseg)

    def finish_rows(k, dst):
        def part(i, _):
            r = rows((2 * k + c) * per + i, sub)
            q = rows(i, sub)
            val = h2[r, :] + ys[r, :].astype(F32) + yr[k, q, :].astype(F32)
            keep = live(((2 * k + c) * per + i) * sub, sub)
            dst[q, :] = jnp.where(keep, val, 0.0).astype(BF16)
            return 0
        lax.fori_loop(0, per, part, 0)

    for cp in ycp:
        cp.wait_recv()
    finish_rows(1 - p, osend)
    ocp = push(osend, outs.at[p], x_peer)
    finish_rows(p, outs.at[p])

    def back_three(j, _):
        exchange(2, j).wait_recv()
        exchange(2, j).wait_send()

        def part(i, _):
            r = rows(j * per + i, sub)
            dx, dgain, dbias = norm_grad(h2[r, :], summed(2, r), gains[4:5, :])
            gacc[4:5, :] += dgain
            gacc[5:6, :] += dbias
            g = gb16[r, :].astype(F32) + dx
            gh[r, :] = g
            gb16[r, :] = g.astype(BF16)
            return 0

        return lax.fori_loop(0, per, part, 0)

    lax.fori_loop(0, 4, back_three, 0)

    if fused:
        rf = reduce_two(8, nseg, rf)

    sel_row = lax.broadcasted_iota(jnp.int32, (8, LANES), 0)
    sel_lane = lax.broadcasted_iota(jnp.int32, (8, LANES), 1)
    selector = (sel_lane // DH == sel_row).astype(F32)

    def attend_back(q_s, k_s, kt, v_s, mix, lse, r, keys, causal):
        def pair(pp, _):
            q = q_s[pp, r, :]
            k = k_s[pp, 0:keys, :]
            v = v_s[pp, 0:keys, :]
            do = dm[pp, r, :]
            prod = do.astype(F32) * mix[pp, r, :].astype(F32)
            delta = lax.dot_general(
                selector, prod, (((1,), (1,)), ((), ())),
                precision=HIGHEST, preferred_element_type=F32,
            )
            parts = []
            dvp = None
            for u in range(2):
                s = masked(nt(only(k, u), q), keys, causal)
                e = jnp.exp(s - lse[2 * pp + u, :, r])
                d = nt(only(v, u), do)
                ds = (e * (d - delta[u : u + 1])).astype(BF16)
                dv_u = nn(e.astype(BF16), only(do, u))
                dk_u = nn(ds, only(q, u))
                dvp = dv_u if dvp is None else dvp + dv_u
                dkp = dk_u if u == 0 else dkp + dk_u
                parts.append(nn(kt[pp, u * DH : (u + 1) * DH, 0:keys], ds) * scale)
            dka[pp, 0:keys, :] += dkp
            dva[pp, 0:keys, :] += dvp
            dq[pp, r, :] = jnp.concatenate(parts, axis=0).T.astype(BF16)
            return 0

        lax.fori_loop(0, 2, pair, 0)

    def transpose_keys(buf):
        def one(j, _):
            r = rows(j)
            for pp in range(2):
                vt[pp, :, r] = buf[pp, r, :].astype(F32).T.astype(BF16)
            return 0
        lax.fori_loop(0, 4, one, 0)

    transpose_keys(cks)
    dka[...] = jnp.zeros_like(dka)
    dva[...] = jnp.zeros_like(dva)

    def cross_back(j, _):
        r = rows(j)
        put_pairs(dm, r, nn(gb16[r, :], weight(7)))
        attend_back(cqs, cks, vt, cvs, cmix, clse, r, rows_all, False)
        send_sum(3, j, nt(pairs(dq, r), weight(4)))
        return 0

    lax.fori_loop(0, 4, cross_back, 0)
    if fused:
        rf = reduce_three(8, nseg, rf)

    def cross_back_keys(j, _):
        r = rows(j)
        for pp in range(2):
            dk[pp, r, :] = dka[pp, r, :].astype(BF16)
            dv[pp, r, :] = dva[pp, r, :].astype(BF16)
        val = nt(pairs(dk, r), weight(5)) + nt(pairs(dv, r), weight(6))
        us[r, :] = val.astype(BF16)
        return 0

    lax.fori_loop(0, 4, cross_back_keys, 0)
    ucp = [
        push(us.at[rows(2 * k + 1 - c)], ur.at[k], core_peer) for k in range(2)
    ]
    weight_grads(gb16, [(7, whole(cmix))])
    weight_grads(n2, [(4, whole(dq))])
    weight_grads(ms, [(5, whole(dk)), (6, whole(dv))])

    def memory_rows(k, dst):
        def part(i, _):
            r = rows((2 * k + c) * per + i, sub)
            q = rows(i, sub)
            dst[q, :] = (us[r, :].astype(F32) + ur[k, q, :].astype(F32)).astype(BF16)
            return 0
        lax.fori_loop(0, per, part, 0)

    for cp in ucp:
        cp.wait_recv()
    memory_rows(1 - p, gmsend)
    mcp = push(gmsend, gms.at[p], x_peer)
    memory_rows(p, gms.at[p])

    def back_two(j, _):
        exchange(3, j).wait_recv()
        exchange(3, j).wait_send()

        def part(i, _):
            r = rows(j * per + i, sub)
            dx, dgain, dbias = norm_grad(h1[r, :], summed(3, r), gains[2:3, :])
            gacc[2:3, :] += dgain
            gacc[3:4, :] += dbias
            g = gh[r, :] + dx
            gh[r, :] = g
            gb16[r, :] = g.astype(BF16)
            return 0

        return lax.fori_loop(0, per, part, 0)

    lax.fori_loop(0, 4, back_two, 0)
    weight_grads(gb16, [(3, whole(smix))])
    if fused:
        reduce_done(8, nseg, rf)
        rc = reduce_one(3, 8)

    transpose_keys(ks)
    dka[...] = jnp.zeros_like(dka)
    dva[...] = jnp.zeros_like(dva)
    for j in reversed(range(4)):
        r = rows(j)
        put_pairs(dm, r, nn(gb16[r, :], weight(3)))
        attend_back(qs, ks, vt, vs, smix, slse, r, own * (j + 1), True)
        for pp in range(2):
            dk[pp, r, :] = dka[pp, r, :].astype(BF16)
            dv[pp, r, :] = dva[pp, r, :].astype(BF16)
        val = nt(pairs(dq, r), weight(0)) + nt(pairs(dk, r), weight(1))
        send_sum(4, j, val + nt(pairs(dv, r), weight(2)))
        if fused and j == 3:
            rc = reduce_two(3, 8, rc)
        if fused and j == 2:
            rc = reduce_three(3, 8, rc)

    weight_grads(n1, [(0, whole(dq)), (1, whole(dk)), (2, whole(dv))])
    if fused:
        rt = reduce_one(0, 3)
        reduce_done(3, 8, rc)

    def back_one(k, j, dst):
        exchange(4, j).wait_recv()

        def part(i, _):
            r = rows(j * per + i, sub)
            q = rows(i, sub)
            dx, dgain, dbias = norm_grad(xs[r, :].astype(F32), summed(4, r), gains[0:1, :])
            gacc[0:1, :] += dgain
            gacc[1:2, :] += dbias
            if dst is not None:
                dst[q, :] = (gh[r, :] + dx).astype(BF16)
            return 0

        lax.fori_loop(0, per, part, 0)

    back_one(0, tx, gisend)
    icp = push(gisend, gis.at[p], x_peer)
    back_one(0, t, gis.at[p])
    back_one(0, 2 * p + 1 - c, None)
    back_one(0, 2 * (1 - p) + 1 - c, None)
    for j in range(4):
        exchange(4, j).wait_send()

    spread_rows = jnp.concatenate(
        [gacc[...], jnp.zeros((LANES - 8, wide), F32)], axis=0
    )
    columns = spread_rows.T.astype(BF16)
    gs[gseg] = jnp.concatenate([columns, columns], axis=1).reshape(nz, ny, rb, 2 * LANES)

    if fused:
        rg = reduce_one(gseg, gseg + 1)
        rt = reduce_two(0, 3, rt)
        rg = reduce_two(gseg, gseg + 1, rg)
        rt = reduce_three(0, 3, rt)
        rg = reduce_three(gseg, gseg + 1, rg)
        reduce_done(0, 3, rt)
        reduce_done(gseg, gseg + 1, rg)
    else:
        last = [local(gs, gw_ref)]

    ocp.wait_recv()
    mcp.wait_recv()
    icp.wait_recv()
    finals = [local(outs, out_ref), local(gms, gm_ref), local(gis, gi_ref)]
    if not fused:
        finals += last
    for cp in finals:
        cp.wait()
    for cp in sent:
        cp.wait_send()


def body(ndp, inputs, memory, tgt_len, src_len, cotangent, w_qkv, w_out, cross_query, cross_kv,
         cross_out, ffn_up, ffn_down, *gain_list):
    own, wide = inputs.shape[1], inputs.shape[2]
    rb = w_qkv.shape[1]
    nf = ffn_up.shape[1] // LANES
    nseg = 8 + 2 * nf
    rows_all = 4 * own
    fused = rb % 16 == 0
    if fused:
        ny = 2 if ndp % 2 == 0 else 1
        nz = ndp // ny
        block = rb
    else:
        ny, nz, block = 1, 1, wide
    cfg = (fused, nz, ny, block, own, wide, nf)

    any_spec = pl.BlockSpec(memory_space=pl.ANY)
    smem = pl.BlockSpec(memory_space=pltpu.SMEM)
    vmem = pl.BlockSpec(memory_space=pltpu.VMEM)
    operands = [inputs, memory, cotangent, tgt_len, src_len]
    specs = [any_spec] * 3 + [smem] * 2
    if fused:
        weights = [w_qkv, w_out, cross_query, cross_kv, cross_out, ffn_up, ffn_down]
        weights += [g[None, :] for g in gain_list]
        operands += weights
        specs += [vmem] * len(weights)
    else:
        pieces = [w_qkv, w_out.T[None], cross_query[None], cross_kv, cross_out.T[None]]
        pieces += [ffn_up.reshape(rb, nf, LANES).swapaxes(0, 1)]
        pieces += [ffn_down.reshape(nf, LANES, rb).swapaxes(1, 2)]
        packed = lax.all_gather(jnp.concatenate(pieces, axis=0), "dp", axis=1, tiled=True)
        index = lax.axis_index("tensor")
        flipped = lax.ppermute(packed, "tensor", [(i, (i + 2) % 4) for i in range(4)])
        low = jnp.where(index < 2, packed, flipped)
        high = jnp.where(index < 2, flipped, packed)
        full = jnp.concatenate([low, high], axis=2)[:, None, None]
        gathered = lax.all_gather(jnp.stack(gain_list), "dp", axis=1, tiled=True)
        operands += [full, jnp.pad(gathered.astype(F32), ((0, 10), (0, 0)))]
        specs += [any_spec, vmem]

    bf = lambda *shape: pltpu.VMEM(shape, BF16)
    fl = lambda *shape: pltpu.VMEM(shape, F32)
    seq = (rows_all, wide)
    heads = (2, rows_all, LANES)
    scratch = [
        bf(*seq), bf(*seq), bf(*seq), bf(nseg, nz, ny, block, 2 * LANES), fl(16, wide),
        bf(*seq), bf(*seq), bf(*seq), fl(*seq), fl(*seq), fl(*seq), bf(*seq),
        bf(*heads), bf(*heads), bf(*heads), bf(*heads), bf(*heads), bf(*heads),
        bf(2, LANES, rows_all), bf(*heads), bf(*heads), fl(4, 1, rows_all), fl(4, 1, rows_all),
        bf(nf, rows_all, 2 * LANES), bf(nf, rows_all, 2 * LANES),
        bf(*heads), bf(*heads), fl(*heads), fl(*heads), bf(*heads), bf(*heads),
        bf(2, *seq), bf(2, *seq), bf(*seq), bf(2, own, wide), bf(*seq), bf(2, own, wide),
        bf(2, own, wide), bf(own, wide), bf(2, own, wide), bf(own, wide),
        bf(2, own, wide), bf(own, wide),
        bf(nseg + 1, nz, ny, block, 2 * LANES), fl(rows_all, LANES), fl(8, wide),
    ]
    if fused:
        scratch += [
            bf(nseg, block, LANES), bf(nz, 16, wide), bf(2, 16, wide),
            bf(nseg + 1, nz, ny, block, LANES), bf(nseg + 1, nz, ny, block, LANES),
            bf(nseg + 1, nz, block, LANES), bf(nseg + 1, nz, block, LANES),
            bf(max(nz - 1, 1), nseg + 1, block, LANES),
        ]
    dma = pltpu.SemaphoreType.DMA
    scratch += [dma((96,)), dma((96,)), dma((20,)), dma((20,)), dma((12,))]

    if fused:
        grads_shape = jax.ShapeDtypeStruct((nseg + 1, block, LANES), F32)
        grads_spec = vmem
    else:
        grads_shape = jax.ShapeDtypeStruct((nseg + 1, nz, ny, block, 2 * LANES), BF16)
        grads_spec = any_spec
    act_shape = jax.ShapeDtypeStruct(inputs.shape, BF16)
    output, grad_in, grad_mem, grads = pl.pallas_call(
        functools.partial(layer_kernel, cfg),
        out_shape=(act_shape, act_shape, act_shape, grads_shape),
        in_specs=specs,
        out_specs=(any_spec, any_spec, any_spec, grads_spec),
        scratch_shapes=scratch,
        compiler_params=pltpu.CompilerParams(
            collective_id=0, has_side_effects=True, vmem_limit_bytes=62 << 20
        ),
        name="layer",
    )(*operands)

    if not fused:
        mine = grads[:, 0, 0].astype(F32)
        index = lax.axis_index("tensor")
        low, high = mine[:, :, :LANES], mine[:, :, LANES:]
        keep = jnp.where(index < 2, low, high)
        give = jnp.where(index < 2, high, low)
        keep = keep + lax.ppermute(give, "tensor", [(i, (i + 2) % 4) for i in range(4)])
        grads = lax.psum_scatter(keep, "dp", scatter_dimension=1, tiled=True)

    def merge(blocks):
        return jnp.swapaxes(blocks, 0, 1).reshape(blocks.shape[1], -1)

    gain_grads = grads[nseg][:, :6].T
    return (
        output,
        grad_in.astype(F32),
        grad_mem.astype(F32),
        grads[0:3],
        grads[3].T,
        grads[4],
        grads[5:7],
        grads[7].T,
        merge(grads[8 : 8 + nf]),
        merge(grads[8 + nf : nseg]).T,
        gain_grads[0],
        gain_grads[1],
        gain_grads[2],
        gain_grads[3],
        gain_grads[4],
        gain_grads[5],
    )


def solution(mesh):
    return jax.shard_map(
        functools.partial(body, mesh.shape["dp"]),
        mesh=mesh,
        in_specs=(
            P("dp", "tensor", None),
            P("dp", "tensor", None),
            P("dp"),
            P("dp"),
            P("dp", "tensor", None),
            P(None, "dp", "tensor"),
            P("tensor", "dp"),
            P("dp", "tensor"),
            P(None, "dp", "tensor"),
            P("tensor", "dp"),
            P("dp", "tensor"),
            P("tensor", "dp"),
            P("dp"),
            P("dp"),
            P("dp"),
            P("dp"),
            P("dp"),
            P("dp"),
        ),
        out_specs=(
            P("dp", "tensor", None),
            P("dp", "tensor", None),
            P("dp", "tensor", None),
            P(None, "dp", "tensor"),
            P("tensor", "dp"),
            P("dp", "tensor"),
            P(None, "dp", "tensor"),
            P("tensor", "dp"),
            P("dp", "tensor"),
            P("tensor", "dp"),
            P("dp"),
            P("dp"),
            P("dp"),
            P("dp"),
            P("dp"),
            P("dp"),
        ),
        check_vma=False,
    )
```

```python
import functools

import jax
import jax.numpy as jnp
from jax import lax
from jax.experimental import pallas as pl
from jax.experimental.pallas import tpu as pltpu
from jax.sharding import PartitionSpec as P

DH = 64
LANES = 128
EPSILON = 1e-05
MASKED = -1e30
F32 = jnp.float32
BF16 = jnp.bfloat16
MESH = pl.DeviceIdType.MESH
HIGHEST = lax.Precision.HIGHEST


def nn(a, b):
    return lax.dot_general(a, b, (((1,), (0,)), ((), ())), preferred_element_type=F32)


def nt(a, b):
    return lax.dot_general(a, b, (((1,), (1,)), ((), ())), preferred_element_type=F32)


def normalize(values):
    center = values - jnp.mean(values, axis=-1, keepdims=True)
    spread = jnp.mean(center * center, axis=-1, keepdims=True)
    inv = lax.rsqrt(spread + EPSILON)
    return center * inv, inv


def norm_grad(values, grad, gain):
    xhat, inv = normalize(values)
    e = grad * gain
    back = inv * (
        e
        - jnp.mean(e, axis=-1, keepdims=True)
        - xhat * jnp.mean(e * xhat, axis=-1, keepdims=True)
    )
    return (
        back,
        jnp.sum(grad * xhat, axis=0, keepdims=True),
        jnp.sum(grad, axis=0, keepdims=True),
    )


def gelu_both(v):
    c = 0.7978845608028654
    v2 = v * v
    t = jnp.tanh(v * (c + (c * 0.044715) * v2))
    half = 0.5 * (1.0 + t)
    slope = half + (0.5 * v) * (1.0 - t * t) * (c + (3.0 * c * 0.044715) * v2)
    return v * half, slope


SUMS = (("xyz", 5), ("yxz", 5), ("yzx", 5))


def sum_shapes(order, segs, nz, ny, rows):
    shapes, left = [], {"x": 2 * LANES, "y": (ny,), "z": (nz,)}
    for i, axis in enumerate(order):
        left[axis] = LANES if axis == "x" else ()
        shape = (segs, *left["z"], *left["y"], rows, left["x"])
        shapes.append((nz - 1, *shape) if axis == "z" else shape)
        if i < 2:
            shapes.append(shape)
    return shapes


def layer_kernel(cfg, *refs):
    fused, nz, ny, rb, own, wide, nf = cfg
    rows_all = 4 * own
    nseg = 8 + 2 * nf
    gseg = 8
    refs = list(refs)

    def take(count):
        got, refs[:count] = refs[:count], []
        return got

    x_ref, m_ref, c_ref, tl_ref, sl_ref = take(5)
    if fused:
        wqkv_ref, wo_ref, cq_ref, ckv_ref, co_ref, up_ref, dn_ref = take(7)
        gain_refs = take(6)
    else:
        wfull_ref, gfull_ref = take(2)
    out_ref, gi_ref, gm_ref, gw_ref = take(4)
    (xs, ms, cs, wg, gains, n1, n2, n3, h1, h2, gh, gb16, qs, ks, vs, cqs, cks, cvs,
     vt, smix, cmix, slse, clse, act, gbf, dm, dq, dka, dva, dk, dv, ps, pr, ys, yr,
     us, ur, outs, osend, gis, gisend, gms, gmsend, gs, bias, gacc) = take(46)
    if fused:
        gz, gy = take(2)
        sums = {order: take(count) for order, count in SUMS}
    ssem, rsem, xss, xrs, lsem = take(5)

    p = lax.axis_index("tensor") // 2
    c = lax.axis_index("tensor") % 2
    t = 2 * p + c
    tx = 2 * (1 - p) + c
    dp_at = lax.axis_index("dp")
    core_peer = {"dp": dp_at, "tensor": 2 * p + 1 - c}
    x_peer = {"dp": dp_at, "tensor": tx}
    z = dp_at // ny
    y = dp_at % ny
    y_peer = {"dp": z * ny + (1 - y), "tensor": t}

    def z_peer(k):
        return {"dp": ((z + k) % nz) * ny + y, "tensor": t}

    counter = [0]
    sent = []

    def push(src, dst, peer):
        i = counter[0]
        counter[0] += 1
        cp = pltpu.make_async_remote_copy(
            src, dst, ssem.at[i], rsem.at[i], device_id=peer, device_id_type=MESH
        )
        cp.start()
        sent.append(cp)
        return cp

    lcount = [0]
    local_open = []

    def local(src, dst):
        cp = pltpu.make_async_copy(src, dst, lsem.at[lcount[0]])
        lcount[0] += 1
        cp.start()
        return cp

    def rows(j, size=own):
        return pl.ds(pl.multiple_of(j * size, size), size)

    peers = [core_peer, x_peer]
    if fused:
        peers.append(y_peer)
        peers += [z_peer(k) for k in range(1, nz)]
    barrier = pltpu.get_barrier_semaphore()
    for peer in peers:
        pl.semaphore_signal(barrier, inc=1, device_id=peer, device_id_type=MESH)

    half = pl.ds(pl.multiple_of(p * LANES, LANES), LANES)
    other_half = pl.ds(pl.multiple_of((1 - p) * LANES, LANES), LANES)

    if fused:
        own_part = [wqkv_ref[...], wo_ref[...][None], ckv_ref[...], cq_ref[...][None]]
        own_part.append(co_ref[...][None])
        at = 0
        for piece in own_part:
            wg[at : at + piece.shape[0], z, y, :, half] = piece
            at += piece.shape[0]
        for i in range(nf):
            wg[8 + i, z, y, :, half] = up_ref[:, i * LANES : (i + 1) * LANES]
            wg[8 + nf + i, z, y, :, half] = dn_ref[:, i * LANES : (i + 1) * LANES]
        place = (
            lax.broadcasted_iota(jnp.int32, (rb, wide), 0) + dp_at * rb
            == lax.broadcasted_iota(jnp.int32, (rb, wide), 1)
        ).astype(BF16)
        gz[0] = jnp.zeros((16, wide), BF16)
        for i in range(6):
            gz[0, i : i + 1, :] = nn(gain_refs[i][...], place).astype(BF16)
    pl.semaphore_wait(barrier, len(peers))

    def spread(src, buf):
        over = push(src.at[1 - p], buf.at[rows(t)], x_peer)
        keep = local(src.at[p], buf.at[rows(t)])
        near = push(src.at[p], buf.at[rows(t)], core_peer)
        return over, keep, near

    def settle(src_copies, buf):
        over, keep, near = src_copies
        over.wait_recv()
        relay = push(buf.at[rows(tx)], buf.at[rows(tx)], core_peer)
        keep.wait()
        near.wait_recv()
        return relay

    def gather(lo, hi, first, last, order):
        r = slice(first, last)
        zi, yi, lanes = z, y, half
        hops = []
        for axis in order:
            for cp in hops:
                cp.wait_recv()
            part = wg.at[lo:hi, zi, yi, r, lanes]
            if axis == "x":
                hops = [push(part, part, x_peer)]
                lanes = pl.ds(0, 2 * LANES)
            elif axis == "y":
                hops = [push(part, part, y_peer)]
                yi = slice(None)
            else:
                hops = [push(part, part, z_peer(k)) for k in range(1, nz)]
                zi = slice(None)
            yield
        for cp in hops:
            cp.wait_recv()
        yield

    def gathers(lo, hi, orders):
        if not fused:
            return []
        size = rb // len(orders)
        return [gather(lo, hi, i * size, (i + 1) * size, o) for i, o in enumerate(orders)]

    def step(parts):
        for part in parts:
            next(part)

    def weight(s):
        return wg[s].reshape(nz * ny * rb, 2 * LANES)

    xin = spread(x_ref, xs)
    wa = gathers(0, 3, ["zxy", "zyx"])
    wo_ = gathers(3, 4, ["zxy", "zyx"])
    wk = gathers(4, 6, ["zxy", "zyx"])
    wq = gathers(6, 8, ["zxy", "zyx"])
    wu = gathers(8, 8 + nf, ["xzy"])
    wd = gathers(8 + nf, nseg, ["xzy"])
    if fused:
        step(wa)
        gcp = [push(gz.at[0], gz.at[k], z_peer(k)) for k in range(1, nz)]
        step(wo_)
        step(wk)
        step(wq)
        step(wa)
        for cp in gcp:
            cp.wait_recv()
        total = gz[0].astype(F32)
        for k in range(1, nz):
            total = total + gz[k].astype(F32)
        gy[0] = total.astype(BF16)
        gcp = push(gy.at[0], gy.at[1], y_peer)
        step(wo_)
        relay = settle(xin, xs)
        gcp.wait_recv()
        total = total + gy[1].astype(F32)
        gains[...] = total
        step(wu)
        step(wd)
    else:
        wcp = local(wfull_ref, wg)
        gains[...] = gfull_ref[...]
        relay = settle(xin, xs)
        wcp.wait()
    relay.wait_recv()

    sub = min(64, own)
    per = own // sub
    gacc[...] = jnp.zeros_like(gacc)

    def norm_rows(i, _):
        r = rows(i, sub)
        xhat, _unused = normalize(xs[r, :].astype(F32))
        n1[r, :] = (xhat * gains[0:1, :] + gains[1:2, :]).astype(BF16)
        return 0

    lax.fori_loop(0, 4 * per, norm_rows, 0)
    step(wa)
    step(wo_)
    step(wk)
    min_ = spread(m_ref, ms)
    step(wa)

    def put_pairs(buf, r, value):
        v = value.astype(BF16)
        buf[0, r, :] = v[:, :LANES]
        buf[1, r, :] = v[:, LANES:]

    def pairs(buf, r):
        return jnp.concatenate([buf[0, r, :], buf[1, r, :]], axis=1)

    scale = DH ** (-0.5)

    def put_transposed(buf, r, value):
        vt_ = value.T.astype(BF16)
        buf[0, :, r] = vt_[:LANES]
        buf[1, :, r] = vt_[LANES:]

    def project(j, _):
        r = rows(j)
        rowsv = n1[r, :]
        put_pairs(qs, r, nn(rowsv, weight(0)).astype(BF16) * jnp.asarray(scale, BF16))
        put_pairs(ks, r, nn(rowsv, weight(1)))
        val = nn(rowsv, weight(2))
        put_pairs(vs, r, val)
        put_transposed(vt, r, val.astype(BF16).astype(F32))
        return 0

    lax.fori_loop(0, 4, project, 0)


    def only(value, u):
        lane = lax.broadcasted_iota(jnp.int32, value.shape, 1)
        keep = (lane // DH) == u
        return jnp.where(keep, value, jnp.zeros_like(value))

    def causal_mask(scores, keys):
        tail = scores[keys - own :]
        key_at = lax.broadcasted_iota(jnp.int32, tail.shape, 0)
        query_at = lax.broadcasted_iota(jnp.int32, tail.shape, 1)
        tail = jnp.where(key_at <= query_at, tail, MASKED)
        if keys == own:
            return tail
        return jnp.concatenate([scores[: keys - own], tail], axis=0)

    def masked(scores, keys, causal):
        if causal:
            return causal_mask(scores, keys)
        b = bias[...]
        return scores + jnp.concatenate([b] * (own // LANES), axis=1)

    def attend(q_s, k_s, v_t, mix, lse, r, keys, causal):
        def pair(pp, _):
            q = q_s[pp, r, :]
            k = k_s[pp, 0:keys, :]
            parts = []
            for u in range(2):
                s = masked(nt(only(k, u), q), keys, causal)
                top = jnp.max(s, axis=0, keepdims=True)
                e = jnp.exp(s - top)
                total = jnp.sum(e, axis=0, keepdims=True)
                o = nn(v_t[pp, u * DH : (u + 1) * DH, 0:keys], e.astype(BF16))
                parts.append(o * (1.0 / total))
                lse[2 * pp + u, :, r] = top + jnp.log(total)
            mix[pp, r, :] = jnp.concatenate(parts, axis=0).T.astype(BF16)
            return 0

        lax.fori_loop(0, 2, pair, 0)

    def exchange(point, j):
        b = point % 2
        i = point * 4 + j
        return pltpu.make_async_remote_copy(
            ps.at[b, rows(j)], pr.at[b, rows(j)], xss.at[i], xrs.at[i],
            device_id=core_peer, device_id_type=MESH,
        )

    def send_sum(point, j, value):
        ps[point % 2, rows(j), :] = value.astype(BF16)
        exchange(point, j).start()

    def summed(point, r):
        b = point % 2
        return ps[b, r, :].astype(F32) + pr[b, r, :].astype(F32)

    for j in range(4):
        r = rows(j)
        attend(qs, ks, vt, smix, slse, r, own * (j + 1), True)
        if j == 0:
            step(wo_)
            step(wu)
        send_sum(0, j, nt(pairs(smix, r), weight(3)))
        if j == 1:
            step(wk)
            step(wq)
        if j == 2:
            mrelay = settle(min_, ms)
            step(wd)
    step(wk)
    step(wq)
    cin = spread(c_ref, cs)
    mrelay.wait_recv()

    key_at = lax.broadcasted_iota(jnp.int32, (rows_all, LANES), 0)
    bias[...] = jnp.where(key_at < sl_ref[p], 0.0, MASKED)

    def project_cross(j, _):
        r = rows(j)
        rowsv = ms[r, :]
        put_pairs(cks, r, nn(rowsv, weight(4)))
        val = nn(rowsv, weight(5))
        put_pairs(cvs, r, val)
        put_transposed(vt, r, val.astype(BF16).astype(F32))
        return 0

    lax.fori_loop(0, 4, project_cross, 0)
    step(wq)

    def second(j, _):
        exchange(0, j).wait_recv()
        exchange(0, j).wait_send()

        def part(i, _):
            r = rows(j * per + i, sub)
            h = xs[r, :].astype(F32) + summed(0, r)
            h1[r, :] = h
            xhat, _unused = normalize(h)
            n2[r, :] = (xhat * gains[2:3, :] + gains[3:4, :]).astype(BF16)
            return 0

        lax.fori_loop(0, per, part, 0)
        r = rows(j)
        put_pairs(cqs, r, nn(n2[r, :], weight(6)).astype(BF16) * jnp.asarray(scale, BF16))
        return 0

    lax.fori_loop(0, 4, second, 0)

    def cross_block(j, _):
        r = rows(j)
        attend(cqs, cks, vt, cmix, clse, r, rows_all, False)
        send_sum(1, j, nt(pairs(cmix, r), weight(7)))
        return 0

    cross_block(0, 0)
    step(wu)
    cross_block(1, 0)
    cross_block(2, 0)
    step(wd)
    step(wu)
    cross_block(3, 0)
    crelay = settle(cin, cs)
    step(wd)
    crelay.wait_recv()

    limit = tl_ref[p]

    def live(r_first, size):
        at = lax.broadcasted_iota(jnp.int32, (size, wide), 0) + r_first
        return at < limit

    def third(j, _):
        exchange(1, j).wait_recv()
        exchange(1, j).wait_send()

        def part(i, _):
            r = rows(j * per + i, sub)
            h = h1[r, :] + summed(1, r)
            h2[r, :] = h
            xhat, _unused = normalize(h)
            n3[r, :] = (xhat * gains[4:5, :] + gains[5:6, :]).astype(BF16)
            first = (j * per + i) * sub
            cot = cs[r, :]
            gb16[r, :] = jnp.where(live(first, sub), cot, jnp.zeros_like(cot))
            return 0

        lax.fori_loop(0, per, part, 0)
        r = rows(j)
        rowsv = n3[r, :]
        cot = gb16[r, :]
        for s in range(nf):
            before = nn(rowsv, weight(8 + s))
            active, slope = gelu_both(before)
            act[s, r, :] = active.astype(BF16)
            gbf[s, r, :] = (nn(cot, weight(8 + nf + s)) * slope).astype(BF16)
        back = nt(gbf[0, r, :], weight(8))
        for s in range(1, nf):
            back = back + nt(gbf[s, r, :], weight(8 + s))
        send_sum(2, j, back)
        val = nt(act[0, r, :], weight(8 + nf))
        for s in range(1, nf):
            val = val + nt(act[s, r, :], weight(8 + nf + s))
        ys[r, :] = val.astype(BF16)
        return 0

    lax.fori_loop(0, 4, third, 0)

    ycp = [
        push(ys.at[rows(2 * k + 1 - c)], yr.at[k], core_peer) for k in range(2)
    ]

    def weight_grads(a_buf, items):
        chunk = ny * rb
        for zi in range(nz):
            at = a_buf[:, zi * chunk : (zi + 1) * chunk].T
            for s, load in items:
                gs[s, zi] = nn(at, load()).astype(BF16).reshape(ny, rb, 2 * LANES)

    every = pl.ds(0, rows_all)

    def whole(buf):
        return lambda: pairs(buf, every)

    def plane(buf, s):
        return lambda: buf[s]

    rh = rb // 2

    def reduce_part(lo, hi, base, first, last, order):
        r = slice(first, last)
        bufs = list(sums[order])
        gone = []

        def at(buf, s, zsel, ysel, lsel):
            index = [s]
            if "z" not in gone:
                index.append(zsel)
            if "y" not in gone:
                index.append(ysel)
            index += [slice(None) if buf is not gs else r, lsel]
            return tuple(index)

        every_one = slice(None)
        cur, shift = gs, 0
        for hop, axis in enumerate(order):
            span = slice(lo - shift, hi - shift)
            land = bufs.pop(0)
            to = slice(lo - base, hi - base)
            lanes = every_one if "x" in gone else slice(0, 2 * LANES)
            pick = {"z": every_one, "y": every_one, "x": lanes}
            here = dict(pick)
            if axis == "x":
                pick["x"], here["x"] = other_half, half
                sends = [(pick, land.at[to], x_peer)]
            elif axis == "y":
                pick["y"], here["y"] = 1 - y, y
                sends = [(pick, land.at[to], y_peer)]
            else:
                here["z"] = z
                sends = [
                    (dict(pick, z=(z + k) % nz), land.at[k - 1, to], z_peer(k))
                    for k in range(1, nz)
                ]
            cps = [
                push(cur.at[at(cur, span, sel["z"], sel["y"], sel["x"])], dst, peer)
                for sel, dst, peer in sends
            ]
            yield
            for cp in cps:
                cp.wait_recv()
            done = hop == 2
            acc = None if done else bufs.pop(0)

            def add(s, _):
                v = cur[at(cur, s - shift, here["z"], here["y"], here["x"])].astype(F32)
                if axis == "z":
                    for k in range(1, nz):
                        v = v + land[k - 1, s - base].astype(F32)
                else:
                    v = v + land[s - base].astype(F32)
                if done:
                    gw_ref[s, r] = v
                else:
                    acc[s - base] = v.astype(BF16)
                return 0

            lax.fori_loop(lo, hi, add, 0)
            gone.append(axis)
            cur, shift = acc, base
        yield

    def reduces(lo, hi, halves):
        if not fused:
            return []
        if halves:
            return [
                reduce_part(lo, hi, 0, 0, rh, "xyz"),
                reduce_part(lo, hi, 0, rh, rb, "yxz"),
            ]
        return [reduce_part(lo, hi, 9, 0, rb, "yzx")]

    rfu = reduces(9, 9 + nf, False)
    rfd = reduces(9 + nf, nseg + 1, False)
    rc = reduces(3, 8, True)
    rt = reduces(0, 3, True)
    rg = reduces(gseg, gseg + 1, True)
    weight_grads(gb16, [(9 + nf + s, plane(act, s)) for s in range(nf)])
    step(rfd)
    weight_grads(n3, [(9 + s, plane(gbf, s)) for s in range(nf)])
    step(rfu)

    def finish_rows(k, dst):
        def part(i, _):
            r = rows((2 * k + c) * per + i, sub)
            q = rows(i, sub)
            val = h2[r, :] + ys[r, :].astype(F32) + yr[k, q, :].astype(F32)
            keep = live(((2 * k + c) * per + i) * sub, sub)
            dst[q, :] = jnp.where(keep, val, 0.0).astype(BF16)
            return 0
        lax.fori_loop(0, per, part, 0)

    for cp in ycp:
        cp.wait_recv()
    finish_rows(1 - p, osend)
    ocp = push(osend, outs.at[p], x_peer)
    finish_rows(p, outs.at[p])

    def back_three(j, _):
        exchange(2, j).wait_recv()
        exchange(2, j).wait_send()

        def part(i, _):
            r = rows(j * per + i, sub)
            dx, dgain, dbias = norm_grad(h2[r, :], summed(2, r), gains[4:5, :])
            gacc[4:5, :] += dgain
            gacc[5:6, :] += dbias
            g = gb16[r, :].astype(F32) + dx
            gh[r, :] = g
            gb16[r, :] = g.astype(BF16)
            return 0

        return lax.fori_loop(0, per, part, 0)

    lax.fori_loop(0, 4, back_three, 0)


    sel_row = lax.broadcasted_iota(jnp.int32, (8, LANES), 0)
    sel_lane = lax.broadcasted_iota(jnp.int32, (8, LANES), 1)
    selector = (sel_lane // DH == sel_row).astype(F32)

    def attend_back(q_s, k_s, kt, v_s, mix, lse, r, keys, causal):
        def pair(pp, _):
            q = q_s[pp, r, :]
            k = k_s[pp, 0:keys, :]
            v = v_s[pp, 0:keys, :]
            do = dm[pp, r, :]
            prod = do.astype(F32) * mix[pp, r, :].astype(F32)
            delta = lax.dot_general(
                selector, prod, (((1,), (1,)), ((), ())),
                precision=HIGHEST, preferred_element_type=F32,
            )
            parts = []
            dvp = None
            for u in range(2):
                s = masked(nt(only(k, u), q), keys, causal)
                e = jnp.exp(s - lse[2 * pp + u, :, r])
                d = nt(only(v, u), do)
                ds = (e * (d - delta[u : u + 1])).astype(BF16)
                dv_u = nn(e.astype(BF16), only(do, u))
                dk_u = nn(ds, only(q, u))
                dvp = dv_u if dvp is None else dvp + dv_u
                dkp = dk_u if u == 0 else dkp + dk_u
                parts.append(nn(kt[pp, u * DH : (u + 1) * DH, 0:keys], ds) * scale)
            dka[pp, 0:keys, :] += dkp
            dva[pp, 0:keys, :] += dvp
            dq[pp, r, :] = jnp.concatenate(parts, axis=0).T.astype(BF16)
            return 0

        lax.fori_loop(0, 2, pair, 0)

    def transpose_keys(buf):
        def one(j, _):
            r = rows(j)
            for pp in range(2):
                vt[pp, :, r] = buf[pp, r, :].astype(F32).T.astype(BF16)
            return 0
        lax.fori_loop(0, 4, one, 0)

    transpose_keys(cks)
    dka[...] = jnp.zeros_like(dka)
    dva[...] = jnp.zeros_like(dva)

    def cross_back(j, _):
        r = rows(j)
        put_pairs(dm, r, nn(gb16[r, :], weight(7)))
        attend_back(cqs, cks, vt, cvs, cmix, clse, r, rows_all, False)
        send_sum(3, j, nt(pairs(dq, r), weight(6)))
        return 0

    lax.fori_loop(0, 2, cross_back, 0)
    step(rfd)
    lax.fori_loop(2, 4, cross_back, 0)

    def cross_back_keys(j, _):
        r = rows(j)
        for pp in range(2):
            dk[pp, r, :] = dka[pp, r, :].astype(BF16)
            dv[pp, r, :] = dva[pp, r, :].astype(BF16)
        val = nt(pairs(dk, r), weight(4)) + nt(pairs(dv, r), weight(5))
        us[r, :] = val.astype(BF16)
        return 0

    lax.fori_loop(0, 4, cross_back_keys, 0)
    ucp = [
        push(us.at[rows(2 * k + 1 - c)], ur.at[k], core_peer) for k in range(2)
    ]
    weight_grads(gb16, [(7, whole(cmix))])
    weight_grads(n2, [(6, whole(dq))])
    weight_grads(ms, [(4, whole(dk)), (5, whole(dv))])

    def memory_rows(k, dst):
        def part(i, _):
            r = rows((2 * k + c) * per + i, sub)
            q = rows(i, sub)
            dst[q, :] = (us[r, :].astype(F32) + ur[k, q, :].astype(F32)).astype(BF16)
            return 0
        lax.fori_loop(0, per, part, 0)

    for cp in ucp:
        cp.wait_recv()
    memory_rows(1 - p, gmsend)
    mcp = push(gmsend, gms.at[p], x_peer)
    memory_rows(p, gms.at[p])

    def back_two(j, _):
        exchange(3, j).wait_recv()
        exchange(3, j).wait_send()

        def part(i, _):
            r = rows(j * per + i, sub)
            dx, dgain, dbias = norm_grad(h1[r, :], summed(3, r), gains[2:3, :])
            gacc[2:3, :] += dgain
            gacc[3:4, :] += dbias
            g = gh[r, :] + dx
            gh[r, :] = g
            gb16[r, :] = g.astype(BF16)
            return 0

        return lax.fori_loop(0, per, part, 0)

    lax.fori_loop(0, 4, back_two, 0)
    weight_grads(gb16, [(3, whole(smix))])
    step(rfu)
    step(rc)

    transpose_keys(ks)
    dka[...] = jnp.zeros_like(dka)
    dva[...] = jnp.zeros_like(dva)
    for j in reversed(range(4)):
        r = rows(j)
        put_pairs(dm, r, nn(gb16[r, :], weight(3)))
        attend_back(qs, ks, vt, vs, smix, slse, r, own * (j + 1), True)
        for pp in range(2):
            dk[pp, r, :] = dka[pp, r, :].astype(BF16)
            dv[pp, r, :] = dva[pp, r, :].astype(BF16)
        val = nt(pairs(dq, r), weight(0)) + nt(pairs(dk, r), weight(1))
        send_sum(4, j, val + nt(pairs(dv, r), weight(2)))
        if j == 3:
            step(rfd)
        if j == 2:
            step(rfu)
            step(rc)
        if j == 1:
            step(rfd)

    weight_grads(n1, [(0, whole(dq)), (1, whole(dk)), (2, whole(dv))])
    step(rt)
    step(rc)

    def back_one(k, j, dst):
        exchange(4, j).wait_recv()

        def part(i, _):
            r = rows(j * per + i, sub)
            q = rows(i, sub)
            dx, dgain, dbias = norm_grad(xs[r, :].astype(F32), summed(4, r), gains[0:1, :])
            gacc[0:1, :] += dgain
            gacc[1:2, :] += dbias
            if dst is not None:
                dst[q, :] = (gh[r, :] + dx).astype(BF16)
            return 0

        lax.fori_loop(0, per, part, 0)

    back_one(0, tx, gisend)
    icp = push(gisend, gis.at[p], x_peer)
    back_one(0, t, gis.at[p])
    back_one(0, 2 * p + 1 - c, None)
    back_one(0, 2 * (1 - p) + 1 - c, None)
    for j in range(4):
        exchange(4, j).wait_send()

    spread_rows = jnp.concatenate(
        [gacc[...], jnp.zeros((LANES - 8, wide), F32)], axis=0
    )
    columns = spread_rows.T.astype(BF16)
    gs[gseg] = jnp.concatenate([columns, columns], axis=1).reshape(nz, ny, rb, 2 * LANES)

    step(rg)
    step(rt)
    step(rfu)
    step(rg)
    step(rc)
    step(rt)
    step(rg)
    step(rt)
    step(rg)
    last = [] if fused else [local(gs, gw_ref)]

    ocp.wait_recv()
    mcp.wait_recv()
    icp.wait_recv()
    finals = [local(outs, out_ref), local(gms, gm_ref), local(gis, gi_ref)]
    for cp in finals + last:
        cp.wait()
    for cp in sent:
        cp.wait_send()


def unpack_kernel(nf, o_ref, gi_ref, gm_ref, gw_ref, *outs):
    outs[0][...] = o_ref[...]
    outs[1][...] = gi_ref[...].astype(F32)
    outs[2][...] = gm_ref[...].astype(F32)
    outs[3][...] = gw_ref[0:3]
    outs[4][...] = gw_ref[3]
    outs[5][...] = gw_ref[6]
    outs[6][...] = gw_ref[4:6]
    outs[7][...] = gw_ref[7]
    for i in range(nf):
        outs[8][:, i * LANES : (i + 1) * LANES] = gw_ref[9 + i]
        outs[9][:, i * LANES : (i + 1) * LANES] = gw_ref[9 + nf + i]
    vectors = gw_ref[8].T
    for i in range(6):
        outs[10 + i][...] = vectors[i : i + 1]


def body(ndp, inputs, memory, tgt_len, src_len, cotangent, w_qkv, w_out, cross_query, cross_kv,
         cross_out, ffn_up, ffn_down, *gain_list):
    own, wide = inputs.shape[1], inputs.shape[2]
    rb = w_qkv.shape[1]
    nf = ffn_up.shape[1] // LANES
    nseg = 8 + 2 * nf
    rows_all = 4 * own
    fused = rb % 32 == 0 and ndp % 2 == 0
    if fused:
        ny, nz, block = 2, ndp // 2, rb
    else:
        ny, nz, block = 1, 1, wide
    cfg = (fused, nz, ny, block, own, wide, nf)

    any_spec = pl.BlockSpec(memory_space=pl.ANY)
    smem = pl.BlockSpec(memory_space=pltpu.SMEM)
    vmem = pl.BlockSpec(memory_space=pltpu.VMEM)
    operands = [inputs, memory, cotangent, tgt_len, src_len]
    specs = [any_spec] * 3 + [smem] * 2
    if fused:
        weights = [w_qkv, w_out.T, cross_query, cross_kv, cross_out.T, ffn_up, ffn_down.T]
        weights += [g[None, :] for g in gain_list]
        operands += weights
        specs += [vmem] * len(weights)
    else:
        pieces = [w_qkv, w_out.T[None], cross_kv, cross_query[None], cross_out.T[None]]
        pieces += [ffn_up.reshape(rb, nf, LANES).swapaxes(0, 1)]
        pieces += [ffn_down.reshape(nf, LANES, rb).swapaxes(1, 2)]
        packed = lax.all_gather(jnp.concatenate(pieces, axis=0), "dp", axis=1, tiled=True)
        index = lax.axis_index("tensor")
        flipped = lax.ppermute(packed, "tensor", [(i, (i + 2) % 4) for i in range(4)])
        low = jnp.where(index < 2, packed, flipped)
        high = jnp.where(index < 2, flipped, packed)
        full = jnp.concatenate([low, high], axis=2)[:, None, None]
        gathered = lax.all_gather(jnp.stack(gain_list), "dp", axis=1, tiled=True)
        operands += [full, jnp.pad(gathered.astype(F32), ((0, 10), (0, 0)))]
        specs += [any_spec, vmem]

    bf = lambda *shape: pltpu.VMEM(shape, BF16)
    fl = lambda *shape: pltpu.VMEM(shape, F32)
    seq = (rows_all, wide)
    heads = (2, rows_all, LANES)
    scratch = [
        bf(*seq), bf(*seq), bf(*seq), bf(nseg, nz, ny, block, 2 * LANES), fl(16, wide),
        bf(*seq), bf(*seq), bf(*seq), fl(*seq), fl(*seq), fl(*seq), bf(*seq),
        bf(*heads), bf(*heads), bf(*heads), bf(*heads), bf(*heads), bf(*heads),
        bf(2, LANES, rows_all), bf(*heads), bf(*heads), fl(4, 1, rows_all), fl(4, 1, rows_all),
        bf(nf, rows_all, 2 * LANES), bf(nf, rows_all, 2 * LANES),
        bf(*heads), bf(*heads), fl(*heads), fl(*heads), bf(*heads), bf(*heads),
        bf(2, *seq), bf(2, *seq), bf(*seq), bf(2, own, wide), bf(*seq), bf(2, own, wide),
        bf(2, own, wide), bf(own, wide), bf(2, own, wide), bf(own, wide),
        bf(2, own, wide), bf(own, wide),
        bf(nseg + 1, nz, ny, block, 2 * LANES), fl(rows_all, LANES), fl(8, wide),
    ]
    if fused:
        small = block // 2
        scratch += [bf(nz, 16, wide), bf(2, 16, wide)]
        for order, _count in SUMS:
            segs, size = (nseg - 8, block) if order == "yzx" else (9, small)
            scratch += [bf(*shape) for shape in sum_shapes(order, segs, nz, ny, size)]
    dma = pltpu.SemaphoreType.DMA
    scratch += [dma((160,)), dma((160,)), dma((20,)), dma((20,)), dma((12,))]

    if fused:
        grads_shape = jax.ShapeDtypeStruct((nseg + 1, block, LANES), F32)
        grads_spec = vmem
    else:
        grads_shape = jax.ShapeDtypeStruct((nseg + 1, nz, ny, block, 2 * LANES), BF16)
        grads_spec = any_spec
    act_shape = jax.ShapeDtypeStruct(inputs.shape, BF16)
    output, grad_in, grad_mem, grads = pl.pallas_call(
        functools.partial(layer_kernel, cfg),
        out_shape=(act_shape, act_shape, act_shape, grads_shape),
        in_specs=specs,
        out_specs=(any_spec, any_spec, any_spec, grads_spec),
        scratch_shapes=scratch,
        compiler_params=pltpu.CompilerParams(
            collective_id=0, has_side_effects=True, vmem_limit_bytes=62 << 20
        ),
        name="layer",
    )(*operands)

    if not fused:
        mine = grads[:, 0, 0].astype(F32)
        index = lax.axis_index("tensor")
        low, high = mine[:, :, :LANES], mine[:, :, LANES:]
        keep = jnp.where(index < 2, low, high)
        give = jnp.where(index < 2, high, low)
        keep = keep + lax.ppermute(give, "tensor", [(i, (i + 2) % 4) for i in range(4)])
        grads = lax.psum_scatter(keep, "dp", scatter_dimension=1, tiled=True)

    shapes = [
        (inputs.shape, BF16), (inputs.shape, F32), (memory.shape, F32),
        (w_qkv.shape, F32), (w_out.shape[::-1], F32), (cross_query.shape, F32),
        (cross_kv.shape, F32), (cross_out.shape[::-1], F32), (ffn_up.shape, F32),
        (ffn_down.shape[::-1], F32),
    ] + [((1, rb), F32)] * 6
    got = pl.pallas_call(
        functools.partial(unpack_kernel, nf),
        out_shape=[jax.ShapeDtypeStruct(*s) for s in shapes],
        in_specs=[vmem] * 4,
        out_specs=[vmem] * len(shapes),
        name="unpack",
    )(output, grad_in, grad_mem, grads)
    return (
        *got[:4], got[4].T, got[5], got[6], got[7].T, got[8], got[9].T,
        *[g[0] for g in got[10:]],
    )


def solution(mesh):
    return jax.shard_map(
        functools.partial(body, mesh.shape["dp"]),
        mesh=mesh,
        in_specs=(
            P("dp", "tensor", None),
            P("dp", "tensor", None),
            P("dp"),
            P("dp"),
            P("dp", "tensor", None),
            P(None, "dp", "tensor"),
            P("tensor", "dp"),
            P("dp", "tensor"),
            P(None, "dp", "tensor"),
            P("tensor", "dp"),
            P("dp", "tensor"),
            P("tensor", "dp"),
            P("dp"),
            P("dp"),
            P("dp"),
            P("dp"),
            P("dp"),
            P("dp"),
        ),
        out_specs=(
            P("dp", "tensor", None),
            P("dp", "tensor", None),
            P("dp", "tensor", None),
            P(None, "dp", "tensor"),
            P("tensor", "dp"),
            P("dp", "tensor"),
            P(None, "dp", "tensor"),
            P("tensor", "dp"),
            P("dp", "tensor"),
            P("tensor", "dp"),
            P("dp"),
            P("dp"),
            P("dp"),
            P("dp"),
            P("dp"),
            P("dp"),
        ),
        check_vma=False,
    )
```

```python
import functools

import jax
import jax.numpy as jnp
from jax import lax
from jax.experimental import pallas as pl
from jax.experimental.pallas import tpu as pltpu
from jax.sharding import PartitionSpec as P

DH = 64
LANES = 128
EPSILON = 1e-05
MASKED = -1e30
F32 = jnp.float32
BF16 = jnp.bfloat16
MESH = pl.DeviceIdType.MESH
HIGHEST = lax.Precision.HIGHEST


def nn(a, b):
    return lax.dot_general(a, b, (((1,), (0,)), ((), ())), preferred_element_type=F32)


def nt(a, b):
    return lax.dot_general(a, b, (((1,), (1,)), ((), ())), preferred_element_type=F32)


def normalize(values):
    center = values - jnp.mean(values, axis=-1, keepdims=True)
    spread = jnp.mean(center * center, axis=-1, keepdims=True)
    inv = lax.rsqrt(spread + EPSILON)
    return center * inv, inv


def norm_grad(values, grad, gain):
    xhat, inv = normalize(values)
    e = grad * gain
    back = inv * (
        e
        - jnp.mean(e, axis=-1, keepdims=True)
        - xhat * jnp.mean(e * xhat, axis=-1, keepdims=True)
    )
    return (
        back,
        jnp.sum(grad * xhat, axis=0, keepdims=True),
        jnp.sum(grad, axis=0, keepdims=True),
    )


def gelu_both(v):
    c = 0.7978845608028654
    v2 = v * v
    t = jnp.tanh(v * (c + (c * 0.044715) * v2))
    half = 0.5 * (1.0 + t)
    slope = half + (0.5 * v) * (1.0 - t * t) * (c + (3.0 * c * 0.044715) * v2)
    return v * half, slope


ORDERS = {
    "A0": ("xzy",),
    "A1": ("yzx",),
    "A2": ("zyx",),
    "W": ("zxy", "zyx"),
    "K": ("zxy", "zyx"),
    "Q0": ("zxy", "zyx"),
    "Q1": ("zxy", "zyx"),
    "U0": ("yxz",),
    "U1": ("zxy",),
    "D0": ("zxy",),
    "D1": ("zyx",),
    "rD0": ("zxy",),
    "rD1": ("zxy",),
    "rU0": ("xzy",),
    "rU1": ("yxz",),
    "rco": ("yzx",),
    "rcq": ("xzy",),
    "rck": ("zxy",),
    "rwo": ("zxy",),
    "rT": ("xyz", "yzx"),
    "rG": ("yzx",),
}

PLAN = {
    "p0": ("A2", "x", "W", "A1", "gz", "A1", "A2", "A0", "W", "gz", "x", "A0", "A2", "A1", "gz"),
    "p1": ("K", "m", "U0", "A2", "A0", "Q0", "A1", "Q1", "U1", "K", "W", "D0", "A0"),
    "p2": ("Q0", "m", "Q1", "U0", "D1"),
    "p3": ("K",),
    "p4": ("W",),
    "p5": (),
    "p6": ("Q0", "Q1", "U0"),
    "p7": ("U1",),
    "p8": ("K", "D1"),
    "p9": ("Q0", "D0"),
    "p10": ("Q1",),
    "p11": ("U1", "c"),
    "p12": (),
    "p13": (),
    "p14": ("D0", "D1"),
    "p15": ("U0",),
    "p16": ("U1",),
    "p17": ("c",),
    "p18": (),
    "p19": ("rD1", "D0", "D1"),
    "p20": (),
    "p21": ("rU0", "rU1"),
    "p22": ("rD0",),
    "p23": ("out", "rco"),
    "p24": (),
    "p25": ("rD1", "rU1"),
    "p26": ("rD1", "out", "rU0"),
    "p27": ("rD1", "rD0", "rU1"),
    "p28": ("rcq", "rck"),
    "p29": ("rD0", "gm"),
    "p30": ("rU0",),
    "p31": ("rU0", "rD0", "rU1"),
    "p32": ("gm", "rwo"),
    "p33": (),
    "p34": (),
    "p35": ("rT", "rcq"),
    "p36": ("rco",),
    "p37": ("rG", "rwo", "gi", "rck", "rT", "rcq", "rwo", "rco", "rG", "rcq", "rwo", "gi", "rT", "rck", "rco", "rG", "rck", "rG", "rT"),
}


def gather_segments(nf):
    mid = 8 + nf // 2
    end = 8 + nf
    last = end + nf // 2
    return {
        "A0": (0, 1), "A1": (1, 2), "A2": (2, 3), "W": (3, 4), "K": (4, 6), "Q0": (6, 7),
        "Q1": (7, 8), "U0": (8, mid), "U1": (mid, end), "D0": (end, last),
        "D1": (last, end + nf),
    }


def sum_segments(nf):
    mid = 9 + nf // 2
    end = 9 + nf
    last = end + nf // 2
    return {
        "rT": (0, 3), "rwo": (3, 4), "rck": (4, 6), "rcq": (6, 7), "rco": (7, 8), "rG": (8, 9),
        "rU0": (9, mid), "rU1": (mid, end), "rD0": (end, last), "rD1": (last, end + nf),
    }


def sum_shapes(order, segs, nz, ny, rows):
    shapes, left = [], {"x": 2 * LANES, "y": (ny,), "z": (nz,)}
    for i, axis in enumerate(order):
        left[axis] = LANES if axis == "x" else ()
        shape = (segs, *left["z"], *left["y"], rows, left["x"])
        shapes.append((nz - 1, *shape) if axis == "z" else shape)
        if i < 2:
            shapes.append(shape)
    return shapes


def layer_kernel(cfg, *refs):
    fused, nz, ny, rb, own, wide, nf = cfg
    rows_all = 4 * own
    nseg = 8 + 2 * nf
    gseg = 8
    refs = list(refs)

    def take(count):
        got, refs[:count] = refs[:count], []
        return got

    x_ref, m_ref, c_ref, tl_ref, sl_ref = take(5)
    if fused:
        wqkv_ref, wo_ref, cq_ref, ckv_ref, co_ref, up_ref, dn_ref = take(7)
        gain_refs = take(6)
    else:
        wfull_ref, gfull_ref = take(2)
    out_ref, gi_ref, gm_ref, gw_ref = take(4)
    (xs, ms, cs, wg, gains, n1, n2, n3, h1, h2, gh, gb16, qs, ks, vs, cqs, cks, cvs,
     vt, smix, cmix, slse, clse, act, gbf, dm, dq, dka, dva, dk, dv, ps, pr, ys, yr,
     us, ur, outs, osend, gis, gisend, gms, gmsend, gs, bias, gacc, score) = take(47)
    if fused:
        gz, gy = take(2)
        sums = {name: [take(5) for _ in ORDERS[name]] for name in sum_segments(nf)}
    ssem, rsem, xss, xrs, lsem = take(5)

    p = lax.axis_index("tensor") // 2
    c = lax.axis_index("tensor") % 2
    t = 2 * p + c
    tx = 2 * (1 - p) + c
    dp_at = lax.axis_index("dp")
    core_peer = {"dp": dp_at, "tensor": 2 * p + 1 - c}
    x_peer = {"dp": dp_at, "tensor": tx}
    z = dp_at // ny
    y = dp_at % ny
    y_peer = {"dp": z * ny + (1 - y), "tensor": t}

    def z_peer(k):
        return {"dp": ((z + k) % nz) * ny + y, "tensor": t}

    counter = [0]
    sent = []

    def push(src, dst, peer):
        i = counter[0]
        counter[0] += 1
        cp = pltpu.make_async_remote_copy(
            src, dst, ssem.at[i], rsem.at[i], device_id=peer, device_id_type=MESH
        )
        cp.start()
        sent.append(cp)
        return cp

    lcount = [0]
    local_open = []

    def local(src, dst):
        cp = pltpu.make_async_copy(src, dst, lsem.at[lcount[0]])
        lcount[0] += 1
        cp.start()
        return cp

    def rows(j, size=own):
        return pl.ds(pl.multiple_of(j * size, size), size)

    peers = [core_peer, x_peer]
    if fused:
        peers.append(y_peer)
        peers += [z_peer(k) for k in range(1, nz)]
    barrier = pltpu.get_barrier_semaphore()
    for peer in peers:
        pl.semaphore_signal(barrier, inc=1, device_id=peer, device_id_type=MESH)

    half = pl.ds(pl.multiple_of(p * LANES, LANES), LANES)
    other_half = pl.ds(pl.multiple_of((1 - p) * LANES, LANES), LANES)

    if fused:
        own_part = [wqkv_ref[...], wo_ref[...][None], ckv_ref[...], cq_ref[...][None]]
        own_part.append(co_ref[...][None])
        at = 0
        for piece in own_part:
            wg[at : at + piece.shape[0], z, y, :, half] = piece
            at += piece.shape[0]
        for i in range(nf):
            wg[8 + i, z, y, :, half] = up_ref[:, i * LANES : (i + 1) * LANES]
            wg[8 + nf + i, z, y, :, half] = dn_ref[:, i * LANES : (i + 1) * LANES]
        place = (
            lax.broadcasted_iota(jnp.int32, (rb, wide), 0) + dp_at * rb
            == lax.broadcasted_iota(jnp.int32, (rb, wide), 1)
        ).astype(BF16)
        gz[0] = jnp.zeros((16, wide), BF16)
        for i in range(6):
            gz[0, i : i + 1, :] = nn(gain_refs[i][...], place).astype(BF16)
    pl.semaphore_wait(barrier, len(peers))

    relays = {}

    def carry(name, src, buf):
        over = push(src.at[1 - p], buf.at[rows(t)], x_peer)
        keep = local(src.at[p], buf.at[rows(t)])
        near = push(src.at[p], buf.at[rows(t)], core_peer)
        yield
        over.wait_recv()
        relays[name] = push(buf.at[rows(tx)], buf.at[rows(tx)], core_peer)
        keep.wait()
        near.wait_recv()
        yield

    def back_over(src, buf):
        cp = push(src, buf.at[p], x_peer)
        yield
        cp.wait_recv()
        yield

    tasks = {
        "x": [carry("x", x_ref, xs)],
        "m": [carry("m", m_ref, ms)],
        "c": [carry("c", c_ref, cs)],
        "out": [back_over(osend, outs)],
        "gm": [back_over(gmsend, gms)],
        "gi": [back_over(gisend, gis)],
        "gz": [],
    }

    def at(name):
        for task in PLAN[name]:
            for part in tasks[task]:
                next(part)

    def gather(lo, hi, first, last, order):
        r = slice(first, last)
        zi, yi, lanes = z, y, half
        hops = []
        for axis in order:
            for cp in hops:
                cp.wait_recv()
            part = wg.at[lo:hi, zi, yi, r, lanes]
            if axis == "x":
                hops = [push(part, part, x_peer)]
                lanes = pl.ds(0, 2 * LANES)
            elif axis == "y":
                hops = [push(part, part, y_peer)]
                yi = slice(None)
            else:
                hops = [push(part, part, z_peer(k)) for k in range(1, nz)]
                zi = slice(None)
            yield
        for cp in hops:
            cp.wait_recv()
        yield

    def gain_rows():
        cps = [push(gz.at[0], gz.at[k], z_peer(k)) for k in range(1, nz)]
        yield
        for cp in cps:
            cp.wait_recv()
        total = gz[0].astype(F32)
        for k in range(1, nz):
            total = total + gz[k].astype(F32)
        gy[0] = total.astype(BF16)
        cp = push(gy.at[0], gy.at[1], y_peer)
        yield
        cp.wait_recv()
        gains[...] = total + gy[1].astype(F32)
        yield

    for name, (lo, hi) in gather_segments(nf).items():
        size = rb // len(ORDERS[name])
        tasks[name] = [
            gather(lo, hi, i * size, (i + 1) * size, order)
            for i, order in enumerate(ORDERS[name])
            if fused
        ]
    if fused:
        tasks["gz"] = [gain_rows()]

    def weight(s):
        return wg[s].reshape(nz * ny * rb, 2 * LANES)

    if not fused:
        wcp = local(wfull_ref, wg)
        gains[...] = gfull_ref[...]
    at("p0")
    relays["x"].wait_recv()
    if not fused:
        wcp.wait()

    sub = min(64, own)
    per = own // sub
    gacc[...] = jnp.zeros_like(gacc)

    def norm_rows(i, _):
        r = rows(i, sub)
        xhat, _unused = normalize(xs[r, :].astype(F32))
        n1[r, :] = (xhat * gains[0:1, :] + gains[1:2, :]).astype(BF16)
        return 0

    lax.fori_loop(0, 4 * per, norm_rows, 0)
    at("p1")

    def put_pairs(buf, r, value):
        v = value.astype(BF16)
        buf[0, r, :] = v[:, :LANES]
        buf[1, r, :] = v[:, LANES:]

    def pairs(buf, r):
        return jnp.concatenate([buf[0, r, :], buf[1, r, :]], axis=1)

    scale = DH ** (-0.5)

    def put_transposed(buf, r, value):
        vt_ = value.T.astype(BF16)
        buf[0, :, r] = vt_[:LANES]
        buf[1, :, r] = vt_[LANES:]

    def project(j, _):
        r = rows(j)
        rowsv = n1[r, :]
        put_pairs(qs, r, nn(rowsv, weight(0)).astype(BF16) * jnp.asarray(scale, BF16))
        put_pairs(ks, r, nn(rowsv, weight(1)))
        val = nn(rowsv, weight(2))
        put_pairs(vs, r, val)
        put_transposed(vt, r, val.astype(BF16).astype(F32))
        return 0

    lax.fori_loop(0, 4, project, 0)
    at("p2")


    lane_at = lax.broadcasted_iota(jnp.int32, (1, LANES), 1)
    head_lanes = [((lane_at // DH) == u).astype(F32).astype(BF16) for u in range(2)]

    def only(value, u):
        return value * head_lanes[u]

    wide_rows = 2 * own

    def qrows(jj):
        return pl.ds(pl.multiple_of(jj * wide_rows, wide_rows), wide_rows)

    def hide(scores, first, diagonal, causal):
        if causal and not diagonal:
            return scores
        if causal:
            key_at = lax.broadcasted_iota(jnp.int32, scores.shape, 0)
            query_at = lax.broadcasted_iota(jnp.int32, scores.shape, 1)
            return jnp.where(key_at <= query_at, scores, MASKED)
        b = bias[first : first + scores.shape[0], :]
        return scores + jnp.concatenate([b] * (wide_rows // LANES), axis=1)

    def attend(pp, q_s, k_s, v_t, mix, lse, r, keys, causal):
        parts_k = [slice(i * wide_rows, (i + 1) * wide_rows) for i in range(keys // wide_rows)]

        q = q_s[pp, r, :]
        tops = [None, None]
        for i, kk in enumerate(parts_k):
            for u in range(2):
                s = nt(only(k_s[pp, kk, :], u), q)
                s = hide(s, kk.start, i == len(parts_k) - 1, causal)
                top = jnp.max(s, axis=0, keepdims=True)
                tops[u] = top if i == 0 else jnp.maximum(tops[u], top)
                score[u, kk, :] = s
        totals, mixed = [None, None], [None, None]
        for i, kk in enumerate(parts_k):
            for u in range(2):
                e = jnp.exp(score[u, kk, :] - tops[u])
                total = jnp.sum(e, axis=0, keepdims=True)
                o = nn(v_t[pp, u * DH : (u + 1) * DH, kk], e.astype(BF16))
                totals[u] = total if i == 0 else totals[u] + total
                mixed[u] = o if i == 0 else mixed[u] + o
        for u in range(2):
            lse[2 * pp + u, :, r] = tops[u] + jnp.log(totals[u])
            mixed[u] = mixed[u] * (1.0 / totals[u])
        mix[pp, r, :] = jnp.concatenate(mixed, axis=0).T.astype(BF16)

    def exchange(point, j):
        b = point % 2
        i = point * 4 + j
        return pltpu.make_async_remote_copy(
            ps.at[b, rows(j)], pr.at[b, rows(j)], xss.at[i], xrs.at[i],
            device_id=core_peer, device_id_type=MESH,
        )

    def send_sum(point, j, value):
        ps[point % 2, rows(j), :] = value.astype(BF16)
        exchange(point, j).start()

    def summed(point, r):
        b = point % 2
        return ps[b, r, :].astype(F32) + pr[b, r, :].astype(F32)

    for jj in range(2):
        first = 3 + 3 * jj
        for pp in range(2):
            attend(pp, qs, ks, vt, smix, slse, qrows(jj), wide_rows * (jj + 1), True)
            at(f"p{first + pp}")
        for j in (2 * jj, 2 * jj + 1):
            send_sum(0, j, nt(pairs(smix, rows(j)), weight(3)))
        at(f"p{first + 2}")
    relays["m"].wait_recv()

    key_at = lax.broadcasted_iota(jnp.int32, (rows_all, LANES), 0)
    bias[...] = jnp.where(key_at < sl_ref[p], 0.0, MASKED)

    def project_cross(j, _):
        r = rows(j)
        rowsv = ms[r, :]
        put_pairs(cks, r, nn(rowsv, weight(4)))
        val = nn(rowsv, weight(5))
        put_pairs(cvs, r, val)
        put_transposed(vt, r, val.astype(BF16).astype(F32))
        return 0

    lax.fori_loop(0, 4, project_cross, 0)
    at("p9")

    def second(j, _):
        exchange(0, j).wait_recv()
        exchange(0, j).wait_send()

        def part(i, _):
            r = rows(j * per + i, sub)
            h = xs[r, :].astype(F32) + summed(0, r)
            h1[r, :] = h
            xhat, _unused = normalize(h)
            n2[r, :] = (xhat * gains[2:3, :] + gains[3:4, :]).astype(BF16)
            return 0

        lax.fori_loop(0, per, part, 0)
        r = rows(j)
        put_pairs(cqs, r, nn(n2[r, :], weight(6)).astype(BF16) * jnp.asarray(scale, BF16))
        return 0

    lax.fori_loop(0, 4, second, 0)
    at("p10")

    for jj in range(2):
        first = 11 + 3 * jj
        for pp in range(2):
            attend(pp, cqs, cks, vt, cmix, clse, qrows(jj), rows_all, False)
            at(f"p{first + pp}")
        for j in (2 * jj, 2 * jj + 1):
            send_sum(1, j, nt(pairs(cmix, rows(j)), weight(7)))
        at(f"p{first + 2}")

    limit = tl_ref[p]

    def live(r_first, size):
        at = lax.broadcasted_iota(jnp.int32, (size, wide), 0) + r_first
        return at < limit

    def weight_grads(a_buf, items):
        chunk = ny * rb
        for zi in range(nz):
            at = a_buf[:, zi * chunk : (zi + 1) * chunk].T
            for s, load in items:
                gs[s, zi] = nn(at, load()).astype(BF16).reshape(ny, rb, 2 * LANES)

    every = pl.ds(0, rows_all)

    def whole(buf):
        return lambda: pairs(buf, every)

    def plane(buf, s):
        return lambda: buf[s]

    def reduce_part(lo, hi, first, last, order, bufs):
        r = slice(first, last)
        base = lo
        bufs = list(bufs)
        gone = []

        def at(buf, s, zsel, ysel, lsel):
            index = [s]
            if "z" not in gone:
                index.append(zsel)
            if "y" not in gone:
                index.append(ysel)
            index += [slice(None) if buf is not gs else r, lsel]
            return tuple(index)

        every_one = slice(None)
        cur, shift = gs, 0
        for hop, axis in enumerate(order):
            span = slice(lo - shift, hi - shift)
            land = bufs.pop(0)
            to = slice(lo - base, hi - base)
            lanes = every_one if "x" in gone else slice(0, 2 * LANES)
            pick = {"z": every_one, "y": every_one, "x": lanes}
            here = dict(pick)
            if axis == "x":
                pick["x"], here["x"] = other_half, half
                sends = [(pick, land.at[to], x_peer)]
            elif axis == "y":
                pick["y"], here["y"] = 1 - y, y
                sends = [(pick, land.at[to], y_peer)]
            else:
                here["z"] = z
                sends = [
                    (dict(pick, z=(z + k) % nz), land.at[k - 1, to], z_peer(k))
                    for k in range(1, nz)
                ]
            cps = [
                push(cur.at[at(cur, span, sel["z"], sel["y"], sel["x"])], dst, peer)
                for sel, dst, peer in sends
            ]
            yield
            for cp in cps:
                cp.wait_recv()
            done = hop == 2
            acc = None if done else bufs.pop(0)

            def add(s, _):
                v = cur[at(cur, s - shift, here["z"], here["y"], here["x"])].astype(F32)
                if axis == "z":
                    for k in range(1, nz):
                        v = v + land[k - 1, s - base].astype(F32)
                else:
                    v = v + land[s - base].astype(F32)
                if done:
                    gw_ref[s, r] = v
                else:
                    acc[s - base] = v.astype(BF16)
                return 0

            lax.fori_loop(lo, hi, add, 0)
            gone.append(axis)
            cur, shift = acc, base
        yield

    for name, (lo, hi) in sum_segments(nf).items():
        size = rb // len(ORDERS[name])
        tasks[name] = [
            reduce_part(lo, hi, i * size, (i + 1) * size, order, sums[name][i])
            for i, order in enumerate(ORDERS[name])
            if fused
        ]

    def third(j, _):
        exchange(1, j).wait_recv()
        exchange(1, j).wait_send()

        def part(i, _):
            r = rows(j * per + i, sub)
            h = h1[r, :] + summed(1, r)
            h2[r, :] = h
            xhat, _unused = normalize(h)
            n3[r, :] = (xhat * gains[4:5, :] + gains[5:6, :]).astype(BF16)
            return 0

        lax.fori_loop(0, per, part, 0)
        r = rows(j)
        rowsv = n3[r, :]
        for s in range(nf):
            active, slope = gelu_both(nn(rowsv, weight(8 + s)))
            act[s, r, :] = active.astype(BF16)
            gbf[s, r, :] = slope.astype(BF16)
        return 0

    lax.fori_loop(0, 2, third, 0)
    at("p17")
    lax.fori_loop(2, 4, third, 0)
    at("p18")
    relays["c"].wait_recv()

    def live_rows(i, _):
        r = rows(i, sub)
        cot = cs[r, :]
        gb16[r, :] = jnp.where(live(i * sub, sub), cot, jnp.zeros_like(cot))
        return 0

    lax.fori_loop(0, 4 * per, live_rows, 0)
    weight_grads(gb16, [(9 + nf + s, plane(act, s)) for s in range(nf)])
    at("p19")

    def third_back(j, _):
        r = rows(j)
        cot = gb16[r, :]
        for s in range(nf):
            slope = gbf[s, r, :].astype(F32)
            gbf[s, r, :] = (nn(cot, weight(8 + nf + s)) * slope).astype(BF16)
        back = nt(gbf[0, r, :], weight(8))
        for s in range(1, nf):
            back = back + nt(gbf[s, r, :], weight(8 + s))
        send_sum(2, j, back)
        val = nt(act[0, r, :], weight(8 + nf))
        for s in range(1, nf):
            val = val + nt(act[s, r, :], weight(8 + nf + s))
        ys[r, :] = val.astype(BF16)
        return 0

    lax.fori_loop(0, 2, third_back, 0)
    at("p20")
    lax.fori_loop(2, 4, third_back, 0)

    ycp = [
        push(ys.at[rows(2 * k + 1 - c)], yr.at[k], core_peer) for k in range(2)
    ]

    weight_grads(n3, [(9 + s, plane(gbf, s)) for s in range(nf)])
    at("p21")

    def finish_rows(k, dst):
        def part(i, _):
            r = rows((2 * k + c) * per + i, sub)
            q = rows(i, sub)
            val = h2[r, :] + ys[r, :].astype(F32) + yr[k, q, :].astype(F32)
            keep = live(((2 * k + c) * per + i) * sub, sub)
            dst[q, :] = jnp.where(keep, val, 0.0).astype(BF16)
            return 0
        lax.fori_loop(0, per, part, 0)

    for cp in ycp:
        cp.wait_recv()
    finish_rows(1 - p, osend)
    finish_rows(p, outs.at[p])
    at("p22")

    def back_three(j, _):
        exchange(2, j).wait_recv()
        exchange(2, j).wait_send()

        def part(i, _):
            r = rows(j * per + i, sub)
            dx, dgain, dbias = norm_grad(h2[r, :], summed(2, r), gains[4:5, :])
            gacc[4:5, :] += dgain
            gacc[5:6, :] += dbias
            g = gb16[r, :].astype(F32) + dx
            gh[r, :] = g
            gb16[r, :] = g.astype(BF16)
            return 0

        return lax.fori_loop(0, per, part, 0)

    lax.fori_loop(0, 4, back_three, 0)
    weight_grads(gb16, [(7, whole(cmix))])
    at("p23")


    sel_row = lax.broadcasted_iota(jnp.int32, (8, LANES), 0)
    sel_lane = lax.broadcasted_iota(jnp.int32, (8, LANES), 1)
    selector = (sel_lane // DH == sel_row).astype(F32)

    def attend_back(pp, q_s, k_s, kt, v_s, mix, lse, r, keys, causal):
        parts_k = [slice(0, keys)]
        if causal and keys > wide_rows:
            parts_k = [slice(0, keys - wide_rows), slice(keys - wide_rows, keys)]

        q = q_s[pp, r, :]
        do = dm[pp, r, :]
        prod = do.astype(F32) * mix[pp, r, :].astype(F32)
        delta = lax.dot_general(
            selector, prod, (((1,), (1,)), ((), ())),
            precision=HIGHEST, preferred_element_type=F32,
        )
        back = None
        for i, kk in enumerate(parts_k):
            parts = []
            for u in range(2):
                s = nt(only(k_s[pp, kk, :], u), q)
                s = hide(s, kk.start, i == len(parts_k) - 1, causal)
                e = jnp.exp(s - lse[2 * pp + u, :, r])
                d = nt(only(v_s[pp, kk, :], u), do)
                ds = (e * (d - delta[u : u + 1])).astype(BF16)
                dv_u = nn(e.astype(BF16), only(do, u))
                dk_u = nn(ds, only(q, u))
                dvp = dv_u if u == 0 else dvp + dv_u
                dkp = dk_u if u == 0 else dkp + dk_u
                parts.append(nn(kt[pp, u * DH : (u + 1) * DH, kk], ds))
            dka[pp, kk, :] += dkp
            dva[pp, kk, :] += dvp
            parts = jnp.concatenate(parts, axis=0)
            back = parts if i == 0 else back + parts
        dq[pp, r, :] = (back * scale).T.astype(BF16)

    def transpose_keys(buf):
        def one(j, _):
            r = rows(j)
            for pp in range(2):
                vt[pp, :, r] = buf[pp, r, :].astype(F32).T.astype(BF16)
            return 0
        lax.fori_loop(0, 4, one, 0)

    transpose_keys(cks)
    dka[...] = jnp.zeros_like(dka)
    dva[...] = jnp.zeros_like(dva)

    for jj in range(2):
        for j in (2 * jj, 2 * jj + 1):
            put_pairs(dm, rows(j), nn(gb16[rows(j), :], weight(7)))
        for pp in range(2):
            attend_back(pp, cqs, cks, vt, cvs, cmix, clse, qrows(jj), rows_all, False)
            at(f"p{24 + 2 * jj + pp}")
        for j in (2 * jj, 2 * jj + 1):
            send_sum(3, j, nt(pairs(dq, rows(j)), weight(6)))

    def cross_back_keys(j, _):
        r = rows(j)
        for pp in range(2):
            dk[pp, r, :] = dka[pp, r, :].astype(BF16)
            dv[pp, r, :] = dva[pp, r, :].astype(BF16)
        val = nt(pairs(dk, r), weight(4)) + nt(pairs(dv, r), weight(5))
        us[r, :] = val.astype(BF16)
        return 0

    lax.fori_loop(0, 4, cross_back_keys, 0)
    ucp = [
        push(us.at[rows(2 * k + 1 - c)], ur.at[k], core_peer) for k in range(2)
    ]
    weight_grads(n2, [(6, whole(dq))])
    weight_grads(ms, [(4, whole(dk)), (5, whole(dv))])
    at("p28")

    def memory_rows(k, dst):
        def part(i, _):
            r = rows((2 * k + c) * per + i, sub)
            q = rows(i, sub)
            dst[q, :] = (us[r, :].astype(F32) + ur[k, q, :].astype(F32)).astype(BF16)
            return 0
        lax.fori_loop(0, per, part, 0)

    for cp in ucp:
        cp.wait_recv()
    memory_rows(1 - p, gmsend)
    memory_rows(p, gms.at[p])
    at("p29")

    def back_two(j, _):
        exchange(3, j).wait_recv()
        exchange(3, j).wait_send()

        def part(i, _):
            r = rows(j * per + i, sub)
            dx, dgain, dbias = norm_grad(h1[r, :], summed(3, r), gains[2:3, :])
            gacc[2:3, :] += dgain
            gacc[3:4, :] += dbias
            g = gh[r, :] + dx
            gh[r, :] = g
            gb16[r, :] = g.astype(BF16)
            return 0

        return lax.fori_loop(0, per, part, 0)

    lax.fori_loop(0, 4, back_two, 0)
    weight_grads(gb16, [(3, whole(smix))])
    at("p30")

    transpose_keys(ks)
    dka[...] = jnp.zeros_like(dka)
    dva[...] = jnp.zeros_like(dva)
    for jj in (1, 0):
        for j in (2 * jj, 2 * jj + 1):
            put_pairs(dm, rows(j), nn(gb16[rows(j), :], weight(3)))
        for pp in range(2):
            attend_back(pp, qs, ks, vt, vs, smix, slse, qrows(jj), wide_rows * (jj + 1), True)
            at(f"p{31 + 2 * (1 - jj) + pp}")
        for j in (2 * jj, 2 * jj + 1):
            r = rows(j)
            for pp in range(2):
                dk[pp, r, :] = dka[pp, r, :].astype(BF16)
                dv[pp, r, :] = dva[pp, r, :].astype(BF16)
            val = nt(pairs(dq, r), weight(0)) + nt(pairs(dk, r), weight(1))
            send_sum(4, j, val + nt(pairs(dv, r), weight(2)))

    weight_grads(n1, [(0, whole(dq)), (1, whole(dk)), (2, whole(dv))])
    at("p35")

    def back_one(k, j, dst):
        exchange(4, j).wait_recv()

        def part(i, _):
            r = rows(j * per + i, sub)
            q = rows(i, sub)
            dx, dgain, dbias = norm_grad(xs[r, :].astype(F32), summed(4, r), gains[0:1, :])
            gacc[0:1, :] += dgain
            gacc[1:2, :] += dbias
            if dst is not None:
                dst[q, :] = (gh[r, :] + dx).astype(BF16)
            return 0

        lax.fori_loop(0, per, part, 0)

    back_one(0, tx, gisend)
    at("p36")
    back_one(0, t, gis.at[p])
    back_one(0, 2 * p + 1 - c, None)
    back_one(0, 2 * (1 - p) + 1 - c, None)
    for j in range(4):
        exchange(4, j).wait_send()

    spread_rows = jnp.concatenate(
        [gacc[...], jnp.zeros((LANES - 8, wide), F32)], axis=0
    )
    columns = spread_rows.T.astype(BF16)
    gs[gseg] = jnp.concatenate([columns, columns], axis=1).reshape(nz, ny, rb, 2 * LANES)

    at("p37")
    last = [] if fused else [local(gs, gw_ref)]

    finals = [local(outs, out_ref), local(gms, gm_ref), local(gis, gi_ref)]
    for cp in finals + last:
        cp.wait()
    for cp in sent:
        cp.wait_send()


def unpack_kernel(nf, o_ref, gi_ref, gm_ref, gw_ref, *outs):
    outs[0][...] = o_ref[...]
    outs[1][...] = gi_ref[...].astype(F32)
    outs[2][...] = gm_ref[...].astype(F32)
    outs[3][...] = gw_ref[0:3]
    outs[4][...] = gw_ref[3]
    outs[5][...] = gw_ref[6]
    outs[6][...] = gw_ref[4:6]
    outs[7][...] = gw_ref[7]
    for i in range(nf):
        outs[8][:, i * LANES : (i + 1) * LANES] = gw_ref[9 + i]
        outs[9][:, i * LANES : (i + 1) * LANES] = gw_ref[9 + nf + i]
    vectors = gw_ref[8].T
    for i in range(6):
        outs[10 + i][...] = vectors[i : i + 1]


def body(ndp, inputs, memory, tgt_len, src_len, cotangent, w_qkv, w_out, cross_query, cross_kv,
         cross_out, ffn_up, ffn_down, *gain_list):
    own, wide = inputs.shape[1], inputs.shape[2]
    rb = w_qkv.shape[1]
    nf = ffn_up.shape[1] // LANES
    nseg = 8 + 2 * nf
    rows_all = 4 * own
    fused = rb % 32 == 0 and ndp % 2 == 0
    if fused:
        ny, nz, block = 2, ndp // 2, rb
    else:
        ny, nz, block = 1, 1, wide
    cfg = (fused, nz, ny, block, own, wide, nf)

    any_spec = pl.BlockSpec(memory_space=pl.ANY)
    smem = pl.BlockSpec(memory_space=pltpu.SMEM)
    vmem = pl.BlockSpec(memory_space=pltpu.VMEM)
    operands = [inputs, memory, cotangent, tgt_len, src_len]
    specs = [any_spec] * 3 + [smem] * 2
    if fused:
        weights = [w_qkv, w_out.T, cross_query, cross_kv, cross_out.T, ffn_up, ffn_down.T]
        weights += [g[None, :] for g in gain_list]
        operands += weights
        specs += [vmem] * len(weights)
    else:
        pieces = [w_qkv, w_out.T[None], cross_kv, cross_query[None], cross_out.T[None]]
        pieces += [ffn_up.reshape(rb, nf, LANES).swapaxes(0, 1)]
        pieces += [ffn_down.reshape(nf, LANES, rb).swapaxes(1, 2)]
        packed = lax.all_gather(jnp.concatenate(pieces, axis=0), "dp", axis=1, tiled=True)
        index = lax.axis_index("tensor")
        flipped = lax.ppermute(packed, "tensor", [(i, (i + 2) % 4) for i in range(4)])
        low = jnp.where(index < 2, packed, flipped)
        high = jnp.where(index < 2, flipped, packed)
        full = jnp.concatenate([low, high], axis=2)[:, None, None]
        gathered = lax.all_gather(jnp.stack(gain_list), "dp", axis=1, tiled=True)
        operands += [full, jnp.pad(gathered.astype(F32), ((0, 10), (0, 0)))]
        specs += [any_spec, vmem]

    bf = lambda *shape: pltpu.VMEM(shape, BF16)
    fl = lambda *shape: pltpu.VMEM(shape, F32)
    seq = (rows_all, wide)
    heads = (2, rows_all, LANES)
    scratch = [
        bf(*seq), bf(*seq), bf(*seq), bf(nseg, nz, ny, block, 2 * LANES), fl(16, wide),
        bf(*seq), bf(*seq), bf(*seq), fl(*seq), fl(*seq), fl(*seq), bf(*seq),
        bf(*heads), bf(*heads), bf(*heads), bf(*heads), bf(*heads), bf(*heads),
        bf(2, LANES, rows_all), bf(*heads), bf(*heads), fl(4, 1, rows_all), fl(4, 1, rows_all),
        bf(nf, rows_all, 2 * LANES), bf(nf, rows_all, 2 * LANES),
        bf(*heads), bf(*heads), fl(*heads), fl(*heads), bf(*heads), bf(*heads),
        bf(2, *seq), bf(2, *seq), bf(*seq), bf(2, own, wide), bf(*seq), bf(2, own, wide),
        bf(2, own, wide), bf(own, wide), bf(2, own, wide), bf(own, wide),
        bf(2, own, wide), bf(own, wide),
        bf(nseg + 1, nz, ny, block, 2 * LANES), fl(rows_all, LANES), fl(8, wide),
        fl(2, rows_all, 2 * own),
    ]
    if fused:
        scratch += [bf(nz, 16, wide), bf(2, 16, wide)]
        for name, (lo, hi) in sum_segments(nf).items():
            for order in ORDERS[name]:
                shapes = sum_shapes(order, hi - lo, nz, ny, block // len(ORDERS[name]))
                scratch += [bf(*shape) for shape in shapes]
    dma = pltpu.SemaphoreType.DMA
    scratch += [dma((250,)), dma((250,)), dma((20,)), dma((20,)), dma((12,))]

    if fused:
        grads_shape = jax.ShapeDtypeStruct((nseg + 1, block, LANES), F32)
        grads_spec = vmem
    else:
        grads_shape = jax.ShapeDtypeStruct((nseg + 1, nz, ny, block, 2 * LANES), BF16)
        grads_spec = any_spec
    act_shape = jax.ShapeDtypeStruct(inputs.shape, BF16)
    output, grad_in, grad_mem, grads = pl.pallas_call(
        functools.partial(layer_kernel, cfg),
        out_shape=(act_shape, act_shape, act_shape, grads_shape),
        in_specs=specs,
        out_specs=(any_spec, any_spec, any_spec, grads_spec),
        scratch_shapes=scratch,
        compiler_params=pltpu.CompilerParams(
            collective_id=0, has_side_effects=True, vmem_limit_bytes=62 << 20
        ),
        name="layer",
    )(*operands)

    if not fused:
        mine = grads[:, 0, 0].astype(F32)
        index = lax.axis_index("tensor")
        low, high = mine[:, :, :LANES], mine[:, :, LANES:]
        keep = jnp.where(index < 2, low, high)
        give = jnp.where(index < 2, high, low)
        keep = keep + lax.ppermute(give, "tensor", [(i, (i + 2) % 4) for i in range(4)])
        grads = lax.psum_scatter(keep, "dp", scatter_dimension=1, tiled=True)

    shapes = [
        (inputs.shape, BF16), (inputs.shape, F32), (memory.shape, F32),
        (w_qkv.shape, F32), (w_out.shape[::-1], F32), (cross_query.shape, F32),
        (cross_kv.shape, F32), (cross_out.shape[::-1], F32), (ffn_up.shape, F32),
        (ffn_down.shape[::-1], F32),
    ] + [((1, rb), F32)] * 6
    got = pl.pallas_call(
        functools.partial(unpack_kernel, nf),
        out_shape=[jax.ShapeDtypeStruct(*s) for s in shapes],
        in_specs=[vmem] * 4,
        out_specs=[vmem] * len(shapes),
        name="unpack",
    )(output, grad_in, grad_mem, grads)
    return (
        *got[:4], got[4].T, got[5], got[6], got[7].T, got[8], got[9].T,
        *[g[0] for g in got[10:]],
    )


def solution(mesh):
    return jax.shard_map(
        functools.partial(body, mesh.shape["dp"]),
        mesh=mesh,
        in_specs=(
            P("dp", "tensor", None),
            P("dp", "tensor", None),
            P("dp"),
            P("dp"),
            P("dp", "tensor", None),
            P(None, "dp", "tensor"),
            P("tensor", "dp"),
            P("dp", "tensor"),
            P(None, "dp", "tensor"),
            P("tensor", "dp"),
            P("dp", "tensor"),
            P("tensor", "dp"),
            P("dp"),
            P("dp"),
            P("dp"),
            P("dp"),
            P("dp"),
            P("dp"),
        ),
        out_specs=(
            P("dp", "tensor", None),
            P("dp", "tensor", None),
            P("dp", "tensor", None),
            P(None, "dp", "tensor"),
            P("tensor", "dp"),
            P("dp", "tensor"),
            P(None, "dp", "tensor"),
            P("tensor", "dp"),
            P("dp", "tensor"),
            P("tensor", "dp"),
            P("dp"),
            P("dp"),
            P("dp"),
            P("dp"),
            P("dp"),
            P("dp"),
        ),
        check_vma=False,
    )
```

```python
import functools

import jax
import jax.numpy as jnp
from jax import lax
from jax.experimental import pallas as pl
from jax.experimental.pallas import tpu as pltpu
from jax.sharding import PartitionSpec as P

DH = 64
LANES = 128
EPSILON = 1e-05
MASKED = -1e30
F32 = jnp.float32
BF16 = jnp.bfloat16
MESH = pl.DeviceIdType.MESH
HIGHEST = lax.Precision.HIGHEST


def nn(a, b):
    return lax.dot_general(a, b, (((1,), (0,)), ((), ())), preferred_element_type=F32)


def nt(a, b):
    return lax.dot_general(a, b, (((1,), (1,)), ((), ())), preferred_element_type=F32)


def normalize(values):
    center = values - jnp.mean(values, axis=-1, keepdims=True)
    spread = jnp.mean(center * center, axis=-1, keepdims=True)
    inv = lax.rsqrt(spread + EPSILON)
    return center * inv, inv


def norm_grad(values, grad, gain):
    xhat, inv = normalize(values)
    e = grad * gain
    back = inv * (
        e
        - jnp.mean(e, axis=-1, keepdims=True)
        - xhat * jnp.mean(e * xhat, axis=-1, keepdims=True)
    )
    return (
        back,
        jnp.sum(grad * xhat, axis=0, keepdims=True),
        jnp.sum(grad, axis=0, keepdims=True),
    )


def gelu_both(v):
    c = 0.7978845608028654
    v2 = v * v
    t = jnp.tanh(v * (c + (c * 0.044715) * v2))
    half = 0.5 * (1.0 + t)
    slope = half + (0.5 * v) * (1.0 - t * t) * (c + (3.0 * c * 0.044715) * v2)
    return v * half, slope


ORDERS = {
    "A0": ("xzy",),
    "A1": ("yzx",),
    "A2": ("zyx",),
    "W": ("zxy", "zyx"),
    "K": ("zxy", "zyx"),
    "Q0": ("zxy", "zyx"),
    "Q1": ("zxy", "zyx"),
    "U0": ("yxz",),
    "U1": ("zxy",),
    "D0": ("zxy",),
    "D1": ("zyx",),
    "rD0": ("zxy",),
    "rD1": ("zxy",),
    "rU0": ("xzy",),
    "rU1": ("yxz",),
    "rco": ("yzx",),
    "rcq": ("xzy",),
    "rck": ("zxy",),
    "rwo": ("zxy",),
    "rT": ("xyz", "yzx"),
    "rG": ("yzx",),
}

PLAN = {
    "p0": ("A2", "x", "W", "A1", "gz", "A1", "A2", "A0", "W", "gz", "x", "A0", "A2", "A1", "gz"),
    "p1": ("K", "m", "U0", "A2", "A0", "Q0", "A1", "Q1", "U1", "K", "W", "D0", "A0"),
    "p2": ("Q0", "m", "Q1", "U0", "D1"),
    "p3": ("K",),
    "p4": ("W",),
    "p5": (),
    "p6": ("Q0", "Q1", "U0"),
    "p7": ("U1",),
    "p8": ("K", "D1"),
    "p9": ("Q0", "D0"),
    "p10": ("Q1",),
    "p11": ("U1", "c"),
    "p12": (),
    "p13": (),
    "p14": ("D0", "D1"),
    "p15": ("U0",),
    "p16": ("U1",),
    "p17": ("c",),
    "p18": (),
    "p19": ("rD1", "D0", "D1"),
    "p20": (),
    "p21": ("rU0", "rU1"),
    "p22": ("rD0",),
    "p23": ("out", "rco"),
    "p24": (),
    "p25": ("rD1", "rU1"),
    "p26": ("rD1", "out", "rU0"),
    "p27": ("rD1", "rD0", "rU1"),
    "p28": ("rcq", "rck"),
    "p29": ("rD0", "gm"),
    "p30": ("rU0",),
    "p31": ("rU0", "rD0", "rU1"),
    "p32": ("gm", "rwo"),
    "p33": (),
    "p34": (),
    "p35": ("rT", "rcq"),
    "p36": ("rco",),
    "p37": ("rG", "rwo", "gi", "rck", "rT", "rcq", "rwo", "rco", "rG", "rcq", "rwo", "gi", "rT", "rck", "rco", "rG", "rck", "rG", "rT"),
}


def gather_segments(nf):
    mid = 8 + nf // 2
    end = 8 + nf
    last = end + nf // 2
    return {
        "A0": (0, 1), "A1": (1, 2), "A2": (2, 3), "W": (3, 4), "K": (4, 6), "Q0": (6, 7),
        "Q1": (7, 8), "U0": (8, mid), "U1": (mid, end), "D0": (end, last),
        "D1": (last, end + nf),
    }


def sum_segments(nf):
    mid = 9 + nf // 2
    end = 9 + nf
    last = end + nf // 2
    return {
        "rT": (0, 3), "rwo": (3, 4), "rck": (4, 6), "rcq": (6, 7), "rco": (7, 8), "rG": (8, 9),
        "rU0": (9, mid), "rU1": (mid, end), "rD0": (end, last), "rD1": (last, end + nf),
    }


def sum_shapes(order, segs, nz, ny, rows):
    shapes, left = [], {"x": 2 * LANES, "y": (ny,), "z": (nz,)}
    for i, axis in enumerate(order):
        left[axis] = LANES if axis == "x" else ()
        shape = (segs, *left["z"], *left["y"], rows, left["x"])
        shapes.append((nz - 1, *shape) if axis == "z" else shape)
        if i < 2:
            shapes.append(shape)
    return shapes


def layer_kernel(cfg, *refs):
    fused, nz, ny, rb, own, wide, nf = cfg
    rows_all = 4 * own
    nseg = 8 + 2 * nf
    gseg = 8
    refs = list(refs)

    def take(count):
        got, refs[:count] = refs[:count], []
        return got

    x_ref, m_ref, c_ref, tl_ref, sl_ref = take(5)
    if fused:
        wqkv_ref, wo_ref, cq_ref, ckv_ref, co_ref, up_ref, dn_ref = take(7)
        gain_refs = take(6)
    else:
        wfull_ref, gfull_ref = take(2)
    out_ref, gi_ref, gm_ref, gw_ref = take(4)
    (xs, ms, cs, wg, gains, n1, n2, n3, h1, h2, gh, gb16, qs, ks, vs, cqs, cks, cvs,
     vt, smix, cmix, slse, clse, act, gbf, dm, dq, dk, dv, ps, pr, ys, yr,
     us, ur, outs, osend, gis, gisend, gms, gmsend, gs, bias, gacc, score) = take(45)
    if fused:
        gz, gy = take(2)
        sums = {name: [take(5) for _ in ORDERS[name]] for name in sum_segments(nf)}
    ssem, rsem, xss, xrs, lsem = take(5)

    p = lax.axis_index("tensor") // 2
    c = lax.axis_index("tensor") % 2
    t = 2 * p + c
    tx = 2 * (1 - p) + c
    dp_at = lax.axis_index("dp")
    core_peer = {"dp": dp_at, "tensor": 2 * p + 1 - c}
    x_peer = {"dp": dp_at, "tensor": tx}
    z = dp_at // ny
    y = dp_at % ny
    y_peer = {"dp": z * ny + (1 - y), "tensor": t}

    y_other, p_other = 1 - y, 1 - p
    z_others = [(z + k) % nz for k in range(1, nz)]
    z_peers = [{"dp": at_z * ny + y, "tensor": t} for at_z in z_others]

    def z_peer(k):
        return z_peers[k - 1]

    counter = [0]
    sent = []

    def view(pair):
        ref, index = pair
        return ref if index is None else ref.at[index]

    class Sent:
        def __init__(self, src, dst, peer):
            self.parts = src, dst, peer, counter[0]
            counter[0] += 1

        def copy(self):
            src, dst, peer, i = self.parts
            return pltpu.make_async_remote_copy(
                view(src), view(dst), ssem.at[i], rsem.at[i],
                device_id=peer, device_id_type=MESH,
            )

        def wait_recv(self):
            self.copy().wait_recv()

    class Kept:
        def __init__(self, src, dst):
            self.parts = src, dst, lcount[0]
            lcount[0] += 1

        def copy(self):
            src, dst, i = self.parts
            return pltpu.make_async_copy(view(src), view(dst), lsem.at[i])

        def wait(self):
            self.copy().wait()

    def push(src, dst, peer):
        cp = Sent(src, dst, peer)
        cp.copy().start()
        sent.append(cp)
        return cp

    lcount = [0]

    def local(src, dst):
        cp = Kept(src, dst)
        cp.copy().start()
        return cp

    def rows(j, size=own):
        return pl.ds(pl.multiple_of(j * size, size), size)

    peers = [core_peer, x_peer]
    if fused:
        peers.append(y_peer)
        peers += [z_peer(k) for k in range(1, nz)]
    rows_t, rows_tx = rows(t), rows(tx)
    barrier = pltpu.get_barrier_semaphore()
    for peer in peers:
        pl.semaphore_signal(barrier, inc=1, device_id=peer, device_id_type=MESH)

    half = pl.ds(pl.multiple_of(p * LANES, LANES), LANES)
    other_half = pl.ds(pl.multiple_of((1 - p) * LANES, LANES), LANES)

    if fused:
        own_part = [wqkv_ref[...], wo_ref[...][None], ckv_ref[...], cq_ref[...][None]]
        own_part.append(co_ref[...][None])
        at = 0
        for piece in own_part:
            wg[at : at + piece.shape[0], z, y, :, half] = piece
            at += piece.shape[0]
        for i in range(nf):
            wg[8 + i, z, y, :, half] = up_ref[:, i * LANES : (i + 1) * LANES]
            wg[8 + nf + i, z, y, :, half] = dn_ref[:, i * LANES : (i + 1) * LANES]
        place = (
            lax.broadcasted_iota(jnp.int32, (rb, wide), 0) + dp_at * rb
            == lax.broadcasted_iota(jnp.int32, (rb, wide), 1)
        ).astype(BF16)
        gz[0] = jnp.zeros((16, wide), BF16)
        for i in range(6):
            gz[0, i : i + 1, :] = nn(gain_refs[i][...], place).astype(BF16)
    pl.semaphore_wait(barrier, len(peers))

    relays = {}

    def carry(name, src, buf):
        over = push((src, p_other), (buf, rows_t), x_peer)
        keep = local((src, p), (buf, rows_t))
        near = push((src, p), (buf, rows_t), core_peer)
        yield
        over.wait_recv()
        relays[name] = push((buf, rows_tx), (buf, rows_tx), core_peer)
        keep.wait()
        near.wait_recv()
        yield

    def back_over(src, buf):
        cp = push((src, None), (buf, p), x_peer)
        yield
        cp.wait_recv()
        yield

    tasks = {
        "x": [carry("x", x_ref, xs)],
        "m": [carry("m", m_ref, ms)],
        "c": [carry("c", c_ref, cs)],
        "out": [back_over(osend, outs)],
        "gm": [back_over(gmsend, gms)],
        "gi": [back_over(gisend, gis)],
        "gz": [],
    }

    def at(name):
        for task in PLAN[name]:
            for part in tasks[task]:
                next(part)

    def at_turn(i, turn, name):
        if PLAN[name]:

            @pl.when(i == turn)
            def _():
                at(name)

    def gather(lo, hi, first, last, order):
        r = slice(first, last)
        zi, yi, lanes = z, y, half
        hops = []
        for axis in order:
            for cp in hops:
                cp.wait_recv()
            part = (wg, (slice(lo, hi), zi, yi, r, lanes))
            if axis == "x":
                hops = [push(part, part, x_peer)]
                lanes = pl.ds(0, 2 * LANES)
            elif axis == "y":
                hops = [push(part, part, y_peer)]
                yi = slice(None)
            else:
                hops = [push(part, part, z_peer(k)) for k in range(1, nz)]
                zi = slice(None)
            yield
        for cp in hops:
            cp.wait_recv()
        yield

    def gain_rows():
        cps = [push((gz, 0), (gz, k), z_peer(k)) for k in range(1, nz)]
        yield
        for cp in cps:
            cp.wait_recv()
        total = gz[0].astype(F32)
        for k in range(1, nz):
            total = total + gz[k].astype(F32)
        gy[0] = total.astype(BF16)
        cp = push((gy, 0), (gy, 1), y_peer)
        yield
        cp.wait_recv()
        gains[...] = total + gy[1].astype(F32)
        yield

    for name, (lo, hi) in gather_segments(nf).items():
        size = rb // len(ORDERS[name])
        tasks[name] = [
            gather(lo, hi, i * size, (i + 1) * size, order)
            for i, order in enumerate(ORDERS[name])
            if fused
        ]
    if fused:
        tasks["gz"] = [gain_rows()]

    def weight(s):
        return wg[s].reshape(nz * ny * rb, 2 * LANES)

    if not fused:
        wcp = local((wfull_ref, None), (wg, None))
        gains[...] = gfull_ref[...]
    at("p0")
    relays["x"].wait_recv()
    if not fused:
        wcp.wait()

    sub = min(64, own)
    per = own // sub
    gacc[...] = jnp.zeros_like(gacc)

    def norm_rows(i, _):
        r = rows(i, sub)
        xhat, _unused = normalize(xs[r, :].astype(F32))
        n1[r, :] = (xhat * gains[0:1, :] + gains[1:2, :]).astype(BF16)
        return 0

    lax.fori_loop(0, 4 * per, norm_rows, 0)
    at("p1")

    def put_pairs(buf, r, value):
        v = value.astype(BF16)
        buf[0, r, :] = v[:, :LANES]
        buf[1, r, :] = v[:, LANES:]

    def pairs(buf, r):
        return jnp.concatenate([buf[0, r, :], buf[1, r, :]], axis=1)

    scale = DH ** (-0.5)

    def put_transposed(buf, r, value):
        vt_ = value.T.astype(BF16)
        buf[0, :, r] = vt_[:LANES]
        buf[1, :, r] = vt_[LANES:]

    def project(j, _):
        r = rows(j)
        rowsv = n1[r, :]
        put_pairs(qs, r, nn(rowsv, weight(0)).astype(BF16) * jnp.asarray(scale, BF16))
        put_pairs(ks, r, nn(rowsv, weight(1)))
        val = nn(rowsv, weight(2))
        put_pairs(vs, r, val)
        put_transposed(vt, r, val.astype(BF16).astype(F32))
        return 0

    lax.fori_loop(0, 4, project, 0)
    at("p2")


    lane_at = lax.broadcasted_iota(jnp.int32, (1, LANES), 1)
    head_lanes = [((lane_at // DH) == u).astype(F32).astype(BF16) for u in range(2)]

    def only(value, u):
        return value * head_lanes[u]

    wide_rows = 2 * own

    def qrows(jj):
        return pl.ds(pl.multiple_of(jj * wide_rows, wide_rows), wide_rows)

    def hide(scores, first, diagonal, causal):
        if causal and not diagonal:
            return scores
        if causal:
            key_at = lax.broadcasted_iota(jnp.int32, scores.shape, 0)
            query_at = lax.broadcasted_iota(jnp.int32, scores.shape, 1)
            return jnp.where(key_at <= query_at, scores, MASKED)
        b = bias[first : first + scores.shape[0], :]
        return scores + jnp.concatenate([b] * (wide_rows // LANES), axis=1)

    def attend(pp, q_s, k_s, v_t, mix, lse, r, keys, causal):
        parts_k = [slice(i * wide_rows, (i + 1) * wide_rows) for i in range(keys // wide_rows)]

        q = q_s[pp, r, :]
        tops = [None, None]
        for i, kk in enumerate(parts_k):
            for u in range(2):
                s = nt(only(k_s[pp, kk, :], u), q)
                s = hide(s, kk.start, i == len(parts_k) - 1, causal)
                top = jnp.max(s, axis=0, keepdims=True)
                tops[u] = top if i == 0 else jnp.maximum(tops[u], top)
                score[u, kk, :] = s
        totals, mixed = [None, None], [None, None]
        for i, kk in enumerate(parts_k):
            for u in range(2):
                e = jnp.exp(score[u, kk, :] - tops[u])
                total = jnp.sum(e, axis=0, keepdims=True)
                o = nn(v_t[pp, u * DH : (u + 1) * DH, kk], e.astype(BF16))
                totals[u] = total if i == 0 else totals[u] + total
                mixed[u] = o if i == 0 else mixed[u] + o
        for u in range(2):
            lse[2 * pp + u, :, r] = tops[u] + jnp.log(totals[u])
            mixed[u] = mixed[u] * (1.0 / totals[u])
        mix[pp, r, :] = jnp.concatenate(mixed, axis=0).T.astype(BF16)

    def exchange(point, j):
        b = point % 2
        i = point * 4 + j
        return pltpu.make_async_remote_copy(
            ps.at[b, rows(j)], pr.at[b, rows(j)], xss.at[i], xrs.at[i],
            device_id=core_peer, device_id_type=MESH,
        )

    def send_sum(point, j, value):
        ps[point % 2, rows(j), :] = value.astype(BF16)
        exchange(point, j).start()

    def summed(point, r):
        b = point % 2
        return ps[b, r, :].astype(F32) + pr[b, r, :].astype(F32)

    for jj in range(2):
        first = 3 + 3 * jj

        def self_pair(pp, _, jj=jj, first=first):
            attend(pp, qs, ks, vt, smix, slse, qrows(jj), wide_rows * (jj + 1), True)
            at_turn(pp, 0, f"p{first}")
            at_turn(pp, 1, f"p{first + 1}")
            return 0

        lax.fori_loop(0, 2, self_pair, 0)
        for j in (2 * jj, 2 * jj + 1):
            send_sum(0, j, nt(pairs(smix, rows(j)), weight(3)))
        at(f"p{first + 2}")
    relays["m"].wait_recv()

    key_at = lax.broadcasted_iota(jnp.int32, (rows_all, LANES), 0)
    bias[...] = jnp.where(key_at < sl_ref[p], 0.0, MASKED)

    def project_cross(j, _):
        r = rows(j)
        rowsv = ms[r, :]
        put_pairs(cks, r, nn(rowsv, weight(4)))
        val = nn(rowsv, weight(5))
        put_pairs(cvs, r, val)
        put_transposed(vt, r, val.astype(BF16).astype(F32))
        return 0

    lax.fori_loop(0, 4, project_cross, 0)
    at("p9")

    def second(j, _):
        exchange(0, j).wait_recv()
        exchange(0, j).wait_send()

        def part(i, _):
            r = rows(j * per + i, sub)
            h = xs[r, :].astype(F32) + summed(0, r)
            h1[r, :] = h
            xhat, _unused = normalize(h)
            n2[r, :] = (xhat * gains[2:3, :] + gains[3:4, :]).astype(BF16)
            return 0

        lax.fori_loop(0, per, part, 0)
        r = rows(j)
        put_pairs(cqs, r, nn(n2[r, :], weight(6)).astype(BF16) * jnp.asarray(scale, BF16))
        return 0

    lax.fori_loop(0, 4, second, 0)
    at("p10")

    def cross_pair(i, _):
        jj, pp = i // 2, i % 2
        attend(pp, cqs, cks, vt, cmix, clse, qrows(jj), rows_all, False)
        for k, name in enumerate(("p11", "p12", "p14", "p15")):
            at_turn(i, k, name)

        @pl.when(pp == 1)
        def _():
            for k in range(2):
                j = 2 * jj + k
                send_sum(1, j, nt(pairs(cmix, rows(j)), weight(7)))

        at_turn(i, 1, "p13")
        return 0

    lax.fori_loop(0, 4, cross_pair, 0)
    at("p16")

    limit = tl_ref[p]

    def live(r_first, size):
        at = lax.broadcasted_iota(jnp.int32, (size, wide), 0) + r_first
        return at < limit

    def weight_grads(a_buf, items):
        chunk = ny * rb
        for zi in range(nz):
            at = a_buf[:, zi * chunk : (zi + 1) * chunk].T
            for s, load in items:
                gs[s, zi] = nn(at, load()).astype(BF16).reshape(ny, rb, 2 * LANES)

    every = pl.ds(0, rows_all)

    def whole(buf):
        return lambda: pairs(buf, every)

    def plane(buf, s):
        return lambda: buf[s]

    def reduce_part(lo, hi, first, last, order, bufs):
        r = slice(first, last)
        base = lo
        bufs = list(bufs)
        gone = []

        def at(buf, s, zsel, ysel, lsel):
            index = [s]
            if "z" not in gone:
                index.append(zsel)
            if "y" not in gone:
                index.append(ysel)
            index += [slice(None) if buf is not gs else r, lsel]
            return tuple(index)

        every_one = slice(None)
        cur, shift = gs, 0
        for hop, axis in enumerate(order):
            span = slice(lo - shift, hi - shift)
            land = bufs.pop(0)
            to = slice(lo - base, hi - base)
            lanes = every_one if "x" in gone else slice(0, 2 * LANES)
            pick = {"z": every_one, "y": every_one, "x": lanes}
            here = dict(pick)
            if axis == "x":
                pick["x"], here["x"] = other_half, half
                sends = [(pick, (land, to), x_peer)]
            elif axis == "y":
                pick["y"], here["y"] = y_other, y
                sends = [(pick, (land, to), y_peer)]
            else:
                here["z"] = z
                sends = [
                    (dict(pick, z=z_others[k - 1]), (land, (k - 1, to)), z_peer(k))
                    for k in range(1, nz)
                ]
            cps = [
                push((cur, at(cur, span, sel["z"], sel["y"], sel["x"])), dst, peer)
                for sel, dst, peer in sends
            ]
            yield
            for cp in cps:
                cp.wait_recv()
            done = hop == 2
            acc = None if done else bufs.pop(0)

            def add(s, _):
                v = cur[at(cur, s - shift, here["z"], here["y"], here["x"])].astype(F32)
                if axis == "z":
                    for k in range(1, nz):
                        v = v + land[k - 1, s - base].astype(F32)
                else:
                    v = v + land[s - base].astype(F32)
                if done:
                    gw_ref[s, r] = v
                else:
                    acc[s - base] = v.astype(BF16)
                return 0

            lax.fori_loop(lo, hi, add, 0)
            gone.append(axis)
            cur, shift = acc, base
        yield

    for name, (lo, hi) in sum_segments(nf).items():
        size = rb // len(ORDERS[name])
        tasks[name] = [
            reduce_part(lo, hi, i * size, (i + 1) * size, order, sums[name][i])
            for i, order in enumerate(ORDERS[name])
            if fused
        ]

    def third(j, _):
        exchange(1, j).wait_recv()
        exchange(1, j).wait_send()

        def part(i, _):
            r = rows(j * per + i, sub)
            h = h1[r, :] + summed(1, r)
            h2[r, :] = h
            xhat, _unused = normalize(h)
            n3[r, :] = (xhat * gains[4:5, :] + gains[5:6, :]).astype(BF16)
            return 0

        lax.fori_loop(0, per, part, 0)
        r = rows(j)
        rowsv = n3[r, :]
        for s in range(nf):
            active, slope = gelu_both(nn(rowsv, weight(8 + s)))
            act[s, r, :] = active.astype(BF16)
            gbf[s, r, :] = slope.astype(BF16)
        at_turn(j, 1, "p17")
        return 0

    lax.fori_loop(0, 4, third, 0)
    at("p18")
    relays["c"].wait_recv()

    def live_rows(i, _):
        r = rows(i, sub)
        cot = cs[r, :]
        gb16[r, :] = jnp.where(live(i * sub, sub), cot, jnp.zeros_like(cot))
        return 0

    lax.fori_loop(0, 4 * per, live_rows, 0)
    weight_grads(gb16, [(9 + nf + s, plane(act, s)) for s in range(nf)])
    at("p19")

    def third_back(j, _):
        r = rows(j)
        cot = gb16[r, :]
        for s in range(nf):
            slope = gbf[s, r, :].astype(F32)
            gbf[s, r, :] = (nn(cot, weight(8 + nf + s)) * slope).astype(BF16)
        back = nt(gbf[0, r, :], weight(8))
        for s in range(1, nf):
            back = back + nt(gbf[s, r, :], weight(8 + s))
        send_sum(2, j, back)
        val = nt(act[0, r, :], weight(8 + nf))
        for s in range(1, nf):
            val = val + nt(act[s, r, :], weight(8 + nf + s))
        ys[r, :] = val.astype(BF16)
        at_turn(j, 1, "p20")
        return 0

    lax.fori_loop(0, 4, third_back, 0)

    ycp = [
        push((ys, rows(2 * k + 1 - c)), (yr, k), core_peer) for k in range(2)
    ]

    weight_grads(n3, [(9 + s, plane(gbf, s)) for s in range(nf)])
    at("p21")

    def finish_rows(k, dst):
        def part(i, _):
            r = rows((2 * k + c) * per + i, sub)
            q = rows(i, sub)
            val = h2[r, :] + ys[r, :].astype(F32) + yr[k, q, :].astype(F32)
            keep = live(((2 * k + c) * per + i) * sub, sub)
            dst[q, :] = jnp.where(keep, val, 0.0).astype(BF16)
            return 0
        lax.fori_loop(0, per, part, 0)

    for cp in ycp:
        cp.wait_recv()
    finish_rows(1 - p, osend)
    finish_rows(p, outs.at[p])
    at("p22")

    def back_three(j, _):
        exchange(2, j).wait_recv()
        exchange(2, j).wait_send()

        def part(i, _):
            r = rows(j * per + i, sub)
            dx, dgain, dbias = norm_grad(h2[r, :], summed(2, r), gains[4:5, :])
            gacc[4:5, :] += dgain
            gacc[5:6, :] += dbias
            g = gb16[r, :].astype(F32) + dx
            gh[r, :] = g
            gb16[r, :] = g.astype(BF16)
            return 0

        return lax.fori_loop(0, per, part, 0)

    lax.fori_loop(0, 4, back_three, 0)
    weight_grads(gb16, [(7, whole(cmix))])
    at("p23")


    sel_row = lax.broadcasted_iota(jnp.int32, (8, LANES), 0)
    sel_lane = lax.broadcasted_iota(jnp.int32, (8, LANES), 1)
    selector = (sel_lane // DH == sel_row).astype(F32)

    def pair_lanes(pp):
        return pl.ds(pl.multiple_of(pp * LANES, LANES), LANES)

    def attend_back(pp, q_s, k_s, kt, v_s, mix, lse, r, keys, causal):
        parts_k = [slice(0, keys)]
        if causal and keys > wide_rows:
            parts_k = [slice(0, keys - wide_rows), slice(keys - wide_rows, keys)]

        q = q_s[pp, r, :]
        do = dm[pp, r, :]
        prod = do.astype(F32) * mix[pp, r, :].astype(F32)
        delta = lax.dot_general(
            selector, prod, (((1,), (1,)), ((), ())),
            precision=HIGHEST, preferred_element_type=F32,
        )
        back = None
        for i, kk in enumerate(parts_k):
            parts = []
            for u in range(2):
                s = nt(only(k_s[pp, kk, :], u), q)
                s = hide(s, kk.start, i == len(parts_k) - 1, causal)
                e = jnp.exp(s - lse[2 * pp + u, :, r])
                d = nt(only(v_s[pp, kk, :], u), do)
                ds = (e * (d - delta[u : u + 1])).astype(BF16)
                dv_u = nn(e.astype(BF16), only(do, u))
                dk_u = nn(ds, only(q, u))
                dvp = dv_u if u == 0 else dvp + dv_u
                dkp = dk_u if u == 0 else dkp + dk_u
                parts.append(nn(kt[pp, u * DH : (u + 1) * DH, kk], ds))
            lanes = pair_lanes(pp)
            score[0, kk, lanes] += dkp
            score[1, kk, lanes] += dvp
            parts = jnp.concatenate(parts, axis=0)
            back = parts if i == 0 else back + parts
        dq[pp, r, :] = (back * scale).T.astype(BF16)

    def transpose_keys(buf):
        def one(j, _):
            r = rows(j)
            for pp in range(2):
                vt[pp, :, r] = buf[pp, r, :].astype(F32).T.astype(BF16)
            return 0
        lax.fori_loop(0, 4, one, 0)

    transpose_keys(cks)
    score[:, :, : 2 * LANES] = jnp.zeros((2, rows_all, 2 * LANES), F32)

    def cross_back_pair(i, _):
        jj, pp = i // 2, i % 2

        @pl.when(pp == 0)
        def _():
            for k in range(2):
                r = rows(2 * jj + k)
                put_pairs(dm, r, nn(gb16[r, :], weight(7)))

        attend_back(pp, cqs, cks, vt, cvs, cmix, clse, qrows(jj), rows_all, False)
        for k in range(4):
            at_turn(i, k, f"p{24 + k}")

        @pl.when(pp == 1)
        def _():
            for k in range(2):
                j = 2 * jj + k
                send_sum(3, j, nt(pairs(dq, rows(j)), weight(6)))

        return 0

    lax.fori_loop(0, 4, cross_back_pair, 0)

    def cross_back_keys(j, _):
        r = rows(j)
        for pp in range(2):
            dk[pp, r, :] = score[0, r, pair_lanes(pp)].astype(BF16)
            dv[pp, r, :] = score[1, r, pair_lanes(pp)].astype(BF16)
        val = nt(pairs(dk, r), weight(4)) + nt(pairs(dv, r), weight(5))
        us[r, :] = val.astype(BF16)
        return 0

    lax.fori_loop(0, 4, cross_back_keys, 0)
    ucp = [
        push((us, rows(2 * k + 1 - c)), (ur, k), core_peer) for k in range(2)
    ]
    weight_grads(n2, [(6, whole(dq))])
    weight_grads(ms, [(4, whole(dk)), (5, whole(dv))])
    at("p28")

    def memory_rows(k, dst):
        def part(i, _):
            r = rows((2 * k + c) * per + i, sub)
            q = rows(i, sub)
            dst[q, :] = (us[r, :].astype(F32) + ur[k, q, :].astype(F32)).astype(BF16)
            return 0
        lax.fori_loop(0, per, part, 0)

    for cp in ucp:
        cp.wait_recv()
    memory_rows(1 - p, gmsend)
    memory_rows(p, gms.at[p])
    at("p29")

    def back_two(j, _):
        exchange(3, j).wait_recv()
        exchange(3, j).wait_send()

        def part(i, _):
            r = rows(j * per + i, sub)
            dx, dgain, dbias = norm_grad(h1[r, :], summed(3, r), gains[2:3, :])
            gacc[2:3, :] += dgain
            gacc[3:4, :] += dbias
            g = gh[r, :] + dx
            gh[r, :] = g
            gb16[r, :] = g.astype(BF16)
            return 0

        return lax.fori_loop(0, per, part, 0)

    lax.fori_loop(0, 4, back_two, 0)
    weight_grads(gb16, [(3, whole(smix))])
    at("p30")

    transpose_keys(ks)
    score[:, :, : 2 * LANES] = jnp.zeros((2, rows_all, 2 * LANES), F32)
    for jj in (1, 0):
        for j in (2 * jj, 2 * jj + 1):
            put_pairs(dm, rows(j), nn(gb16[rows(j), :], weight(3)))
        first = 33 - 2 * jj

        def self_back_pair(pp, _, jj=jj, first=first):
            attend_back(pp, qs, ks, vt, vs, smix, slse, qrows(jj), wide_rows * (jj + 1), True)
            at_turn(pp, 0, f"p{first}")
            at_turn(pp, 1, f"p{first + 1}")
            return 0

        lax.fori_loop(0, 2, self_back_pair, 0)
        for j in (2 * jj, 2 * jj + 1):
            r = rows(j)
            for pp in range(2):
                dk[pp, r, :] = score[0, r, pair_lanes(pp)].astype(BF16)
                dv[pp, r, :] = score[1, r, pair_lanes(pp)].astype(BF16)
            val = nt(pairs(dq, r), weight(0)) + nt(pairs(dk, r), weight(1))
            send_sum(4, j, val + nt(pairs(dv, r), weight(2)))

    weight_grads(n1, [(0, whole(dq)), (1, whole(dk)), (2, whole(dv))])
    at("p35")

    def back_one(k, j, dst):
        exchange(4, j).wait_recv()

        def part(i, _):
            r = rows(j * per + i, sub)
            q = rows(i, sub)
            dx, dgain, dbias = norm_grad(xs[r, :].astype(F32), summed(4, r), gains[0:1, :])
            gacc[0:1, :] += dgain
            gacc[1:2, :] += dbias
            if dst is not None:
                dst[q, :] = (gh[r, :] + dx).astype(BF16)
            return 0

        lax.fori_loop(0, per, part, 0)

    back_one(0, tx, gisend)
    at("p36")
    back_one(0, t, gis.at[p])
    back_one(0, 2 * p + 1 - c, None)
    back_one(0, 2 * (1 - p) + 1 - c, None)
    for j in range(4):
        exchange(4, j).wait_send()

    spread_rows = jnp.concatenate(
        [gacc[...], jnp.zeros((LANES - 8, wide), F32)], axis=0
    )
    columns = spread_rows.T.astype(BF16)
    gs[gseg] = jnp.concatenate([columns, columns], axis=1).reshape(nz, ny, rb, 2 * LANES)

    at("p37")
    last = [] if fused else [local((gs, None), (gw_ref, None))]

    finals = [
        local((outs, None), (out_ref, None)),
        local((gms, None), (gm_ref, None)),
        local((gis, None), (gi_ref, None)),
    ]
    for cp in finals + last:
        cp.wait()
    for cp in sent:
        cp.copy().wait_send()


def unpack_kernel(nf, o_ref, gi_ref, gm_ref, gw_ref, *outs):
    outs[0][...] = o_ref[...]
    outs[1][...] = gi_ref[...].astype(F32)
    outs[2][...] = gm_ref[...].astype(F32)
    outs[3][...] = gw_ref[0:3]
    outs[4][...] = gw_ref[3]
    outs[5][...] = gw_ref[6]
    outs[6][...] = gw_ref[4:6]
    outs[7][...] = gw_ref[7]
    for i in range(nf):
        outs[8][:, i * LANES : (i + 1) * LANES] = gw_ref[9 + i]
        outs[9][:, i * LANES : (i + 1) * LANES] = gw_ref[9 + nf + i]
    vectors = gw_ref[8].T
    for i in range(6):
        outs[10 + i][...] = vectors[i : i + 1]


def body(ndp, inputs, memory, tgt_len, src_len, cotangent, w_qkv, w_out, cross_query, cross_kv,
         cross_out, ffn_up, ffn_down, *gain_list):
    own, wide = inputs.shape[1], inputs.shape[2]
    rb = w_qkv.shape[1]
    nf = ffn_up.shape[1] // LANES
    nseg = 8 + 2 * nf
    rows_all = 4 * own
    fused = rb % 32 == 0 and ndp % 2 == 0
    if fused:
        ny, nz, block = 2, ndp // 2, rb
    else:
        ny, nz, block = 1, 1, wide
    cfg = (fused, nz, ny, block, own, wide, nf)

    any_spec = pl.BlockSpec(memory_space=pl.ANY)
    smem = pl.BlockSpec(memory_space=pltpu.SMEM)
    vmem = pl.BlockSpec(memory_space=pltpu.VMEM)
    operands = [inputs, memory, cotangent, tgt_len, src_len]
    specs = [any_spec] * 3 + [smem] * 2
    if fused:
        weights = [w_qkv, w_out.T, cross_query, cross_kv, cross_out.T, ffn_up, ffn_down.T]
        weights += [g[None, :] for g in gain_list]
        operands += weights
        specs += [vmem] * len(weights)
    else:
        pieces = [w_qkv, w_out.T[None], cross_kv, cross_query[None], cross_out.T[None]]
        pieces += [ffn_up.reshape(rb, nf, LANES).swapaxes(0, 1)]
        pieces += [ffn_down.reshape(nf, LANES, rb).swapaxes(1, 2)]
        packed = lax.all_gather(jnp.concatenate(pieces, axis=0), "dp", axis=1, tiled=True)
        index = lax.axis_index("tensor")
        flipped = lax.ppermute(packed, "tensor", [(i, (i + 2) % 4) for i in range(4)])
        low = jnp.where(index < 2, packed, flipped)
        high = jnp.where(index < 2, flipped, packed)
        full = jnp.concatenate([low, high], axis=2)[:, None, None]
        gathered = lax.all_gather(jnp.stack(gain_list), "dp", axis=1, tiled=True)
        operands += [full, jnp.pad(gathered.astype(F32), ((0, 10), (0, 0)))]
        specs += [any_spec, vmem]

    bf = lambda *shape: pltpu.VMEM(shape, BF16)
    fl = lambda *shape: pltpu.VMEM(shape, F32)
    seq = (rows_all, wide)
    heads = (2, rows_all, LANES)
    scratch = [
        bf(*seq), bf(*seq), bf(*seq), bf(nseg, nz, ny, block, 2 * LANES), fl(16, wide),
        bf(*seq), bf(*seq), bf(*seq), fl(*seq), fl(*seq), fl(*seq), bf(*seq),
        bf(*heads), bf(*heads), bf(*heads), bf(*heads), bf(*heads), bf(*heads),
        bf(2, LANES, rows_all), bf(*heads), bf(*heads), fl(4, 1, rows_all), fl(4, 1, rows_all),
        bf(nf, rows_all, 2 * LANES), bf(nf, rows_all, 2 * LANES),
        bf(*heads), bf(*heads), bf(*heads), bf(*heads),
        bf(2, *seq), bf(2, *seq), bf(*seq), bf(2, own, wide), bf(*seq), bf(2, own, wide),
        bf(2, own, wide), bf(own, wide), bf(2, own, wide), bf(own, wide),
        bf(2, own, wide), bf(own, wide),
        bf(nseg + 1, nz, ny, block, 2 * LANES), fl(rows_all, LANES), fl(8, wide),
        fl(2, rows_all, 2 * own),
    ]
    if fused:
        scratch += [bf(nz, 16, wide), bf(2, 16, wide)]
        for name, (lo, hi) in sum_segments(nf).items():
            for order in ORDERS[name]:
                shapes = sum_shapes(order, hi - lo, nz, ny, block // len(ORDERS[name]))
                scratch += [bf(*shape) for shape in shapes]
    dma = pltpu.SemaphoreType.DMA
    scratch += [dma((250,)), dma((250,)), dma((20,)), dma((20,)), dma((12,))]

    if fused:
        grads_shape = jax.ShapeDtypeStruct((nseg + 1, block, LANES), F32)
        grads_spec = vmem
    else:
        grads_shape = jax.ShapeDtypeStruct((nseg + 1, nz, ny, block, 2 * LANES), BF16)
        grads_spec = any_spec
    act_shape = jax.ShapeDtypeStruct(inputs.shape, BF16)
    output, grad_in, grad_mem, grads = pl.pallas_call(
        functools.partial(layer_kernel, cfg),
        out_shape=(act_shape, act_shape, act_shape, grads_shape),
        in_specs=specs,
        out_specs=(any_spec, any_spec, any_spec, grads_spec),
        scratch_shapes=scratch,
        compiler_params=pltpu.CompilerParams(
            collective_id=0, has_side_effects=True, vmem_limit_bytes=62 << 20
        ),
        name="layer",
    )(*operands)

    if not fused:
        mine = grads[:, 0, 0].astype(F32)
        index = lax.axis_index("tensor")
        low, high = mine[:, :, :LANES], mine[:, :, LANES:]
        keep = jnp.where(index < 2, low, high)
        give = jnp.where(index < 2, high, low)
        keep = keep + lax.ppermute(give, "tensor", [(i, (i + 2) % 4) for i in range(4)])
        grads = lax.psum_scatter(keep, "dp", scatter_dimension=1, tiled=True)

    shapes = [
        (inputs.shape, BF16), (inputs.shape, F32), (memory.shape, F32),
        (w_qkv.shape, F32), (w_out.shape[::-1], F32), (cross_query.shape, F32),
        (cross_kv.shape, F32), (cross_out.shape[::-1], F32), (ffn_up.shape, F32),
        (ffn_down.shape[::-1], F32),
    ] + [((1, rb), F32)] * 6
    got = pl.pallas_call(
        functools.partial(unpack_kernel, nf),
        out_shape=[jax.ShapeDtypeStruct(*s) for s in shapes],
        in_specs=[vmem] * 4,
        out_specs=[vmem] * len(shapes),
        name="unpack",
    )(output, grad_in, grad_mem, grads)
    return (
        *got[:4], got[4].T, got[5], got[6], got[7].T, got[8], got[9].T,
        *[g[0] for g in got[10:]],
    )


def solution(mesh):
    return jax.shard_map(
        functools.partial(body, mesh.shape["dp"]),
        mesh=mesh,
        in_specs=(
            P("dp", "tensor", None),
            P("dp", "tensor", None),
            P("dp"),
            P("dp"),
            P("dp", "tensor", None),
            P(None, "dp", "tensor"),
            P("tensor", "dp"),
            P("dp", "tensor"),
            P(None, "dp", "tensor"),
            P("tensor", "dp"),
            P("dp", "tensor"),
            P("tensor", "dp"),
            P("dp"),
            P("dp"),
            P("dp"),
            P("dp"),
            P("dp"),
            P("dp"),
        ),
        out_specs=(
            P("dp", "tensor", None),
            P("dp", "tensor", None),
            P("dp", "tensor", None),
            P(None, "dp", "tensor"),
            P("tensor", "dp"),
            P("dp", "tensor"),
            P(None, "dp", "tensor"),
            P("tensor", "dp"),
            P("dp", "tensor"),
            P("tensor", "dp"),
            P("dp"),
            P("dp"),
            P("dp"),
            P("dp"),
            P("dp"),
            P("dp"),
        ),
        check_vma=False,
    )
```

```python
import functools

import jax
import jax.numpy as jnp
from jax import lax
from jax.experimental import pallas as pl
from jax.experimental.pallas import tpu as pltpu
from jax.sharding import PartitionSpec as P

DH = 64
LANES = 128
EPSILON = 1e-05
MASKED = -1e30
F32 = jnp.float32
BF16 = jnp.bfloat16
MESH = pl.DeviceIdType.MESH
HIGHEST = lax.Precision.HIGHEST


def nn(a, b):
    return lax.dot_general(a, b, (((1,), (0,)), ((), ())), preferred_element_type=F32)


def nt(a, b):
    return lax.dot_general(a, b, (((1,), (1,)), ((), ())), preferred_element_type=F32)


def normalize(values):
    center = values - jnp.mean(values, axis=-1, keepdims=True)
    spread = jnp.mean(center * center, axis=-1, keepdims=True)
    inv = lax.rsqrt(spread + EPSILON)
    return center * inv, inv


def norm_grad(values, grad, gain):
    xhat, inv = normalize(values)
    e = grad * gain
    back = inv * (
        e
        - jnp.mean(e, axis=-1, keepdims=True)
        - xhat * jnp.mean(e * xhat, axis=-1, keepdims=True)
    )
    return (
        back,
        jnp.sum(grad * xhat, axis=0, keepdims=True),
        jnp.sum(grad, axis=0, keepdims=True),
    )


def gelu_both(v):
    c = 0.7978845608028654
    v2 = v * v
    t = jnp.tanh(v * (c + (c * 0.044715) * v2))
    half = 0.5 * (1.0 + t)
    slope = half + (0.5 * v) * (1.0 - t * t) * (c + (3.0 * c * 0.044715) * v2)
    return v * half, slope


ORDERS = {
    "A0": ("xzy",),
    "A1": ("yzx",),
    "A2": ("zyx",),
    "W": ("zxy", "zyx"),
    "K": ("zxy", "zyx"),
    "Q0": ("zxy", "zyx"),
    "Q1": ("zxy", "zyx"),
    "U0": ("yxz",),
    "U1": ("zxy",),
    "D0": ("zxy",),
    "D1": ("zyx",),
    "rD0": ("zxy",),
    "rD1": ("zxy",),
    "rU0": ("xzy",),
    "rU1": ("yxz",),
    "rco": ("yzx",),
    "rcq": ("xzy",),
    "rck": ("zxy",),
    "rwo": ("zxy",),
    "rT": ("xyz", "yzx"),
    "rG": ("yzx",),
}

PLAN = {
    "p0": ("A2", "x", "W", "A1", "gz", "A1", "A2", "A0", "W", "gz", "x", "A0", "A2", "A1", "gz"),
    "p1": ("K", "m", "U0", "A2", "A0", "Q0", "A1", "Q1", "U1", "K", "W", "D0", "A0"),
    "p2": ("Q0", "m", "Q1", "U0", "D1"),
    "p3": ("K",),
    "p4": ("W",),
    "p5": (),
    "p6": ("Q0", "Q1", "U0"),
    "p7": ("U1",),
    "p8": ("K", "D1"),
    "p9": ("Q0", "D0"),
    "p10": ("Q1",),
    "p11": ("U1", "c"),
    "p12": (),
    "p13": (),
    "p14": ("D0", "D1"),
    "p15": ("U0",),
    "p16": ("U1",),
    "p17": ("c",),
    "p18": (),
    "p19": ("rD1", "D0", "D1"),
    "p20": (),
    "p21": ("rU0", "rU1"),
    "p22": ("rD0",),
    "p23": ("out", "rco"),
    "p24": (),
    "p25": ("rD1", "rU1"),
    "p26": ("rD1", "out", "rU0"),
    "p27": ("rD1", "rD0", "rU1"),
    "p28": ("rcq", "rck"),
    "p29": ("rD0", "gm"),
    "p30": ("rU0",),
    "p31": ("rU0", "rD0", "rU1"),
    "p32": ("gm", "rwo"),
    "p33": (),
    "p34": (),
    "p35": ("rT", "rcq"),
    "p36": ("rco",),
    "p37": ("rG", "rwo", "gi", "rck", "rT", "rcq", "rwo", "rco", "rG", "rcq", "rwo", "gi", "rT", "rck", "rco", "rG", "rck", "rG", "rT"),
}


def gather_segments(nf):
    mid = 8 + nf // 2
    end = 8 + nf
    last = end + nf // 2
    return {
        "A0": (0, 1), "A1": (1, 2), "A2": (2, 3), "W": (3, 4), "K": (4, 6), "Q0": (6, 7),
        "Q1": (7, 8), "U0": (8, mid), "U1": (mid, end), "D0": (end, last),
        "D1": (last, end + nf),
    }


def sum_segments(nf):
    mid = 9 + nf // 2
    end = 9 + nf
    last = end + nf // 2
    return {
        "rT": (0, 3), "rwo": (3, 4), "rck": (4, 6), "rcq": (6, 7), "rco": (7, 8), "rG": (8, 9),
        "rU0": (9, mid), "rU1": (mid, end), "rD0": (end, last), "rD1": (last, end + nf),
    }


def sum_shapes(order, segs, nz, ny, rows):
    shapes, left = [], {"x": 2 * LANES, "y": (ny,), "z": (nz,)}
    for i, axis in enumerate(order):
        left[axis] = LANES if axis == "x" else ()
        shape = (segs, *left["z"], *left["y"], rows, left["x"])
        shapes.append((nz - 1, *shape) if axis == "z" else shape)
        if i < 2:
            shapes.append(shape)
    return shapes


def layer_kernel(cfg, *refs):
    fused, nz, ny, rb, own, wide, nf = cfg
    rows_all = 4 * own
    nseg = 8 + 2 * nf
    gseg = 8
    refs = list(refs)

    def take(count):
        got, refs[:count] = refs[:count], []
        return got

    x_ref, m_ref, c_ref, tl_ref, sl_ref = take(5)
    if fused:
        wqkv_ref, wo_ref, cq_ref, ckv_ref, co_ref, up_ref, dn_ref = take(7)
        gain_refs = take(6)
    else:
        wfull_ref, gfull_ref = take(2)
    out_ref, gi_ref, gm_ref, gw_ref = take(4)
    (xs, ms, cs, wg, gains, n1, n2, n3, h1, h2, gh, gb16, qs, ks, vs, cqs, cks, cvs,
     vt, smix, cmix, slse, clse, act, gbf, dm, dq, dk, dv, ps, pr, ys, yr,
     us, ur, outs, osend, gis, gisend, gms, gmsend, gs, bias, gacc, score) = take(45)
    if fused:
        gz, gy = take(2)
        sums = {name: [take(5) for _ in ORDERS[name]] for name in sum_segments(nf)}
    ssem, rsem, xss, xrs, lsem = take(5)

    p = lax.axis_index("tensor") // 2
    c = lax.axis_index("tensor") % 2
    t = 2 * p + c
    tx = 2 * (1 - p) + c
    dp_at = lax.axis_index("dp")
    core_peer = {"dp": dp_at, "tensor": 2 * p + 1 - c}
    x_peer = {"dp": dp_at, "tensor": tx}
    z = dp_at // ny
    y = dp_at % ny
    y_peer = {"dp": z * ny + (1 - y), "tensor": t}

    y_other, p_other = 1 - y, 1 - p
    z_others = [(z + k) % nz for k in range(1, nz)]
    z_peers = [{"dp": at_z * ny + y, "tensor": t} for at_z in z_others]

    def z_peer(k):
        return z_peers[k - 1]

    counter = [0]
    sent = []

    def view(pair):
        ref, index = pair
        return ref if index is None else ref.at[index]

    class Sent:
        def __init__(self, src, dst, peer):
            self.parts = src, dst, peer, counter[0]
            counter[0] += 1

        def copy(self):
            src, dst, peer, i = self.parts
            return pltpu.make_async_remote_copy(
                view(src), view(dst), ssem.at[i], rsem.at[i],
                device_id=peer, device_id_type=MESH,
            )

        def wait_recv(self):
            self.copy().wait_recv()

    class Kept:
        def __init__(self, src, dst):
            self.parts = src, dst, lcount[0]
            lcount[0] += 1

        def copy(self):
            src, dst, i = self.parts
            return pltpu.make_async_copy(view(src), view(dst), lsem.at[i])

        def wait(self):
            self.copy().wait()

    def push(src, dst, peer):
        cp = Sent(src, dst, peer)
        cp.copy().start()
        sent.append(cp)
        return cp

    lcount = [0]

    def local(src, dst):
        cp = Kept(src, dst)
        cp.copy().start()
        return cp

    def rows(j, size=own):
        return pl.ds(pl.multiple_of(j * size, size), size)

    peers = [core_peer, x_peer]
    if fused:
        peers.append(y_peer)
        peers += [z_peer(k) for k in range(1, nz)]
    rows_t, rows_tx = rows(t), rows(tx)
    barrier = pltpu.get_barrier_semaphore()
    for peer in peers:
        pl.semaphore_signal(barrier, inc=1, device_id=peer, device_id_type=MESH)

    half = pl.ds(pl.multiple_of(p * LANES, LANES), LANES)
    other_half = pl.ds(pl.multiple_of((1 - p) * LANES, LANES), LANES)

    if fused:
        own_part = [wqkv_ref[...], wo_ref[...][None], ckv_ref[...], cq_ref[...][None]]
        own_part.append(co_ref[...][None])
        at = 0
        for piece in own_part:
            wg[at : at + piece.shape[0], z, y, :, half] = piece
            at += piece.shape[0]
        for i in range(nf):
            wg[8 + i, z, y, :, half] = up_ref[:, i * LANES : (i + 1) * LANES]
            wg[8 + nf + i, z, y, :, half] = dn_ref[:, i * LANES : (i + 1) * LANES]
        place = (
            lax.broadcasted_iota(jnp.int32, (rb, wide), 0) + dp_at * rb
            == lax.broadcasted_iota(jnp.int32, (rb, wide), 1)
        ).astype(BF16)
        gz[0] = jnp.zeros((16, wide), BF16)
        for i in range(6):
            gz[0, i : i + 1, :] = nn(gain_refs[i][...], place).astype(BF16)
    pl.semaphore_wait(barrier, len(peers))

    relays = {}

    def carry(name, src, buf):
        over = push((src, p_other), (buf, rows_t), x_peer)
        keep = local((src, p), (buf, rows_t))
        near = push((src, p), (buf, rows_t), core_peer)
        yield
        over.wait_recv()
        relays[name] = push((buf, rows_tx), (buf, rows_tx), core_peer)
        keep.wait()
        near.wait_recv()
        yield

    def back_over(src, buf):
        cp = push((src, None), (buf, p), x_peer)
        yield
        cp.wait_recv()
        yield

    tasks = {
        "x": [carry("x", x_ref, xs)],
        "m": [carry("m", m_ref, ms)],
        "c": [carry("c", c_ref, cs)],
        "out": [back_over(osend, outs)],
        "gm": [back_over(gmsend, gms)],
        "gi": [back_over(gisend, gis)],
        "gz": [],
    }

    def at(name):
        for task in PLAN[name]:
            for part in tasks[task]:
                next(part)

    def at_turn(i, turn, name):
        if PLAN[name]:

            @pl.when(i == turn)
            def _():
                at(name)

    def gather(lo, hi, first, last, order):
        r = slice(first, last)
        zi, yi, lanes = z, y, half
        hops = []
        for axis in order:
            for cp in hops:
                cp.wait_recv()
            part = (wg, (slice(lo, hi), zi, yi, r, lanes))
            if axis == "x":
                hops = [push(part, part, x_peer)]
                lanes = pl.ds(0, 2 * LANES)
            elif axis == "y":
                hops = [push(part, part, y_peer)]
                yi = slice(None)
            else:
                hops = [push(part, part, z_peer(k)) for k in range(1, nz)]
                zi = slice(None)
            yield
        for cp in hops:
            cp.wait_recv()
        yield

    def gain_rows():
        cps = [push((gz, 0), (gz, k), z_peer(k)) for k in range(1, nz)]
        yield
        for cp in cps:
            cp.wait_recv()
        total = gz[0].astype(F32)
        for k in range(1, nz):
            total = total + gz[k].astype(F32)
        gy[0] = total.astype(BF16)
        cp = push((gy, 0), (gy, 1), y_peer)
        yield
        cp.wait_recv()
        gains[...] = total + gy[1].astype(F32)
        yield

    for name, (lo, hi) in gather_segments(nf).items():
        size = rb // len(ORDERS[name])
        tasks[name] = [
            gather(lo, hi, i * size, (i + 1) * size, order)
            for i, order in enumerate(ORDERS[name])
            if fused
        ]
    if fused:
        tasks["gz"] = [gain_rows()]

    def weight(s):
        return wg[s].reshape(nz * ny * rb, 2 * LANES)

    if not fused:
        wcp = local((wfull_ref, None), (wg, None))
        gains[...] = gfull_ref[...]
    at("p0")
    relays["x"].wait_recv()
    if not fused:
        wcp.wait()

    sub = min(128, own)
    per = own // sub
    gacc[...] = jnp.zeros_like(gacc)

    def norm_rows(i, _):
        r = rows(i, sub)
        xhat, _unused = normalize(xs[r, :].astype(F32))
        n1[r, :] = (xhat * gains[0:1, :] + gains[1:2, :]).astype(BF16)
        return 0

    lax.fori_loop(0, 4 * per, norm_rows, 0)
    at("p1")

    def put_pairs(buf, r, value):
        v = value.astype(BF16)
        buf[0, r, :] = v[:, :LANES]
        buf[1, r, :] = v[:, LANES:]

    def pairs(buf, r):
        return jnp.concatenate([buf[0, r, :], buf[1, r, :]], axis=1)

    scale = DH ** (-0.5)

    def put_transposed(buf, r, value):
        vt_ = value.T.astype(BF16)
        buf[0, :, r] = vt_[:LANES]
        buf[1, :, r] = vt_[LANES:]

    def project(j, _):
        r = rows(j)
        rowsv = n1[r, :]
        put_pairs(qs, r, nn(rowsv, weight(0)).astype(BF16) * jnp.asarray(scale, BF16))
        put_pairs(ks, r, nn(rowsv, weight(1)))
        val = nn(rowsv, weight(2))
        put_pairs(vs, r, val)
        put_transposed(vt, r, val.astype(BF16).astype(F32))
        return 0

    lax.fori_loop(0, 4, project, 0)
    at("p2")


    lane_at = lax.broadcasted_iota(jnp.int32, (1, LANES), 1)
    head_lanes = [((lane_at // DH) == u).astype(F32).astype(BF16) for u in range(2)]

    def only(value, u):
        return value * head_lanes[u]

    wide_rows = 2 * own

    def qrows(jj):
        return pl.ds(pl.multiple_of(jj * wide_rows, wide_rows), wide_rows)

    def hide(scores, first, diagonal, causal):
        if causal and not diagonal:
            return scores
        if causal:
            key_at = lax.broadcasted_iota(jnp.int32, scores.shape, 0)
            query_at = lax.broadcasted_iota(jnp.int32, scores.shape, 1)
            return jnp.where(key_at <= query_at, scores, MASKED)
        b = bias[first : first + scores.shape[0], :]
        return scores + jnp.concatenate([b] * (wide_rows // LANES), axis=1)

    def attend(pp, q_s, k_s, v_t, mix, lse, r, keys, causal):
        parts_k = [slice(i * wide_rows, (i + 1) * wide_rows) for i in range(keys // wide_rows)]

        q = q_s[pp, r, :]
        tops = [None, None]
        for i, kk in enumerate(parts_k):
            for u in range(2):
                s = nt(only(k_s[pp, kk, :], u), q)
                s = hide(s, kk.start, i == len(parts_k) - 1, causal)
                top = jnp.max(s, axis=0, keepdims=True)
                tops[u] = top if i == 0 else jnp.maximum(tops[u], top)
                score[u, kk, :] = s
        totals, mixed = [None, None], [None, None]
        for i, kk in enumerate(parts_k):
            for u in range(2):
                e = jnp.exp(score[u, kk, :] - tops[u])
                total = jnp.sum(e, axis=0, keepdims=True)
                o = nn(v_t[pp, u * DH : (u + 1) * DH, kk], e.astype(BF16))
                totals[u] = total if i == 0 else totals[u] + total
                mixed[u] = o if i == 0 else mixed[u] + o
        for u in range(2):
            lse[2 * pp + u, :, r] = tops[u] + jnp.log(totals[u])
            mixed[u] = mixed[u] * (1.0 / totals[u])
        mix[pp, r, :] = jnp.concatenate(mixed, axis=0).T.astype(BF16)

    def exchange(point, j):
        b = point % 2
        i = point * 4 + j
        return pltpu.make_async_remote_copy(
            ps.at[b, rows(j)], pr.at[b, rows(j)], xss.at[i], xrs.at[i],
            device_id=core_peer, device_id_type=MESH,
        )

    def send_sum(point, j, value):
        ps[point % 2, rows(j), :] = value.astype(BF16)
        exchange(point, j).start()

    def summed(point, r):
        b = point % 2
        return ps[b, r, :].astype(F32) + pr[b, r, :].astype(F32)

    for jj in range(2):
        first = 3 + 3 * jj

        def self_pair(pp, _, jj=jj, first=first):
            attend(pp, qs, ks, vt, smix, slse, qrows(jj), wide_rows * (jj + 1), True)
            at_turn(pp, 0, f"p{first}")
            at_turn(pp, 1, f"p{first + 1}")
            return 0

        lax.fori_loop(0, 2, self_pair, 0)
        for j in (2 * jj, 2 * jj + 1):
            send_sum(0, j, nt(pairs(smix, rows(j)), weight(3)))
        at(f"p{first + 2}")
    relays["m"].wait_recv()

    key_at = lax.broadcasted_iota(jnp.int32, (rows_all, LANES), 0)
    bias[...] = jnp.where(key_at < sl_ref[p], 0.0, MASKED)

    def project_cross(j, _):
        r = rows(j)
        rowsv = ms[r, :]
        put_pairs(cks, r, nn(rowsv, weight(4)))
        val = nn(rowsv, weight(5))
        put_pairs(cvs, r, val)
        put_transposed(vt, r, val.astype(BF16).astype(F32))
        return 0

    lax.fori_loop(0, 4, project_cross, 0)
    at("p9")

    def second(j, _):
        exchange(0, j).wait_recv()
        exchange(0, j).wait_send()

        def part(i, _):
            r = rows(j * per + i, sub)
            h = xs[r, :].astype(F32) + summed(0, r)
            h1[r, :] = h
            xhat, _unused = normalize(h)
            n2[r, :] = (xhat * gains[2:3, :] + gains[3:4, :]).astype(BF16)
            return 0

        lax.fori_loop(0, per, part, 0)
        r = rows(j)
        put_pairs(cqs, r, nn(n2[r, :], weight(6)).astype(BF16) * jnp.asarray(scale, BF16))
        return 0

    lax.fori_loop(0, 4, second, 0)
    at("p10")

    def cross_pair(i, _):
        jj, pp = i // 2, i % 2
        attend(pp, cqs, cks, vt, cmix, clse, qrows(jj), rows_all, False)
        for k, name in enumerate(("p11", "p12", "p14", "p15")):
            at_turn(i, k, name)

        @pl.when(pp == 1)
        def _():
            for k in range(2):
                j = 2 * jj + k
                send_sum(1, j, nt(pairs(cmix, rows(j)), weight(7)))

        at_turn(i, 1, "p13")
        return 0

    lax.fori_loop(0, 4, cross_pair, 0)
    at("p16")

    limit = tl_ref[p]

    def live(r_first, size):
        at = lax.broadcasted_iota(jnp.int32, (size, wide), 0) + r_first
        return at < limit

    def weight_grads(a_buf, items):
        chunk = ny * rb
        for zi in range(nz):
            at = a_buf[:, zi * chunk : (zi + 1) * chunk].T
            for s, load in items:
                gs[s, zi] = nn(at, load()).astype(BF16).reshape(ny, rb, 2 * LANES)

    every = pl.ds(0, rows_all)

    def whole(buf):
        return lambda: pairs(buf, every)

    def plane(buf, s):
        return lambda: buf[s]

    def reduce_part(lo, hi, first, last, order, bufs):
        r = slice(first, last)
        base = lo
        bufs = list(bufs)
        gone = []

        def at(buf, s, zsel, ysel, lsel):
            index = [s]
            if "z" not in gone:
                index.append(zsel)
            if "y" not in gone:
                index.append(ysel)
            index += [slice(None) if buf is not gs else r, lsel]
            return tuple(index)

        every_one = slice(None)
        cur, shift = gs, 0
        for hop, axis in enumerate(order):
            span = slice(lo - shift, hi - shift)
            land = bufs.pop(0)
            to = slice(lo - base, hi - base)
            lanes = every_one if "x" in gone else slice(0, 2 * LANES)
            pick = {"z": every_one, "y": every_one, "x": lanes}
            here = dict(pick)
            if axis == "x":
                pick["x"], here["x"] = other_half, half
                sends = [(pick, (land, to), x_peer)]
            elif axis == "y":
                pick["y"], here["y"] = y_other, y
                sends = [(pick, (land, to), y_peer)]
            else:
                here["z"] = z
                sends = [
                    (dict(pick, z=z_others[k - 1]), (land, (k - 1, to)), z_peer(k))
                    for k in range(1, nz)
                ]
            cps = [
                push((cur, at(cur, span, sel["z"], sel["y"], sel["x"])), dst, peer)
                for sel, dst, peer in sends
            ]
            yield
            for cp in cps:
                cp.wait_recv()
            done = hop == 2
            acc = None if done else bufs.pop(0)

            def add(s, _):
                v = cur[at(cur, s - shift, here["z"], here["y"], here["x"])].astype(F32)
                if axis == "z":
                    for k in range(1, nz):
                        v = v + land[k - 1, s - base].astype(F32)
                else:
                    v = v + land[s - base].astype(F32)
                if done:
                    gw_ref[s, r] = v
                else:
                    acc[s - base] = v.astype(BF16)
                return 0

            lax.fori_loop(lo, hi, add, 0)
            gone.append(axis)
            cur, shift = acc, base
        yield

    for name, (lo, hi) in sum_segments(nf).items():
        size = rb // len(ORDERS[name])
        tasks[name] = [
            reduce_part(lo, hi, i * size, (i + 1) * size, order, sums[name][i])
            for i, order in enumerate(ORDERS[name])
            if fused
        ]

    def third(j, _):
        exchange(1, j).wait_recv()
        exchange(1, j).wait_send()

        def part(i, _):
            r = rows(j * per + i, sub)
            h = h1[r, :] + summed(1, r)
            h2[r, :] = h
            xhat, _unused = normalize(h)
            n3[r, :] = (xhat * gains[4:5, :] + gains[5:6, :]).astype(BF16)
            return 0

        lax.fori_loop(0, per, part, 0)
        r = rows(j)
        rowsv = n3[r, :]
        for s in range(nf):
            active, slope = gelu_both(nn(rowsv, weight(8 + s)))
            act[s, r, :] = active.astype(BF16)
            gbf[s, r, :] = slope.astype(BF16)
        at_turn(j, 1, "p17")
        return 0

    lax.fori_loop(0, 4, third, 0)
    at("p18")
    relays["c"].wait_recv()

    def live_rows(i, _):
        r = rows(i, sub)
        cot = cs[r, :]
        gb16[r, :] = jnp.where(live(i * sub, sub), cot, jnp.zeros_like(cot))
        return 0

    lax.fori_loop(0, 4 * per, live_rows, 0)
    weight_grads(gb16, [(9 + nf + s, plane(act, s)) for s in range(nf)])
    at("p19")

    def third_back(j, _):
        r = rows(j)
        cot = gb16[r, :]
        for s in range(nf):
            slope = gbf[s, r, :].astype(F32)
            gbf[s, r, :] = (nn(cot, weight(8 + nf + s)) * slope).astype(BF16)
        back = nt(gbf[0, r, :], weight(8))
        for s in range(1, nf):
            back = back + nt(gbf[s, r, :], weight(8 + s))
        send_sum(2, j, back)
        val = nt(act[0, r, :], weight(8 + nf))
        for s in range(1, nf):
            val = val + nt(act[s, r, :], weight(8 + nf + s))
        ys[r, :] = val.astype(BF16)
        at_turn(j, 1, "p20")
        return 0

    lax.fori_loop(0, 4, third_back, 0)

    ycp = [
        push((ys, rows(2 * k + 1 - c)), (yr, k), core_peer) for k in range(2)
    ]

    weight_grads(n3, [(9 + s, plane(gbf, s)) for s in range(nf)])
    at("p21")

    def finish_rows(k, dst):
        def part(i, _):
            r = rows((2 * k + c) * per + i, sub)
            q = rows(i, sub)
            val = h2[r, :] + ys[r, :].astype(F32) + yr[k, q, :].astype(F32)
            keep = live(((2 * k + c) * per + i) * sub, sub)
            dst[q, :] = jnp.where(keep, val, 0.0).astype(BF16)
            return 0
        lax.fori_loop(0, per, part, 0)

    for cp in ycp:
        cp.wait_recv()
    finish_rows(1 - p, osend)
    finish_rows(p, outs.at[p])
    at("p22")

    def back_three(j, _):
        exchange(2, j).wait_recv()
        exchange(2, j).wait_send()

        def part(i, _):
            r = rows(j * per + i, sub)
            dx, dgain, dbias = norm_grad(h2[r, :], summed(2, r), gains[4:5, :])
            gacc[4:5, :] += dgain
            gacc[5:6, :] += dbias
            g = gb16[r, :].astype(F32) + dx
            gh[r, :] = g
            gb16[r, :] = g.astype(BF16)
            return 0

        return lax.fori_loop(0, per, part, 0)

    lax.fori_loop(0, 4, back_three, 0)
    weight_grads(gb16, [(7, whole(cmix))])
    at("p23")


    sel_row = lax.broadcasted_iota(jnp.int32, (8, LANES), 0)
    sel_lane = lax.broadcasted_iota(jnp.int32, (8, LANES), 1)
    selector = (sel_lane // DH == sel_row).astype(F32)

    def pair_lanes(pp):
        return pl.ds(pl.multiple_of(pp * LANES, LANES), LANES)

    def attend_back(pp, q_s, k_s, kt, v_s, mix, lse, r, keys, causal):
        parts_k = [slice(0, keys)]
        if causal and keys > wide_rows:
            parts_k = [slice(0, keys - wide_rows), slice(keys - wide_rows, keys)]

        q = q_s[pp, r, :]
        do = dm[pp, r, :]
        prod = do.astype(F32) * mix[pp, r, :].astype(F32)
        delta = lax.dot_general(
            selector, prod, (((1,), (1,)), ((), ())),
            precision=HIGHEST, preferred_element_type=F32,
        )
        back = None
        for i, kk in enumerate(parts_k):
            parts = []
            for u in range(2):
                s = nt(only(k_s[pp, kk, :], u), q)
                s = hide(s, kk.start, i == len(parts_k) - 1, causal)
                e = jnp.exp(s - lse[2 * pp + u, :, r])
                d = nt(only(v_s[pp, kk, :], u), do)
                ds = (e * (d - delta[u : u + 1])).astype(BF16)
                dv_u = nn(e.astype(BF16), only(do, u))
                dk_u = nn(ds, only(q, u))
                dvp = dv_u if u == 0 else dvp + dv_u
                dkp = dk_u if u == 0 else dkp + dk_u
                parts.append(nn(kt[pp, u * DH : (u + 1) * DH, kk], ds))
            lanes = pair_lanes(pp)
            score[0, kk, lanes] += dkp
            score[1, kk, lanes] += dvp
            parts = jnp.concatenate(parts, axis=0)
            back = parts if i == 0 else back + parts
        dq[pp, r, :] = (back * scale).T.astype(BF16)

    def transpose_keys(buf):
        def one(j, _):
            r = rows(j)
            for pp in range(2):
                vt[pp, :, r] = buf[pp, r, :].astype(F32).T.astype(BF16)
            return 0
        lax.fori_loop(0, 4, one, 0)

    transpose_keys(cks)
    score[:, :, : 2 * LANES] = jnp.zeros((2, rows_all, 2 * LANES), F32)

    def cross_back_pair(i, _):
        jj, pp = i // 2, i % 2

        @pl.when(pp == 0)
        def _():
            for k in range(2):
                r = rows(2 * jj + k)
                put_pairs(dm, r, nn(gb16[r, :], weight(7)))

        attend_back(pp, cqs, cks, vt, cvs, cmix, clse, qrows(jj), rows_all, False)
        for k in range(4):
            at_turn(i, k, f"p{24 + k}")

        @pl.when(pp == 1)
        def _():
            for k in range(2):
                j = 2 * jj + k
                send_sum(3, j, nt(pairs(dq, rows(j)), weight(6)))

        return 0

    lax.fori_loop(0, 4, cross_back_pair, 0)

    def cross_back_keys(j, _):
        r = rows(j)
        for pp in range(2):
            dk[pp, r, :] = score[0, r, pair_lanes(pp)].astype(BF16)
            dv[pp, r, :] = score[1, r, pair_lanes(pp)].astype(BF16)
        val = nt(pairs(dk, r), weight(4)) + nt(pairs(dv, r), weight(5))
        us[r, :] = val.astype(BF16)
        return 0

    lax.fori_loop(0, 4, cross_back_keys, 0)
    ucp = [
        push((us, rows(2 * k + 1 - c)), (ur, k), core_peer) for k in range(2)
    ]
    weight_grads(n2, [(6, whole(dq))])
    weight_grads(ms, [(4, whole(dk)), (5, whole(dv))])
    at("p28")

    def memory_rows(k, dst):
        def part(i, _):
            r = rows((2 * k + c) * per + i, sub)
            q = rows(i, sub)
            dst[q, :] = (us[r, :].astype(F32) + ur[k, q, :].astype(F32)).astype(BF16)
            return 0
        lax.fori_loop(0, per, part, 0)

    for cp in ucp:
        cp.wait_recv()
    memory_rows(1 - p, gmsend)
    memory_rows(p, gms.at[p])
    at("p29")

    def back_two(j, _):
        exchange(3, j).wait_recv()
        exchange(3, j).wait_send()

        def part(i, _):
            r = rows(j * per + i, sub)
            dx, dgain, dbias = norm_grad(h1[r, :], summed(3, r), gains[2:3, :])
            gacc[2:3, :] += dgain
            gacc[3:4, :] += dbias
            g = gh[r, :] + dx
            gh[r, :] = g
            gb16[r, :] = g.astype(BF16)
            return 0

        return lax.fori_loop(0, per, part, 0)

    lax.fori_loop(0, 4, back_two, 0)
    weight_grads(gb16, [(3, whole(smix))])
    at("p30")

    transpose_keys(ks)
    score[:, :, : 2 * LANES] = jnp.zeros((2, rows_all, 2 * LANES), F32)
    for jj in (1, 0):
        for j in (2 * jj, 2 * jj + 1):
            put_pairs(dm, rows(j), nn(gb16[rows(j), :], weight(3)))
        first = 33 - 2 * jj

        def self_back_pair(pp, _, jj=jj, first=first):
            attend_back(pp, qs, ks, vt, vs, smix, slse, qrows(jj), wide_rows * (jj + 1), True)
            at_turn(pp, 0, f"p{first}")
            at_turn(pp, 1, f"p{first + 1}")
            return 0

        lax.fori_loop(0, 2, self_back_pair, 0)
        for j in (2 * jj, 2 * jj + 1):
            r = rows(j)
            for pp in range(2):
                dk[pp, r, :] = score[0, r, pair_lanes(pp)].astype(BF16)
                dv[pp, r, :] = score[1, r, pair_lanes(pp)].astype(BF16)
            val = nt(pairs(dq, r), weight(0)) + nt(pairs(dk, r), weight(1))
            send_sum(4, j, val + nt(pairs(dv, r), weight(2)))

    weight_grads(n1, [(0, whole(dq)), (1, whole(dk)), (2, whole(dv))])
    at("p35")

    def back_one(k, j, dst):
        exchange(4, j).wait_recv()

        def part(i, _):
            r = rows(j * per + i, sub)
            q = rows(i, sub)
            dx, dgain, dbias = norm_grad(xs[r, :].astype(F32), summed(4, r), gains[0:1, :])
            gacc[0:1, :] += dgain
            gacc[1:2, :] += dbias
            if dst is not None:
                dst[q, :] = (gh[r, :] + dx).astype(BF16)
            return 0

        lax.fori_loop(0, per, part, 0)

    back_one(0, tx, gisend)
    at("p36")
    back_one(0, t, gis.at[p])
    back_one(0, 2 * p + 1 - c, None)
    back_one(0, 2 * (1 - p) + 1 - c, None)
    for j in range(4):
        exchange(4, j).wait_send()

    spread_rows = jnp.concatenate(
        [gacc[...], jnp.zeros((LANES - 8, wide), F32)], axis=0
    )
    columns = spread_rows.T.astype(BF16)
    gs[gseg] = jnp.concatenate([columns, columns], axis=1).reshape(nz, ny, rb, 2 * LANES)

    at("p37")
    last = [] if fused else [local((gs, None), (gw_ref, None))]

    finals = [
        local((outs, None), (out_ref, None)),
        local((gms, None), (gm_ref, None)),
        local((gis, None), (gi_ref, None)),
    ]
    for cp in finals + last:
        cp.wait()
    for cp in sent:
        cp.copy().wait_send()


def unpack_kernel(nf, o_ref, gi_ref, gm_ref, gw_ref, *outs):
    outs[0][...] = o_ref[...]
    outs[1][...] = gi_ref[...].astype(F32)
    outs[2][...] = gm_ref[...].astype(F32)
    outs[3][...] = gw_ref[0:3]
    outs[4][...] = gw_ref[3]
    outs[5][...] = gw_ref[6]
    outs[6][...] = gw_ref[4:6]
    outs[7][...] = gw_ref[7]
    for i in range(nf):
        outs[8][:, i * LANES : (i + 1) * LANES] = gw_ref[9 + i]
        outs[9][:, i * LANES : (i + 1) * LANES] = gw_ref[9 + nf + i]
    vectors = gw_ref[8].T
    for i in range(6):
        outs[10 + i][...] = vectors[i : i + 1]


def body(ndp, inputs, memory, tgt_len, src_len, cotangent, w_qkv, w_out, cross_query, cross_kv,
         cross_out, ffn_up, ffn_down, *gain_list):
    own, wide = inputs.shape[1], inputs.shape[2]
    rb = w_qkv.shape[1]
    nf = ffn_up.shape[1] // LANES
    nseg = 8 + 2 * nf
    rows_all = 4 * own
    fused = rb % 32 == 0 and ndp % 2 == 0
    if fused:
        ny, nz, block = 2, ndp // 2, rb
    else:
        ny, nz, block = 1, 1, wide
    cfg = (fused, nz, ny, block, own, wide, nf)

    any_spec = pl.BlockSpec(memory_space=pl.ANY)
    smem = pl.BlockSpec(memory_space=pltpu.SMEM)
    vmem = pl.BlockSpec(memory_space=pltpu.VMEM)
    operands = [inputs, memory, cotangent, tgt_len, src_len]
    specs = [any_spec] * 3 + [smem] * 2
    if fused:
        weights = [w_qkv, w_out.T, cross_query, cross_kv, cross_out.T, ffn_up, ffn_down.T]
        weights += [g[None, :] for g in gain_list]
        operands += weights
        specs += [vmem] * len(weights)
    else:
        pieces = [w_qkv, w_out.T[None], cross_kv, cross_query[None], cross_out.T[None]]
        pieces += [ffn_up.reshape(rb, nf, LANES).swapaxes(0, 1)]
        pieces += [ffn_down.reshape(nf, LANES, rb).swapaxes(1, 2)]
        packed = lax.all_gather(jnp.concatenate(pieces, axis=0), "dp", axis=1, tiled=True)
        index = lax.axis_index("tensor")
        flipped = lax.ppermute(packed, "tensor", [(i, (i + 2) % 4) for i in range(4)])
        low = jnp.where(index < 2, packed, flipped)
        high = jnp.where(index < 2, flipped, packed)
        full = jnp.concatenate([low, high], axis=2)[:, None, None]
        gathered = lax.all_gather(jnp.stack(gain_list), "dp", axis=1, tiled=True)
        operands += [full, jnp.pad(gathered.astype(F32), ((0, 10), (0, 0)))]
        specs += [any_spec, vmem]

    bf = lambda *shape: pltpu.VMEM(shape, BF16)
    fl = lambda *shape: pltpu.VMEM(shape, F32)
    seq = (rows_all, wide)
    heads = (2, rows_all, LANES)
    scratch = [
        bf(*seq), bf(*seq), bf(*seq), bf(nseg, nz, ny, block, 2 * LANES), fl(16, wide),
        bf(*seq), bf(*seq), bf(*seq), fl(*seq), fl(*seq), fl(*seq), bf(*seq),
        bf(*heads), bf(*heads), bf(*heads), bf(*heads), bf(*heads), bf(*heads),
        bf(2, LANES, rows_all), bf(*heads), bf(*heads), fl(4, 1, rows_all), fl(4, 1, rows_all),
        bf(nf, rows_all, 2 * LANES), bf(nf, rows_all, 2 * LANES),
        bf(*heads), bf(*heads), bf(*heads), bf(*heads),
        bf(2, *seq), bf(2, *seq), bf(*seq), bf(2, own, wide), bf(*seq), bf(2, own, wide),
        bf(2, own, wide), bf(own, wide), bf(2, own, wide), bf(own, wide),
        bf(2, own, wide), bf(own, wide),
        bf(nseg + 1, nz, ny, block, 2 * LANES), fl(rows_all, LANES), fl(8, wide),
        fl(2, rows_all, 2 * own),
    ]
    if fused:
        scratch += [bf(nz, 16, wide), bf(2, 16, wide)]
        for name, (lo, hi) in sum_segments(nf).items():
            for order in ORDERS[name]:
                shapes = sum_shapes(order, hi - lo, nz, ny, block // len(ORDERS[name]))
                scratch += [bf(*shape) for shape in shapes]
    dma = pltpu.SemaphoreType.DMA
    scratch += [dma((250,)), dma((250,)), dma((20,)), dma((20,)), dma((12,))]

    if fused:
        grads_shape = jax.ShapeDtypeStruct((nseg + 1, block, LANES), F32)
        grads_spec = vmem
    else:
        grads_shape = jax.ShapeDtypeStruct((nseg + 1, nz, ny, block, 2 * LANES), BF16)
        grads_spec = any_spec
    act_shape = jax.ShapeDtypeStruct(inputs.shape, BF16)
    output, grad_in, grad_mem, grads = pl.pallas_call(
        functools.partial(layer_kernel, cfg),
        out_shape=(act_shape, act_shape, act_shape, grads_shape),
        in_specs=specs,
        out_specs=(any_spec, any_spec, any_spec, grads_spec),
        scratch_shapes=scratch,
        compiler_params=pltpu.CompilerParams(
            collective_id=0, has_side_effects=True, vmem_limit_bytes=62 << 20
        ),
        name="layer",
    )(*operands)

    if not fused:
        mine = grads[:, 0, 0].astype(F32)
        index = lax.axis_index("tensor")
        low, high = mine[:, :, :LANES], mine[:, :, LANES:]
        keep = jnp.where(index < 2, low, high)
        give = jnp.where(index < 2, high, low)
        keep = keep + lax.ppermute(give, "tensor", [(i, (i + 2) % 4) for i in range(4)])
        grads = lax.psum_scatter(keep, "dp", scatter_dimension=1, tiled=True)

    shapes = [
        (inputs.shape, BF16), (inputs.shape, F32), (memory.shape, F32),
        (w_qkv.shape, F32), (w_out.shape[::-1], F32), (cross_query.shape, F32),
        (cross_kv.shape, F32), (cross_out.shape[::-1], F32), (ffn_up.shape, F32),
        (ffn_down.shape[::-1], F32),
    ] + [((1, rb), F32)] * 6
    got = pl.pallas_call(
        functools.partial(unpack_kernel, nf),
        out_shape=[jax.ShapeDtypeStruct(*s) for s in shapes],
        in_specs=[vmem] * 4,
        out_specs=[vmem] * len(shapes),
        name="unpack",
    )(output, grad_in, grad_mem, grads)
    return (
        *got[:4], got[4].T, got[5], got[6], got[7].T, got[8], got[9].T,
        *[g[0] for g in got[10:]],
    )


def solution(mesh):
    return jax.shard_map(
        functools.partial(body, mesh.shape["dp"]),
        mesh=mesh,
        in_specs=(
            P("dp", "tensor", None),
            P("dp", "tensor", None),
            P("dp"),
            P("dp"),
            P("dp", "tensor", None),
            P(None, "dp", "tensor"),
            P("tensor", "dp"),
            P("dp", "tensor"),
            P(None, "dp", "tensor"),
            P("tensor", "dp"),
            P("dp", "tensor"),
            P("tensor", "dp"),
            P("dp"),
            P("dp"),
            P("dp"),
            P("dp"),
            P("dp"),
            P("dp"),
        ),
        out_specs=(
            P("dp", "tensor", None),
            P("dp", "tensor", None),
            P("dp", "tensor", None),
            P(None, "dp", "tensor"),
            P("tensor", "dp"),
            P("dp", "tensor"),
            P(None, "dp", "tensor"),
            P("tensor", "dp"),
            P("dp", "tensor"),
            P("tensor", "dp"),
            P("dp"),
            P("dp"),
            P("dp"),
            P("dp"),
            P("dp"),
            P("dp"),
        ),
        check_vma=False,
    )
```

```python
import functools

import jax
import jax.numpy as jnp
from jax import lax
from jax.experimental import pallas as pl
from jax.experimental.pallas import tpu as pltpu
from jax.sharding import PartitionSpec as P

DH = 64
LANES = 128
EPSILON = 1e-05
MASKED = -1e30
F32 = jnp.float32
BF16 = jnp.bfloat16
MESH = pl.DeviceIdType.MESH
HIGHEST = lax.Precision.HIGHEST


def nn(a, b):
    return lax.dot_general(a, b, (((1,), (0,)), ((), ())), preferred_element_type=F32)


def nt(a, b):
    return lax.dot_general(a, b, (((1,), (1,)), ((), ())), preferred_element_type=F32)


def normalize(values):
    center = values - jnp.mean(values, axis=-1, keepdims=True)
    spread = jnp.mean(center * center, axis=-1, keepdims=True)
    inv = lax.rsqrt(spread + EPSILON)
    return center * inv, inv


def norm_grad(values, grad, gain):
    xhat, inv = normalize(values)
    e = grad * gain
    back = inv * (
        e
        - jnp.mean(e, axis=-1, keepdims=True)
        - xhat * jnp.mean(e * xhat, axis=-1, keepdims=True)
    )
    return (
        back,
        jnp.sum(grad * xhat, axis=0, keepdims=True),
        jnp.sum(grad, axis=0, keepdims=True),
    )


def gelu_both(v):
    c = 0.7978845608028654
    v2 = v * v
    t = jnp.tanh(v * (c + (c * 0.044715) * v2))
    half = 0.5 * (1.0 + t)
    slope = half + (0.5 * v) * (1.0 - t * t) * (c + (3.0 * c * 0.044715) * v2)
    return v * half, slope


ORDERS = {
    "A0": ("xzy",),
    "A1": ("yzx",),
    "A2": ("zyx",),
    "W": ("zxy", "zyx"),
    "K": ("zxy", "zyx"),
    "Q0": ("zxy", "zyx"),
    "Q1": ("zxy", "zyx"),
    "U0": ("yxz",),
    "U1": ("zxy",),
    "D0": ("zxy",),
    "D1": ("zyx",),
    "rD0": ("zxy",),
    "rD1": ("zxy",),
    "rU0": ("xzy",),
    "rU1": ("yxz",),
    "rco": ("yzx",),
    "rcq": ("xzy",),
    "rck": ("zxy",),
    "rwo": ("zxy",),
    "rT": ("xyz", "yzx"),
    "rG": ("yzx",),
}

PLAN = {
    "p0": ("A2", "x", "W", "A1", "gz", "A1", "A2", "A0", "W", "gz", "x", "A0", "A2", "A1", "gz"),
    "p1": ("K", "m", "U0", "A2", "A0", "Q0", "A1", "Q1", "U1", "K", "W", "D0", "A0"),
    "p2": ("Q0", "m", "Q1", "U0", "D1"),
    "p3": ("K",),
    "p4": ("W",),
    "p5": (),
    "p6": ("Q0", "Q1", "U0"),
    "p7": ("U1",),
    "p8": ("K", "D1"),
    "p9": ("Q0", "D0"),
    "p10": ("Q1",),
    "p11": ("U1", "c"),
    "p12": (),
    "p13": (),
    "p14": ("D0", "D1"),
    "p15": ("U0",),
    "p16": ("U1",),
    "p17": ("c",),
    "p18": (),
    "p19": ("rD1", "D0", "D1"),
    "p20": (),
    "p21": ("rU0", "rU1"),
    "p22": ("rD0",),
    "p23": ("out", "rco"),
    "p24": (),
    "p25": ("rD1", "rU1"),
    "p26": ("rD1", "out", "rU0"),
    "p27": ("rD1", "rD0", "rU1"),
    "p28": ("rcq", "rck"),
    "p29": ("rD0", "gm"),
    "p30": ("rU0",),
    "p31": ("rU0", "rD0", "rU1"),
    "p32": ("gm", "rwo"),
    "p33": (),
    "p34": (),
    "p35": ("rT", "rcq"),
    "p36": ("rco",),
    "p37": ("rG", "rwo", "gi", "rck", "rT", "rcq", "rwo", "rco", "rG", "rcq", "rwo", "gi", "rT", "rck", "rco", "rG", "rck", "rG", "rT"),
}


def gather_segments(nf):
    mid = 8 + nf // 2
    end = 8 + nf
    last = end + nf // 2
    return {
        "A0": (0, 1), "A1": (1, 2), "A2": (2, 3), "W": (3, 4), "K": (4, 6), "Q0": (6, 7),
        "Q1": (7, 8), "U0": (8, mid), "U1": (mid, end), "D0": (end, last),
        "D1": (last, end + nf),
    }


def sum_segments(nf):
    mid = 9 + nf // 2
    end = 9 + nf
    last = end + nf // 2
    return {
        "rT": (0, 3), "rwo": (3, 4), "rck": (4, 6), "rcq": (6, 7), "rco": (7, 8), "rG": (8, 9),
        "rU0": (9, mid), "rU1": (mid, end), "rD0": (end, last), "rD1": (last, end + nf),
    }


def sum_shapes(order, segs, nz, ny, rows):
    shapes, left = [], {"x": 2 * LANES, "y": (ny,), "z": (nz,)}
    for i, axis in enumerate(order):
        left[axis] = LANES if axis == "x" else ()
        shape = (segs, *left["z"], *left["y"], rows, left["x"])
        shapes.append((nz - 1, *shape) if axis == "z" else shape)
        if i < 2:
            shapes.append(shape)
    return shapes


def layer_kernel(cfg, *refs):
    fused, nz, ny, rb, own, wide, nf = cfg
    rows_all = 4 * own
    nseg = 8 + 2 * nf
    gseg = 8
    refs = list(refs)

    def take(count):
        got, refs[:count] = refs[:count], []
        return got

    x_ref, m_ref, c_ref, tl_ref, sl_ref = take(5)
    if fused:
        wqkv_ref, wo_ref, cq_ref, ckv_ref, co_ref, up_ref, dn_ref = take(7)
        gain_refs = take(6)
    else:
        wfull_ref, gfull_ref = take(2)
    out_ref, gi_ref, gm_ref, gw_ref = take(4)
    (xs, ms, cs, wg, gains, n1, n2, n3, h1, h2, gh, gb16, qs, ks, vs, cqs, cks, cvs,
     vt, smix, cmix, slse, clse, act, gbf, dm, dq, dk, dv, ps, pr, ys, yr,
     us, ur, outs, osend, gis, gisend, gms, gmsend, gs, bias, gacc, score) = take(45)
    if fused:
        gz, gy = take(2)
        sums = {name: [take(5) for _ in ORDERS[name]] for name in sum_segments(nf)}
    ssem, rsem, xss, xrs, lsem = take(5)

    p = lax.axis_index("tensor") // 2
    c = lax.axis_index("tensor") % 2
    t = 2 * p + c
    tx = 2 * (1 - p) + c
    dp_at = lax.axis_index("dp")
    core_peer = {"dp": dp_at, "tensor": 2 * p + 1 - c}
    x_peer = {"dp": dp_at, "tensor": tx}
    z = dp_at // ny
    y = dp_at % ny
    y_peer = {"dp": z * ny + (1 - y), "tensor": t}

    y_other, p_other = 1 - y, 1 - p
    z_others = [(z + k) % nz for k in range(1, nz)]
    z_peers = [{"dp": at_z * ny + y, "tensor": t} for at_z in z_others]

    def z_peer(k):
        return z_peers[k - 1]

    counter = [0]
    sent = []

    def view(pair):
        ref, index = pair
        return ref if index is None else ref.at[index]

    class Sent:
        def __init__(self, src, dst, peer):
            self.parts = src, dst, peer, counter[0]
            counter[0] += 1

        def copy(self):
            src, dst, peer, i = self.parts
            return pltpu.make_async_remote_copy(
                view(src), view(dst), ssem.at[i], rsem.at[i],
                device_id=peer, device_id_type=MESH,
            )

        def wait_recv(self):
            self.copy().wait_recv()

    class Kept:
        def __init__(self, src, dst):
            self.parts = src, dst, lcount[0]
            lcount[0] += 1

        def copy(self):
            src, dst, i = self.parts
            return pltpu.make_async_copy(view(src), view(dst), lsem.at[i])

        def wait(self):
            self.copy().wait()

    def push(src, dst, peer):
        cp = Sent(src, dst, peer)
        cp.copy().start()
        sent.append(cp)
        return cp

    lcount = [0]

    def local(src, dst):
        cp = Kept(src, dst)
        cp.copy().start()
        return cp

    def rows(j, size=own):
        return pl.ds(pl.multiple_of(j * size, size), size)

    peers = [core_peer, x_peer]
    if fused:
        peers.append(y_peer)
        peers += [z_peer(k) for k in range(1, nz)]
    rows_t, rows_tx = rows(t), rows(tx)
    barrier = pltpu.get_barrier_semaphore()
    for peer in peers:
        pl.semaphore_signal(barrier, inc=1, device_id=peer, device_id_type=MESH)

    half = pl.ds(pl.multiple_of(p * LANES, LANES), LANES)
    other_half = pl.ds(pl.multiple_of((1 - p) * LANES, LANES), LANES)

    if fused:
        own_part = [wqkv_ref[...], wo_ref[...][None], ckv_ref[...], cq_ref[...][None]]
        own_part.append(co_ref[...][None])
        at = 0
        for piece in own_part:
            wg[at : at + piece.shape[0], z, y, :, half] = piece
            at += piece.shape[0]
        for i in range(nf):
            wg[8 + i, z, y, :, half] = up_ref[:, i * LANES : (i + 1) * LANES]
            wg[8 + nf + i, z, y, :, half] = dn_ref[:, i * LANES : (i + 1) * LANES]
        place = (
            lax.broadcasted_iota(jnp.int32, (rb, wide), 0) + dp_at * rb
            == lax.broadcasted_iota(jnp.int32, (rb, wide), 1)
        ).astype(BF16)
        gz[0] = jnp.zeros((16, wide), BF16)
        for i in range(6):
            gz[0, i : i + 1, :] = nn(gain_refs[i][...], place).astype(BF16)
    pl.semaphore_wait(barrier, len(peers))

    relays = {}

    def carry(name, src, buf):
        over = push((src, p_other), (buf, rows_t), x_peer)
        keep = local((src, p), (buf, rows_t))
        near = push((src, p), (buf, rows_t), core_peer)
        yield
        over.wait_recv()
        relays[name] = push((buf, rows_tx), (buf, rows_tx), core_peer)
        keep.wait()
        near.wait_recv()
        yield

    def back_over(src, buf):
        cp = push((src, None), (buf, p), x_peer)
        yield
        cp.wait_recv()
        yield

    tasks = {
        "x": [carry("x", x_ref, xs)],
        "m": [carry("m", m_ref, ms)],
        "c": [carry("c", c_ref, cs)],
        "out": [back_over(osend, outs)],
        "gm": [back_over(gmsend, gms)],
        "gi": [back_over(gisend, gis)],
        "gz": [],
    }

    def at(name):
        for task in PLAN[name]:
            for part in tasks[task]:
                next(part)

    def at_turn(i, turn, name):
        if PLAN[name]:

            @pl.when(i == turn)
            def _():
                at(name)

    def gather(lo, hi, first, last, order):
        r = slice(first, last)
        zi, yi, lanes = z, y, half
        hops = []
        for axis in order:
            for cp in hops:
                cp.wait_recv()
            part = (wg, (slice(lo, hi), zi, yi, r, lanes))
            if axis == "x":
                hops = [push(part, part, x_peer)]
                lanes = pl.ds(0, 2 * LANES)
            elif axis == "y":
                hops = [push(part, part, y_peer)]
                yi = slice(None)
            else:
                hops = [push(part, part, z_peer(k)) for k in range(1, nz)]
                zi = slice(None)
            yield
        for cp in hops:
            cp.wait_recv()
        yield

    def gain_rows():
        cps = [push((gz, 0), (gz, k), z_peer(k)) for k in range(1, nz)]
        yield
        for cp in cps:
            cp.wait_recv()
        total = gz[0].astype(F32)
        for k in range(1, nz):
            total = total + gz[k].astype(F32)
        gy[0] = total.astype(BF16)
        cp = push((gy, 0), (gy, 1), y_peer)
        yield
        cp.wait_recv()
        gains[...] = total + gy[1].astype(F32)
        yield

    for name, (lo, hi) in gather_segments(nf).items():
        size = rb // len(ORDERS[name])
        tasks[name] = [
            gather(lo, hi, i * size, (i + 1) * size, order)
            for i, order in enumerate(ORDERS[name])
            if fused
        ]
    if fused:
        tasks["gz"] = [gain_rows()]

    def weight(s):
        return wg[s].reshape(nz * ny * rb, 2 * LANES)

    if not fused:
        wcp = local((wfull_ref, None), (wg, None))
        gains[...] = gfull_ref[...]
    at("p0")
    relays["x"].wait_recv()
    if not fused:
        wcp.wait()

    sub = min(128, own)
    per = own // sub
    gacc[...] = jnp.zeros_like(gacc)

    def norm_rows(i, _):
        r = rows(i, sub)
        xhat, _unused = normalize(xs[r, :].astype(F32))
        n1[r, :] = (xhat * gains[0:1, :] + gains[1:2, :]).astype(BF16)
        return 0

    lax.fori_loop(0, 4 * per, norm_rows, 0)
    at("p1")

    wide_rows = 2 * own

    def qrows(jj):
        return pl.ds(pl.multiple_of(jj * wide_rows, wide_rows), wide_rows)

    def put_pairs(buf, r, value):
        v = value.astype(BF16)
        buf[0, r, :] = v[:, :LANES]
        buf[1, r, :] = v[:, LANES:]

    def pairs(buf, r):
        return jnp.concatenate([buf[0, r, :], buf[1, r, :]], axis=1)

    scale = DH ** (-0.5)

    def put_transposed(buf, r, value):
        vt_ = value.T.astype(BF16)
        buf[0, :, r] = vt_[:LANES]
        buf[1, :, r] = vt_[LANES:]

    def project(j, _):
        r = qrows(j)
        rowsv = n1[r, :]
        put_pairs(qs, r, nn(rowsv, weight(0)).astype(BF16) * jnp.asarray(scale, BF16))
        put_pairs(ks, r, nn(rowsv, weight(1)))
        val = nn(rowsv, weight(2))
        put_pairs(vs, r, val)
        put_transposed(vt, r, val.astype(BF16).astype(F32))
        return 0

    lax.fori_loop(0, 2, project, 0)
    at("p2")


    lane_at = lax.broadcasted_iota(jnp.int32, (1, LANES), 1)
    head_lanes = [((lane_at // DH) == u).astype(F32).astype(BF16) for u in range(2)]

    def only(value, u):
        return value * head_lanes[u]

    def hide(scores, first, diagonal, causal):
        if causal and not diagonal:
            return scores
        if causal:
            key_at = lax.broadcasted_iota(jnp.int32, scores.shape, 0)
            query_at = lax.broadcasted_iota(jnp.int32, scores.shape, 1)
            return jnp.where(key_at <= query_at, scores, MASKED)
        b = bias[first : first + scores.shape[0], :]
        return scores + jnp.concatenate([b] * (wide_rows // LANES), axis=1)

    def attend(pp, q_s, k_s, v_t, mix, lse, r, keys, causal):
        parts_k = [slice(i * wide_rows, (i + 1) * wide_rows) for i in range(keys // wide_rows)]

        q = q_s[pp, r, :]
        tops = [None, None]
        for i, kk in enumerate(parts_k):
            for u in range(2):
                s = nt(only(k_s[pp, kk, :], u), q)
                s = hide(s, kk.start, i == len(parts_k) - 1, causal)
                top = jnp.max(s, axis=0, keepdims=True)
                tops[u] = top if i == 0 else jnp.maximum(tops[u], top)
                score[u, kk, :] = s
        totals, mixed = [None, None], [None, None]
        for i, kk in enumerate(parts_k):
            for u in range(2):
                e = jnp.exp(score[u, kk, :] - tops[u])
                total = jnp.sum(e, axis=0, keepdims=True)
                o = nn(v_t[pp, u * DH : (u + 1) * DH, kk], e.astype(BF16))
                totals[u] = total if i == 0 else totals[u] + total
                mixed[u] = o if i == 0 else mixed[u] + o
        for u in range(2):
            lse[2 * pp + u, :, r] = tops[u] + jnp.log(totals[u])
            mixed[u] = mixed[u] * (1.0 / totals[u])
        mix[pp, r, :] = jnp.concatenate(mixed, axis=0).T.astype(BF16)

    def exchange(point, j):
        b = point % 2
        i = point * 4 + j
        return pltpu.make_async_remote_copy(
            ps.at[b, rows(j)], pr.at[b, rows(j)], xss.at[i], xrs.at[i],
            device_id=core_peer, device_id_type=MESH,
        )

    def send_sum(point, j, value):
        ps[point % 2, rows(j), :] = value.astype(BF16)
        exchange(point, j).start()

    def summed(point, r):
        b = point % 2
        return ps[b, r, :].astype(F32) + pr[b, r, :].astype(F32)

    for jj in range(2):
        first = 3 + 3 * jj

        def self_pair(pp, _, jj=jj, first=first):
            attend(pp, qs, ks, vt, smix, slse, qrows(jj), wide_rows * (jj + 1), True)
            at_turn(pp, 0, f"p{first}")
            at_turn(pp, 1, f"p{first + 1}")
            return 0

        lax.fori_loop(0, 2, self_pair, 0)
        for j in (2 * jj, 2 * jj + 1):
            send_sum(0, j, nt(pairs(smix, rows(j)), weight(3)))
        at(f"p{first + 2}")
    relays["m"].wait_recv()

    key_at = lax.broadcasted_iota(jnp.int32, (rows_all, LANES), 0)
    bias[...] = jnp.where(key_at < sl_ref[p], 0.0, MASKED)

    def project_cross(j, _):
        r = qrows(j)
        rowsv = ms[r, :]
        put_pairs(cks, r, nn(rowsv, weight(4)))
        val = nn(rowsv, weight(5))
        put_pairs(cvs, r, val)
        put_transposed(vt, r, val.astype(BF16).astype(F32))
        return 0

    lax.fori_loop(0, 2, project_cross, 0)
    at("p9")

    def second(j, _):
        exchange(0, j).wait_recv()
        exchange(0, j).wait_send()

        def part(i, _):
            r = rows(j * per + i, sub)
            h = xs[r, :].astype(F32) + summed(0, r)
            h1[r, :] = h
            xhat, _unused = normalize(h)
            n2[r, :] = (xhat * gains[2:3, :] + gains[3:4, :]).astype(BF16)
            return 0

        lax.fori_loop(0, per, part, 0)
        r = rows(j)
        put_pairs(cqs, r, nn(n2[r, :], weight(6)).astype(BF16) * jnp.asarray(scale, BF16))
        return 0

    lax.fori_loop(0, 4, second, 0)
    at("p10")

    def cross_pair(i, _):
        jj, pp = i // 2, i % 2
        attend(pp, cqs, cks, vt, cmix, clse, qrows(jj), rows_all, False)
        for k, name in enumerate(("p11", "p12", "p14", "p15")):
            at_turn(i, k, name)

        @pl.when(pp == 1)
        def _():
            for k in range(2):
                j = 2 * jj + k
                send_sum(1, j, nt(pairs(cmix, rows(j)), weight(7)))

        at_turn(i, 1, "p13")
        return 0

    lax.fori_loop(0, 4, cross_pair, 0)
    at("p16")

    limit = tl_ref[p]

    def live(r_first, size):
        at = lax.broadcasted_iota(jnp.int32, (size, wide), 0) + r_first
        return at < limit

    def weight_grads(a_buf, items):
        chunk = ny * rb
        for zi in range(nz):
            at = a_buf[:, zi * chunk : (zi + 1) * chunk].T
            for s, load in items:
                gs[s, zi] = nn(at, load()).astype(BF16).reshape(ny, rb, 2 * LANES)

    every = pl.ds(0, rows_all)

    def whole(buf):
        return lambda: pairs(buf, every)

    def plane(buf, s):
        return lambda: buf[s]

    def reduce_part(lo, hi, first, last, order, bufs):
        r = slice(first, last)
        base = lo
        bufs = list(bufs)
        gone = []

        def at(buf, s, zsel, ysel, lsel):
            index = [s]
            if "z" not in gone:
                index.append(zsel)
            if "y" not in gone:
                index.append(ysel)
            index += [slice(None) if buf is not gs else r, lsel]
            return tuple(index)

        every_one = slice(None)
        cur, shift = gs, 0
        for hop, axis in enumerate(order):
            span = slice(lo - shift, hi - shift)
            land = bufs.pop(0)
            to = slice(lo - base, hi - base)
            lanes = every_one if "x" in gone else slice(0, 2 * LANES)
            pick = {"z": every_one, "y": every_one, "x": lanes}
            here = dict(pick)
            if axis == "x":
                pick["x"], here["x"] = other_half, half
                sends = [(pick, (land, to), x_peer)]
            elif axis == "y":
                pick["y"], here["y"] = y_other, y
                sends = [(pick, (land, to), y_peer)]
            else:
                here["z"] = z
                sends = [
                    (dict(pick, z=z_others[k - 1]), (land, (k - 1, to)), z_peer(k))
                    for k in range(1, nz)
                ]
            cps = [
                push((cur, at(cur, span, sel["z"], sel["y"], sel["x"])), dst, peer)
                for sel, dst, peer in sends
            ]
            yield
            for cp in cps:
                cp.wait_recv()
            done = hop == 2
            acc = None if done else bufs.pop(0)

            def add(s, _):
                v = cur[at(cur, s - shift, here["z"], here["y"], here["x"])].astype(F32)
                if axis == "z":
                    for k in range(1, nz):
                        v = v + land[k - 1, s - base].astype(F32)
                else:
                    v = v + land[s - base].astype(F32)
                if done:
                    gw_ref[s, r] = v
                else:
                    acc[s - base] = v.astype(BF16)
                return 0

            lax.fori_loop(lo, hi, add, 0)
            gone.append(axis)
            cur, shift = acc, base
        yield

    for name, (lo, hi) in sum_segments(nf).items():
        size = rb // len(ORDERS[name])
        tasks[name] = [
            reduce_part(lo, hi, i * size, (i + 1) * size, order, sums[name][i])
            for i, order in enumerate(ORDERS[name])
            if fused
        ]

    def third(j, _):
        for k in range(2):
            exchange(1, 2 * j + k).wait_recv()
            exchange(1, 2 * j + k).wait_send()

        def part(i, _):
            r = rows(2 * j * per + i, sub)
            h = h1[r, :] + summed(1, r)
            h2[r, :] = h
            xhat, _unused = normalize(h)
            n3[r, :] = (xhat * gains[4:5, :] + gains[5:6, :]).astype(BF16)
            return 0

        lax.fori_loop(0, 2 * per, part, 0)
        r = qrows(j)
        rowsv = n3[r, :]
        for s in range(nf):
            active, slope = gelu_both(nn(rowsv, weight(8 + s)))
            act[s, r, :] = active.astype(BF16)
            gbf[s, r, :] = slope.astype(BF16)
        at_turn(j, 0, "p17")
        return 0

    lax.fori_loop(0, 2, third, 0)
    at("p18")
    relays["c"].wait_recv()

    def live_rows(i, _):
        r = rows(i, sub)
        cot = cs[r, :]
        gb16[r, :] = jnp.where(live(i * sub, sub), cot, jnp.zeros_like(cot))
        return 0

    lax.fori_loop(0, 4 * per, live_rows, 0)
    weight_grads(gb16, [(9 + nf + s, plane(act, s)) for s in range(nf)])
    at("p19")

    def third_back(j, _):
        r = qrows(j)
        cot = gb16[r, :]
        for s in range(nf):
            slope = gbf[s, r, :].astype(F32)
            gbf[s, r, :] = (nn(cot, weight(8 + nf + s)) * slope).astype(BF16)
        back = nt(gbf[0, r, :], weight(8))
        for s in range(1, nf):
            back = back + nt(gbf[s, r, :], weight(8 + s))
        for k in range(2):
            send_sum(2, 2 * j + k, back[k * own : (k + 1) * own])
        val = nt(act[0, r, :], weight(8 + nf))
        for s in range(1, nf):
            val = val + nt(act[s, r, :], weight(8 + nf + s))
        ys[r, :] = val.astype(BF16)
        at_turn(j, 0, "p20")
        return 0

    lax.fori_loop(0, 2, third_back, 0)

    ycp = [
        push((ys, rows(2 * k + 1 - c)), (yr, k), core_peer) for k in range(2)
    ]

    weight_grads(n3, [(9 + s, plane(gbf, s)) for s in range(nf)])
    at("p21")

    def finish_rows(k, dst):
        def part(i, _):
            r = rows((2 * k + c) * per + i, sub)
            q = rows(i, sub)
            val = h2[r, :] + ys[r, :].astype(F32) + yr[k, q, :].astype(F32)
            keep = live(((2 * k + c) * per + i) * sub, sub)
            dst[q, :] = jnp.where(keep, val, 0.0).astype(BF16)
            return 0
        lax.fori_loop(0, per, part, 0)

    for cp in ycp:
        cp.wait_recv()
    finish_rows(1 - p, osend)
    finish_rows(p, outs.at[p])
    at("p22")

    def back_three(j, _):
        exchange(2, j).wait_recv()
        exchange(2, j).wait_send()

        def part(i, _):
            r = rows(j * per + i, sub)
            dx, dgain, dbias = norm_grad(h2[r, :], summed(2, r), gains[4:5, :])
            gacc[4:5, :] += dgain
            gacc[5:6, :] += dbias
            g = gb16[r, :].astype(F32) + dx
            gh[r, :] = g
            gb16[r, :] = g.astype(BF16)
            return 0

        return lax.fori_loop(0, per, part, 0)

    lax.fori_loop(0, 4, back_three, 0)
    weight_grads(gb16, [(7, whole(cmix))])
    at("p23")


    sel_row = lax.broadcasted_iota(jnp.int32, (8, LANES), 0)
    sel_lane = lax.broadcasted_iota(jnp.int32, (8, LANES), 1)
    selector = (sel_lane // DH == sel_row).astype(F32)

    def pair_lanes(pp):
        return pl.ds(pl.multiple_of(pp * LANES, LANES), LANES)

    def attend_back(pp, q_s, k_s, kt, v_s, mix, lse, r, keys, causal):
        parts_k = [slice(0, keys)]
        if causal and keys > wide_rows:
            parts_k = [slice(0, keys - wide_rows), slice(keys - wide_rows, keys)]

        q = q_s[pp, r, :]
        do = dm[pp, r, :]
        prod = do.astype(F32) * mix[pp, r, :].astype(F32)
        delta = lax.dot_general(
            selector, prod, (((1,), (1,)), ((), ())),
            precision=HIGHEST, preferred_element_type=F32,
        )
        back = None
        for i, kk in enumerate(parts_k):
            parts = []
            for u in range(2):
                s = nt(only(k_s[pp, kk, :], u), q)
                s = hide(s, kk.start, i == len(parts_k) - 1, causal)
                e = jnp.exp(s - lse[2 * pp + u, :, r])
                d = nt(only(v_s[pp, kk, :], u), do)
                ds = (e * (d - delta[u : u + 1])).astype(BF16)
                dv_u = nn(e.astype(BF16), only(do, u))
                dk_u = nn(ds, only(q, u))
                dvp = dv_u if u == 0 else dvp + dv_u
                dkp = dk_u if u == 0 else dkp + dk_u
                parts.append(nn(kt[pp, u * DH : (u + 1) * DH, kk], ds))
            lanes = pair_lanes(pp)
            score[0, kk, lanes] += dkp
            score[1, kk, lanes] += dvp
            parts = jnp.concatenate(parts, axis=0)
            back = parts if i == 0 else back + parts
        dq[pp, r, :] = (back * scale).T.astype(BF16)

    def transpose_keys(buf):
        def one(j, _):
            r = rows(j)
            for pp in range(2):
                vt[pp, :, r] = buf[pp, r, :].astype(F32).T.astype(BF16)
            return 0
        lax.fori_loop(0, 4, one, 0)

    transpose_keys(cks)
    score[:, :, : 2 * LANES] = jnp.zeros((2, rows_all, 2 * LANES), F32)

    def cross_back_pair(i, _):
        jj, pp = i // 2, i % 2

        @pl.when(pp == 0)
        def _():
            for k in range(2):
                r = rows(2 * jj + k)
                put_pairs(dm, r, nn(gb16[r, :], weight(7)))

        attend_back(pp, cqs, cks, vt, cvs, cmix, clse, qrows(jj), rows_all, False)
        for k in range(4):
            at_turn(i, k, f"p{24 + k}")

        @pl.when(pp == 1)
        def _():
            for k in range(2):
                j = 2 * jj + k
                send_sum(3, j, nt(pairs(dq, rows(j)), weight(6)))

        return 0

    lax.fori_loop(0, 4, cross_back_pair, 0)

    def cross_back_keys(j, _):
        r = rows(j)
        for pp in range(2):
            dk[pp, r, :] = score[0, r, pair_lanes(pp)].astype(BF16)
            dv[pp, r, :] = score[1, r, pair_lanes(pp)].astype(BF16)
        val = nt(pairs(dk, r), weight(4)) + nt(pairs(dv, r), weight(5))
        us[r, :] = val.astype(BF16)
        return 0

    lax.fori_loop(0, 4, cross_back_keys, 0)
    ucp = [
        push((us, rows(2 * k + 1 - c)), (ur, k), core_peer) for k in range(2)
    ]
    weight_grads(n2, [(6, whole(dq))])
    weight_grads(ms, [(4, whole(dk)), (5, whole(dv))])
    at("p28")

    def memory_rows(k, dst):
        def part(i, _):
            r = rows((2 * k + c) * per + i, sub)
            q = rows(i, sub)
            dst[q, :] = (us[r, :].astype(F32) + ur[k, q, :].astype(F32)).astype(BF16)
            return 0
        lax.fori_loop(0, per, part, 0)

    for cp in ucp:
        cp.wait_recv()
    memory_rows(1 - p, gmsend)
    memory_rows(p, gms.at[p])
    at("p29")

    def back_two(j, _):
        exchange(3, j).wait_recv()
        exchange(3, j).wait_send()

        def part(i, _):
            r = rows(j * per + i, sub)
            dx, dgain, dbias = norm_grad(h1[r, :], summed(3, r), gains[2:3, :])
            gacc[2:3, :] += dgain
            gacc[3:4, :] += dbias
            g = gh[r, :] + dx
            gh[r, :] = g
            gb16[r, :] = g.astype(BF16)
            return 0

        return lax.fori_loop(0, per, part, 0)

    lax.fori_loop(0, 4, back_two, 0)
    weight_grads(gb16, [(3, whole(smix))])
    at("p30")

    transpose_keys(ks)
    score[:, :, : 2 * LANES] = jnp.zeros((2, rows_all, 2 * LANES), F32)
    for jj in (1, 0):
        for j in (2 * jj, 2 * jj + 1):
            put_pairs(dm, rows(j), nn(gb16[rows(j), :], weight(3)))
        first = 33 - 2 * jj

        def self_back_pair(pp, _, jj=jj, first=first):
            attend_back(pp, qs, ks, vt, vs, smix, slse, qrows(jj), wide_rows * (jj + 1), True)
            at_turn(pp, 0, f"p{first}")
            at_turn(pp, 1, f"p{first + 1}")
            return 0

        lax.fori_loop(0, 2, self_back_pair, 0)
        for j in (2 * jj, 2 * jj + 1):
            r = rows(j)
            for pp in range(2):
                dk[pp, r, :] = score[0, r, pair_lanes(pp)].astype(BF16)
                dv[pp, r, :] = score[1, r, pair_lanes(pp)].astype(BF16)
            val = nt(pairs(dq, r), weight(0)) + nt(pairs(dk, r), weight(1))
            send_sum(4, j, val + nt(pairs(dv, r), weight(2)))

    weight_grads(n1, [(0, whole(dq)), (1, whole(dk)), (2, whole(dv))])
    at("p35")

    def back_one(k, j, dst):
        exchange(4, j).wait_recv()

        def part(i, _):
            r = rows(j * per + i, sub)
            q = rows(i, sub)
            dx, dgain, dbias = norm_grad(xs[r, :].astype(F32), summed(4, r), gains[0:1, :])
            gacc[0:1, :] += dgain
            gacc[1:2, :] += dbias
            if dst is not None:
                dst[q, :] = (gh[r, :] + dx).astype(BF16)
            return 0

        lax.fori_loop(0, per, part, 0)

    back_one(0, tx, gisend)
    at("p36")
    back_one(0, t, gis.at[p])
    back_one(0, 2 * p + 1 - c, None)
    back_one(0, 2 * (1 - p) + 1 - c, None)
    for j in range(4):
        exchange(4, j).wait_send()

    spread_rows = jnp.concatenate(
        [gacc[...], jnp.zeros((LANES - 8, wide), F32)], axis=0
    )
    columns = spread_rows.T.astype(BF16)
    gs[gseg] = jnp.concatenate([columns, columns], axis=1).reshape(nz, ny, rb, 2 * LANES)

    at("p37")
    last = [] if fused else [local((gs, None), (gw_ref, None))]

    finals = [
        local((outs, None), (out_ref, None)),
        local((gms, None), (gm_ref, None)),
        local((gis, None), (gi_ref, None)),
    ]
    for cp in finals + last:
        cp.wait()
    for cp in sent:
        cp.copy().wait_send()


def unpack_kernel(nf, o_ref, gi_ref, gm_ref, gw_ref, *outs):
    outs[0][...] = o_ref[...]
    outs[1][...] = gi_ref[...].astype(F32)
    outs[2][...] = gm_ref[...].astype(F32)
    outs[3][...] = gw_ref[0:3]
    outs[4][...] = gw_ref[3]
    outs[5][...] = gw_ref[6]
    outs[6][...] = gw_ref[4:6]
    outs[7][...] = gw_ref[7]
    for i in range(nf):
        outs[8][:, i * LANES : (i + 1) * LANES] = gw_ref[9 + i]
        outs[9][:, i * LANES : (i + 1) * LANES] = gw_ref[9 + nf + i]
    vectors = gw_ref[8].T
    for i in range(6):
        outs[10 + i][...] = vectors[i : i + 1]


def body(ndp, inputs, memory, tgt_len, src_len, cotangent, w_qkv, w_out, cross_query, cross_kv,
         cross_out, ffn_up, ffn_down, *gain_list):
    own, wide = inputs.shape[1], inputs.shape[2]
    rb = w_qkv.shape[1]
    nf = ffn_up.shape[1] // LANES
    nseg = 8 + 2 * nf
    rows_all = 4 * own
    fused = rb % 32 == 0 and ndp % 2 == 0
    if fused:
        ny, nz, block = 2, ndp // 2, rb
    else:
        ny, nz, block = 1, 1, wide
    cfg = (fused, nz, ny, block, own, wide, nf)

    any_spec = pl.BlockSpec(memory_space=pl.ANY)
    smem = pl.BlockSpec(memory_space=pltpu.SMEM)
    vmem = pl.BlockSpec(memory_space=pltpu.VMEM)
    operands = [inputs, memory, cotangent, tgt_len, src_len]
    specs = [any_spec] * 3 + [smem] * 2
    if fused:
        weights = [w_qkv, w_out.T, cross_query, cross_kv, cross_out.T, ffn_up, ffn_down.T]
        weights += [g[None, :] for g in gain_list]
        operands += weights
        specs += [vmem] * len(weights)
    else:
        pieces = [w_qkv, w_out.T[None], cross_kv, cross_query[None], cross_out.T[None]]
        pieces += [ffn_up.reshape(rb, nf, LANES).swapaxes(0, 1)]
        pieces += [ffn_down.reshape(nf, LANES, rb).swapaxes(1, 2)]
        packed = lax.all_gather(jnp.concatenate(pieces, axis=0), "dp", axis=1, tiled=True)
        index = lax.axis_index("tensor")
        flipped = lax.ppermute(packed, "tensor", [(i, (i + 2) % 4) for i in range(4)])
        low = jnp.where(index < 2, packed, flipped)
        high = jnp.where(index < 2, flipped, packed)
        full = jnp.concatenate([low, high], axis=2)[:, None, None]
        gathered = lax.all_gather(jnp.stack(gain_list), "dp", axis=1, tiled=True)
        operands += [full, jnp.pad(gathered.astype(F32), ((0, 10), (0, 0)))]
        specs += [any_spec, vmem]

    bf = lambda *shape: pltpu.VMEM(shape, BF16)
    fl = lambda *shape: pltpu.VMEM(shape, F32)
    seq = (rows_all, wide)
    heads = (2, rows_all, LANES)
    scratch = [
        bf(*seq), bf(*seq), bf(*seq), bf(nseg, nz, ny, block, 2 * LANES), fl(16, wide),
        bf(*seq), bf(*seq), bf(*seq), fl(*seq), fl(*seq), fl(*seq), bf(*seq),
        bf(*heads), bf(*heads), bf(*heads), bf(*heads), bf(*heads), bf(*heads),
        bf(2, LANES, rows_all), bf(*heads), bf(*heads), fl(4, 1, rows_all), fl(4, 1, rows_all),
        bf(nf, rows_all, 2 * LANES), bf(nf, rows_all, 2 * LANES),
        bf(*heads), bf(*heads), bf(*heads), bf(*heads),
        bf(2, *seq), bf(2, *seq), bf(*seq), bf(2, own, wide), bf(*seq), bf(2, own, wide),
        bf(2, own, wide), bf(own, wide), bf(2, own, wide), bf(own, wide),
        bf(2, own, wide), bf(own, wide),
        bf(nseg + 1, nz, ny, block, 2 * LANES), fl(rows_all, LANES), fl(8, wide),
        fl(2, rows_all, 2 * own),
    ]
    if fused:
        scratch += [bf(nz, 16, wide), bf(2, 16, wide)]
        for name, (lo, hi) in sum_segments(nf).items():
            for order in ORDERS[name]:
                shapes = sum_shapes(order, hi - lo, nz, ny, block // len(ORDERS[name]))
                scratch += [bf(*shape) for shape in shapes]
    dma = pltpu.SemaphoreType.DMA
    scratch += [dma((250,)), dma((250,)), dma((20,)), dma((20,)), dma((12,))]

    if fused:
        grads_shape = jax.ShapeDtypeStruct((nseg + 1, block, LANES), F32)
        grads_spec = vmem
    else:
        grads_shape = jax.ShapeDtypeStruct((nseg + 1, nz, ny, block, 2 * LANES), BF16)
        grads_spec = any_spec
    act_shape = jax.ShapeDtypeStruct(inputs.shape, BF16)
    output, grad_in, grad_mem, grads = pl.pallas_call(
        functools.partial(layer_kernel, cfg),
        out_shape=(act_shape, act_shape, act_shape, grads_shape),
        in_specs=specs,
        out_specs=(any_spec, any_spec, any_spec, grads_spec),
        scratch_shapes=scratch,
        compiler_params=pltpu.CompilerParams(
            collective_id=0, has_side_effects=True, vmem_limit_bytes=62 << 20
        ),
        name="layer",
    )(*operands)

    if not fused:
        mine = grads[:, 0, 0].astype(F32)
        index = lax.axis_index("tensor")
        low, high = mine[:, :, :LANES], mine[:, :, LANES:]
        keep = jnp.where(index < 2, low, high)
        give = jnp.where(index < 2, high, low)
        keep = keep + lax.ppermute(give, "tensor", [(i, (i + 2) % 4) for i in range(4)])
        grads = lax.psum_scatter(keep, "dp", scatter_dimension=1, tiled=True)

    shapes = [
        (inputs.shape, BF16), (inputs.shape, F32), (memory.shape, F32),
        (w_qkv.shape, F32), (w_out.shape[::-1], F32), (cross_query.shape, F32),
        (cross_kv.shape, F32), (cross_out.shape[::-1], F32), (ffn_up.shape, F32),
        (ffn_down.shape[::-1], F32),
    ] + [((1, rb), F32)] * 6
    got = pl.pallas_call(
        functools.partial(unpack_kernel, nf),
        out_shape=[jax.ShapeDtypeStruct(*s) for s in shapes],
        in_specs=[vmem] * 4,
        out_specs=[vmem] * len(shapes),
        name="unpack",
    )(output, grad_in, grad_mem, grads)
    return (
        *got[:4], got[4].T, got[5], got[6], got[7].T, got[8], got[9].T,
        *[g[0] for g in got[10:]],
    )


def solution(mesh):
    return jax.shard_map(
        functools.partial(body, mesh.shape["dp"]),
        mesh=mesh,
        in_specs=(
            P("dp", "tensor", None),
            P("dp", "tensor", None),
            P("dp"),
            P("dp"),
            P("dp", "tensor", None),
            P(None, "dp", "tensor"),
            P("tensor", "dp"),
            P("dp", "tensor"),
            P(None, "dp", "tensor"),
            P("tensor", "dp"),
            P("dp", "tensor"),
            P("tensor", "dp"),
            P("dp"),
            P("dp"),
            P("dp"),
            P("dp"),
            P("dp"),
            P("dp"),
        ),
        out_specs=(
            P("dp", "tensor", None),
            P("dp", "tensor", None),
            P("dp", "tensor", None),
            P(None, "dp", "tensor"),
            P("tensor", "dp"),
            P("dp", "tensor"),
            P(None, "dp", "tensor"),
            P("tensor", "dp"),
            P("dp", "tensor"),
            P("tensor", "dp"),
            P("dp"),
            P("dp"),
            P("dp"),
            P("dp"),
            P("dp"),
            P("dp"),
        ),
        check_vma=False,
    )
```
